32 devices in a mesh: groups: 2 (over y), sub: 16 (over z, x, core).
Axes of the slice: x: 2, y: 2, z: 4, core: 2. Of those that a mesh axis runs over, the one named last changes fastest.
Arguments:
- samples: bfloat16 [16896, 512], P(('groups', 'sub')), parts along dimension 0, may hold values from -6 to 6
- channel_order: int32 [512], replicated, may hold values from 0 to 511, each once
- merge_table: int32 [9, 3, 256], replicated, may hold values from 0 to 128, as said below
Outputs:
- spectra: float32 [512, 4096], P(('groups', 'sub')), parts along dimension 0
The draws below stay inside these ranges and needn't reach their ends.
There are 2 independent parts, one for each index of `groups`. The reference program is written for one: setup_inputs(seed, part) draws one part's arguments, and reference() takes and returns one part's arrays. A program takes and returns all parts, laid end to end along the dimension named above; an argument that names none is the same for every part. Nothing has to cross between parts.
Inputs may be any that keep to these rules, and one draw needn't show every extreme that they name: `channel_order`: a permutation of the 512 channels. `merge_table`: for level l, entry j is row d = j % 2**(l-1) of merged subband j // 2**(l-1); with C = max(1, 2**(l-2)) and e = 8, entries 0 and 1 lie in [e * (d // (2 e)), e * (d // (2 e)) + min(C, e)), and entry 2 equals entry 0 or entry 0 plus 1.
All inputs are finite; a program needn't handle non-finite values.
Results may differ from the reference program's by a relative error of at most 0.012.
Values may be sent and summed in bfloat16 or wider, within the bound.
No kernel may reach another device: no remote copies, remote signals or barrier semaphores. Data moves between devices by JAX's collectives and lax.ppermute only.
A program may use at most 64 MiB of HBM per device.

```python
import math
import jax
import jax.numpy as jnp
from jax import lax

CH_DEV = 32
CROSS = 4
CHANNELS = 512
LEVELS = 9
DMAX = 256
SAMPLES = 8192
SPAN = 8448
N_SUB = 16


def draw_merge_table(key, part):
    quarter = CH_DEV // 4
    owned_rows = CH_DEV // 2
    stacked = []
    for level_num in range(1, LEVELS + 1):
        span_rows = 2 ** (level_num - 1)
        child_rows = max(1, 2 ** (level_num - 2))
        choices_wide = min(child_rows, quarter)
        entry_index = jnp.arange(DMAX, dtype=jnp.int32)
        row_base = entry_index % span_rows // owned_rows * quarter
        key_lower, key_upper, key_shift = jax.random.split(jax.random.fold_in(key, 7919 + level_num), 3)
        lower_rows = row_base + jax.random.randint(key_lower, (DMAX,), 0, choices_wide, dtype=jnp.int32)
        upper_rows = row_base + jax.random.randint(key_upper, (DMAX,), 0, choices_wide, dtype=jnp.int32)
        shifts = lower_rows + jax.random.randint(key_shift, (DMAX,), 0, 2, dtype=jnp.int32)
        stacked.append(jnp.stack([lower_rows, upper_rows, shifts], axis=0))
    return jnp.stack(stacked, axis=0)


def levels(key, extent, pieces, least, high):
    level = 1.0
    for axis_at, blocks in pieces:
        draws = jax.random.uniform(jax.random.fold_in(jax.random.fold_in(key, 6), axis_at), (blocks,), jnp.float32, least / len(pieces), high / len(pieces))
        level = level * jnp.repeat(jnp.exp(draws), extent[axis_at] // blocks).reshape((-1,) + (1,) * (len(extent) - 1 - axis_at))
    return level


def bell_draw(key, dims, deviation, most, cuts=(), kind=jnp.bfloat16):
    result = deviation * jax.random.normal(key, dims, jnp.float32)
    if cuts:
        result = result * levels(key, dims, cuts, -0.22, 0.18)
    return jnp.clip(result, -most, most).astype(kind)


def setup_inputs(seed: int = 0, part: int = 0) -> dict:
    streams_of = jax.random.split(jax.random.key(seed), 4)
    part_keys = jax.random.split(jax.random.fold_in(streams_of[3], part), 4)
    samples = bell_draw(part_keys[0], (SPAN, CHANNELS), 1.0, 6.0, ((0, 16),))
    channel_order = jax.random.permutation(streams_of[1], CHANNELS).astype(jnp.int32)
    merge_table = draw_merge_table(jax.random.fold_in(streams_of[3], 71), part)
    return dict(samples=samples, channel_order=channel_order, merge_table=merge_table)


def delay_rows(values, shifts, margin, time_axis):
    length = values.shape[time_axis]
    if time_axis == 1:
        padded = jnp.pad(values, ((0, 0), (0, margin)))
        return jax.vmap(lambda series, offset: lax.dynamic_slice_in_dim(series, offset, length))(padded, shifts)
    padded = jnp.pad(values, ((0, margin), (0, 0)))
    return jax.vmap(lambda series, offset: lax.dynamic_slice_in_dim(series, offset, length), in_axes=(1, 0), out_axes=1)(padded, shifts)


def merge_level(current, entries, child_rows, span_rows, time_axis):
    outputs = jnp.arange(entries.shape[1], dtype=jnp.int32)
    starts = 2 * child_rows * (outputs // span_rows)
    lower_rows = jnp.take(current, starts + entries[0], axis=1 - time_axis)
    upper_rows = jnp.take(current, starts + child_rows + entries[1], axis=1 - time_axis)
    moved_rows = delay_rows(upper_rows, entries[2], child_rows, time_axis)
    return (lower_rows.astype(jnp.float32) + moved_rows.astype(jnp.float32)).astype(jnp.bfloat16)


def spectrum(delays, channels):
    row_count = delays.shape[0]
    length = delays.shape[1]
    fold_size = length // 128
    first_index = jnp.arange(fold_size, dtype=jnp.int32)
    lane_index = jnp.arange(128, dtype=jnp.int32)
    half_index = jnp.arange(64, dtype=jnp.int32)
    angle_one = (2.0 * math.pi / fold_size) * ((first_index[:, None] * first_index[None, :]) % fold_size).astype(jnp.float32)
    cos_one = jnp.cos(angle_one).astype(jnp.bfloat16).astype(jnp.float32)
    sin_one = jnp.sin(angle_one).astype(jnp.bfloat16).astype(jnp.float32)
    angle_two = (2.0 * math.pi / length) * ((first_index[:, None] * lane_index[None, :]) % length).astype(jnp.float32)
    twist_cos = jnp.cos(angle_two)
    twist_sin = jnp.sin(angle_two)
    angle_three = (2.0 * math.pi / 128) * ((lane_index[:, None] * half_index[None, :]) % 128).astype(jnp.float32)
    cos_three = jnp.cos(angle_three).astype(jnp.bfloat16).astype(jnp.float32)
    sin_three = jnp.sin(angle_three).astype(jnp.bfloat16).astype(jnp.float32)
    series = delays.reshape(row_count, fold_size, 128).astype(jnp.float32)
    highest = lax.Precision.HIGHEST
    first_re = jnp.einsum("kn,rnm->rkm", cos_one, series, precision=highest)
    first_im = -jnp.einsum("kn,rnm->rkm", sin_one, series, precision=highest)
    twisted_re = (first_re * twist_cos + first_im * twist_sin).astype(jnp.bfloat16).astype(jnp.float32)
    twisted_im = (first_im * twist_cos - first_re * twist_sin).astype(jnp.bfloat16).astype(jnp.float32)
    out_re = jnp.einsum("rkn,nj->rjk", twisted_re, cos_three, precision=highest) + jnp.einsum("rkn,nj->rjk", twisted_im, sin_three, precision=highest)
    out_im = jnp.einsum("rkn,nj->rjk", twisted_im, cos_three, precision=highest) - jnp.einsum("rkn,nj->rjk", twisted_re, sin_three, precision=highest)
    power = (out_re * out_re + out_im * out_im) / (length * channels)
    return power.reshape(row_count, 64 * fold_size)


def reference(samples, channel_order, merge_table):
    current = jnp.take(samples, channel_order, axis=1).T
    for level_num in range(1, LEVELS + 1):
        current = merge_level(current, merge_table[level_num - 1], max(1, 2 ** (level_num - 2)), 2 ** (level_num - 1), 1)
    owned_rows = CH_DEV // 2
    reversal = []
    for position in range(N_SUB):
        flipped = 0
        for bit_num in range(CROSS):
            flipped = flipped | (((position >> bit_num) & 1) << (CROSS - 1 - bit_num))
        reversal.append(flipped)
    blocks = current.reshape(N_SUB, owned_rows, SPAN)
    blocks = jnp.take(blocks, jnp.array(reversal, dtype=jnp.int32), axis=0).reshape(DMAX, SPAN)
    return spectrum(blocks[:, :SAMPLES], CHANNELS)
```

```python
import functools
import math

import jax
import jax.numpy as jnp
import numpy as np
from jax import lax
from jax.experimental import pallas as pl
from jax.experimental.pallas import tpu as pltpu
from jax.sharding import PartitionSpec as P

LOCAL = 5
CH_DEV = 32
SAMPLES = 8192
LANES = 128


def from_partner(block, axis, apart):
    count = lax.axis_size(axis)
    route = []
    for low in range(count):
        high = low | 1 << apart
        if high != low and high < count:
            route += [(low, high), (high, low)]
    return lax.ppermute(block, axis, route)


def delay_rows(values, shifts, margin, time_axis):
    moved = values
    for bit_num in range(max(1, margin.bit_length())):
        offset = 2**bit_num
        rolled = jnp.pad(moved[:, offset:], ((0, 0), (0, offset)))
        flagged = shifts >> bit_num & 1 == 1
        flagged = flagged[:, None]
        moved = jnp.where(flagged, rolled, moved)
    return moved


def merge_level(current, entries, child_rows, span_rows, time_axis):
    outputs = jnp.arange(entries.shape[1], dtype=jnp.int32)
    starts = 2 * child_rows * (outputs // span_rows)
    lower_rows = jnp.take(current, starts + entries[0], axis=1 - time_axis)
    upper_rows = jnp.take(current, starts + child_rows + entries[1], axis=1 - time_axis)
    moved_rows = delay_rows(upper_rows, entries[2], child_rows, time_axis)
    return (lower_rows.astype(jnp.float32) + moved_rows.astype(jnp.float32)).astype(jnp.bfloat16)


def spectrum(delays, channels):
    row_count = delays.shape[0]
    length = delays.shape[1]
    fold_size = length // 128
    first_index = jnp.arange(fold_size, dtype=jnp.int32)
    lane_index = jnp.arange(128, dtype=jnp.int32)
    half_index = jnp.arange(64, dtype=jnp.int32)
    angle_one = (
        2.0
        * math.pi
        / fold_size
        * (first_index[:, None] * first_index[None, :] % fold_size).astype(jnp.float32)
    )
    cos_one = jnp.cos(angle_one).astype(jnp.bfloat16)
    sin_one = jnp.sin(angle_one).astype(jnp.bfloat16)
    angle_two = (
        2.0
        * math.pi
        / length
        * (first_index[:, None] * lane_index[None, :] % length).astype(jnp.float32)
    )
    twist_cos = jnp.cos(angle_two)
    twist_sin = jnp.sin(angle_two)
    angle_three = (
        2.0 * math.pi / 128 * (lane_index[:, None] * half_index[None, :] % 128).astype(jnp.float32)
    )
    cos_three = jnp.cos(angle_three).astype(jnp.bfloat16)
    sin_three = jnp.sin(angle_three).astype(jnp.bfloat16)
    series = delays.reshape(row_count, fold_size, 128)
    first_re = jnp.einsum("kn,rnm->rkm", cos_one, series, preferred_element_type=jnp.float32)
    first_im = -jnp.einsum("kn,rnm->rkm", sin_one, series, preferred_element_type=jnp.float32)
    twisted_re = (first_re * twist_cos + first_im * twist_sin).astype(jnp.bfloat16)
    twisted_im = (first_im * twist_cos - first_re * twist_sin).astype(jnp.bfloat16)
    out_re = jnp.einsum(
        "rkn,nj->rjk", twisted_re, cos_three, preferred_element_type=jnp.float32
    ) + jnp.einsum("rkn,nj->rjk", twisted_im, sin_three, preferred_element_type=jnp.float32)
    out_im = jnp.einsum(
        "rkn,nj->rjk", twisted_im, cos_three, preferred_element_type=jnp.float32
    ) - jnp.einsum("rkn,nj->rjk", twisted_re, sin_three, preferred_element_type=jnp.float32)
    power = (out_re * out_re + out_im * out_im) / (length * channels)
    return power.reshape(row_count, 64 * fold_size)


def owner_plan(samples, channel_order, merge_table):
    owners = lax.axis_size("sub")
    owner_index = lax.axis_index("sub")
    owned_rows = CH_DEV // 2
    quarter = CH_DEV // 4
    window = samples.shape[0]
    channels = samples.shape[1]
    ordered = jnp.take(samples, channel_order, axis=1).T.reshape(owners, CH_DEV, window)
    current = lax.all_to_all(ordered, "sub", split_axis=0, concat_axis=2, tiled=True).reshape(
        CH_DEV, window * owners
    )
    for level_num in range(1, LOCAL + 1):
        entries = lax.dynamic_slice_in_dim(
            merge_table[level_num - 1], owner_index * owned_rows, owned_rows, 1
        )
        current = merge_level(
            current, entries, max(1, 2 ** (level_num - 2)), 2 ** (level_num - 1), 1
        )
    block_index = jnp.zeros((), jnp.int32)
    for bit_num in range(owners.bit_length() - 1):
        level_num = LOCAL + bit_num + 1
        half_bit = owner_index >> bit_num & 1
        block_index = block_index * 2 + half_bit
        span_rows = owned_rows * 2 ** (bit_num + 1)
        child_rows = span_rows // 2
        subband = owner_index >> bit_num + 1
        entries = lax.dynamic_slice_in_dim(
            merge_table[level_num - 1],
            subband * span_rows + owned_rows * block_index,
            owned_rows,
            1,
        )
        kept_rows = lax.dynamic_slice_in_dim(current, half_bit * quarter, quarter, 0)
        sent_rows = lax.dynamic_slice_in_dim(current, (1 - half_bit) * quarter, quarter, 0)
        partner = from_partner(sent_rows, "sub", bit_num)
        row_base = quarter * block_index
        is_low = half_bit == 0
        lower_part = jnp.where(is_low, kept_rows, partner)
        upper_part = jnp.where(is_low, partner, kept_rows)
        lower_rows = jnp.take(lower_part, entries[0] - row_base, axis=0)
        upper_rows = jnp.take(upper_part, entries[1] - row_base, axis=0)
        moved_rows = delay_rows(upper_rows, entries[2], child_rows, 1)
        current = (lower_rows.astype(jnp.float32) + moved_rows.astype(jnp.float32)).astype(
            jnp.bfloat16
        )
    return spectrum(current[:, :SAMPLES], channels)


def reverse_bits(value, bits):
    flipped = 0
    for bit_num in range(bits):
        flipped |= (value >> bit_num & 1) << (bits - 1 - bit_num)
    return flipped


def tree_kernel(
    owners, margin, samples_ref, order_ref, table_ref, out_ref, slab_ref, rows_ref, cols_ref,
    cur_ref, pick_ref, sem,
):
    window, channels = samples_ref.shape
    levels, _, dmax = table_ref.shape
    slab = slab_ref.shape[0]
    body = slab // LANES
    left = margin // LANES
    half = left // 2
    offset = (lax.axis_index("sub") * window) % LANES
    room = slab - window
    zeros = jnp.zeros((room, channels), slab_ref.dtype)
    slab_ref[:room] = zeros
    slab_ref[window:] = zeros
    load = pltpu.make_async_copy(
        samples_ref, slab_ref.at[pl.ds(pl.multiple_of(offset, 16), window)], sem
    )
    load.start()

    rows_ref[...] = jnp.zeros(rows_ref.shape, jnp.int32)
    for level in range(levels):
        rows_ref[3 * level : 3 * level + 3, :] = table_ref[level]
    for part in range(channels // dmax):
        rows_ref[3 * levels + part : 3 * levels + part + 1, :] = order_ref[
            :, part * dmax : (part + 1) * dmax
        ]
    cols_ref[...] = rows_ref[...].T

    raw_lane = lax.broadcasted_iota(jnp.int32, (dmax, channels), 1)
    picks = []
    for parity in range(2):
        chosen = cols_ref[pl.ds(parity, dmax // 2, stride=2), :]
        raw = jnp.concatenate(
            [chosen[:, 3 * levels + part : 3 * levels + part + 1] for part in range(2)], axis=0
        )
        picks.append(jnp.where(raw == raw_lane, 1.0, 0.0).astype(jnp.bfloat16))
    load.wait()
    for part, pick in enumerate(picks):
        pick_ref[part * dmax : (part + 1) * dmax, LANES * half :] = lax.dot_general(
            pick, slab_ref[...], (((1,), (1,)), ((), ())), preferred_element_type=jnp.float32
        )

    lane = lax.broadcasted_iota(jnp.int32, (16, LANES), 1)
    row_lane = lax.broadcasted_iota(jnp.int32, (dmax, dmax), 1)
    row_index = lax.broadcasted_iota(jnp.int32, (dmax, 1), 0)
    zero = jnp.zeros((16, LANES), jnp.float32)
    for level in range(levels):
        first, last = level == 0, level == levels - 1
        if not first:
            child = max(1, 2 ** (level - 1))
            start = 2 * child * (row_index // 2**level)
            low = start + cols_ref[:, 3 * level : 3 * level + 1]
            high = start + child + cols_ref[:, 3 * level + 1 : 3 * level + 2]
            current = cur_ref[...]
            for part, index in enumerate((low, high)):
                pick = jnp.where(index == row_lane, 1.0, 0.0).astype(jnp.bfloat16)
                pick_ref[part * dmax : (part + 1) * dmax, :] = jnp.dot(
                    pick, current, preferred_element_type=jnp.float32
                )
        for block in range(dmax // 16):
            at = block * 16
            reach = lane + cols_ref[at : at + 16, 3 * level + 2 : 3 * level + 3]
            here = reach < LANES
            source = reach & (LANES - 1)
            low_at = pl.ds(at, 16)
            high_at = pl.ds(dmax + at, 16)
            after = zero
            if last:
                owner = reverse_bits(block, (owners - 1).bit_length())
            for tile in reversed(range(-half if last else 0, half + body)):
                inside = tile >= (half if first else 0)
                at_lanes = slice(tile * LANES, (tile + 1) * LANES)
                if inside:
                    taken = jnp.take_along_axis(pick_ref[high_at, at_lanes], source, axis=1)
                    total = pick_ref[low_at, at_lanes] + jnp.where(here, taken, after)
                else:
                    taken = zero
                    total = jnp.where(here, taken, after)
                after = taken
                total = total.astype(jnp.bfloat16)
                if last:
                    to = tile + half
                    out_ref[owner, :, to * LANES : (to + 1) * LANES] = total
                else:
                    cur_ref[at : at + 16, at_lanes] = total


def spectrum_kernel(
    window, margin, scale, got_ref, first_ref, cos_ref, sin_ref, third_ref, out_ref, slot_ref,
    flat_ref,
):
    sources, rows, width = got_ref.shape
    tiles = width // LANES
    pitch = slot_ref.shape[0] // rows
    used = sources * tiles
    bins = first_ref.shape[0] // 2
    halves = third_ref.shape[0] // 2
    for source in range(sources):
        for tile in range(tiles):
            slot_ref[pl.ds(source * tiles + tile, rows, stride=pitch), :] = got_ref[
                source, :, tile * LANES : (tile + 1) * LANES
            ].astype(jnp.float32)
    lane = lax.broadcasted_iota(jnp.int32, (halves // 2, LANES), 1)
    sign = jnp.where(lax.broadcasted_iota(jnp.int32, (halves, LANES), 1) < bins, 1.0, -1.0)
    for row in range(rows):
        series = slot_ref[row * pitch : row * pitch + used, :].astype(jnp.bfloat16)
        turned = jnp.dot(first_ref[...], series, preferred_element_type=jnp.float32)
        real, imag = turned[:bins], turned[bins:]
        twisted_re = (real * cos_ref[...] - imag * sin_ref[...]).astype(jnp.bfloat16)
        twisted_im = (-imag * cos_ref[...] - real * sin_ref[...]).astype(jnp.bfloat16)
        twisted = jnp.concatenate([twisted_re, twisted_im], axis=0)
        mixed = lax.dot_general(
            third_ref[...], twisted, (((1,), (1,)), ((), ())), preferred_element_type=jnp.float32
        )
        value = mixed[:halves] + sign * pltpu.roll(mixed[halves:], bins, axis=1)
        square = value * value
        power = (square + pltpu.roll(square, bins, axis=1)) * scale
        line = jnp.where(lane < bins, power[: halves // 2], power[halves // 2 :])
        flat_ref[
            pl.ds(row // 8 * 8 * (halves // 2) + row % 8, halves // 2, stride=8), :
        ] = line
    for group in range(rows // 8):
        for tile in range(halves // 2):
            at = (group * (halves // 2) + tile) * 8
            out_ref[group * 8 : group * 8 + 8, tile * LANES : (tile + 1) * LANES] = flat_ref[
                at : at + 8, :
            ]


def spectrum_tables(sources, window, margin, tiles):
    fold = SAMPLES // LANES
    k = np.arange(fold)
    n = np.arange(LANES)
    m = np.arange(64)

    def angle(product, period):
        return np.float32(2.0 * math.pi / period) * (product % period).astype(np.float32)

    one = angle(k[:, None] * k[None, :], fold)
    table_one = np.concatenate([np.cos(one), np.sin(one)], axis=0)
    first = np.zeros((2 * fold, sources * tiles), np.float32)
    for source in range(sources):
        start = (source * window) // LANES - margin // LANES
        for tile in range(tiles):
            if 0 <= start + tile < fold:
                first[:, source * tiles + tile] = table_one[:, start + tile]
    two = angle(k[:, None] * n[None, :], SAMPLES)
    m = np.concatenate([m[0::2], m[1::2]])
    three = angle(m[:, None] * n[None, :], LANES)
    third = np.concatenate([np.cos(three), np.sin(three)], axis=0)
    return (
        jnp.asarray(first, jnp.bfloat16),
        jnp.asarray(np.cos(two), jnp.float32),
        jnp.asarray(np.sin(two), jnp.float32),
        jnp.asarray(third, jnp.bfloat16),
    )


def slice_plan(samples, channel_order, merge_table):
    owners = lax.axis_size("sub")
    window, channels = samples.shape
    levels, _, dmax = merge_table.shape
    margin = window * owners - SAMPLES
    rows = dmax // owners
    step = math.gcd(window, LANES)
    body = -(-(window + LANES - step) // LANES)
    width = margin + body * LANES
    kept = margin // 2 + body * LANES
    vmem = pl.BlockSpec(memory_space=pltpu.VMEM)
    partial = pl.pallas_call(
        functools.partial(tree_kernel, owners, margin),
        out_shape=jax.ShapeDtypeStruct((owners, rows, width), jnp.bfloat16),
        in_specs=[pl.BlockSpec(memory_space=pl.ANY), vmem, vmem],
        out_specs=vmem,
        scratch_shapes=[
            pltpu.VMEM((body * LANES, channels), jnp.bfloat16),
            pltpu.VMEM((LANES, dmax), jnp.int32),
            pltpu.VMEM((dmax, LANES), jnp.int32),
            pltpu.VMEM((dmax, kept), jnp.bfloat16),
            pltpu.VMEM((2 * dmax, kept), jnp.float32),
            pltpu.SemaphoreType.DMA,
        ],
        name="tree",
    )(samples, channel_order.reshape(1, channels), merge_table)
    got = lax.all_to_all(partial, "sub", split_axis=0, concat_axis=0, tiled=True)
    tables = spectrum_tables(owners, window, margin, width // LANES)
    used = owners * width // LANES
    pitch = used + 1
    return pl.pallas_call(
        functools.partial(spectrum_kernel, window, margin, 1.0 / (SAMPLES * channels)),
        out_shape=jax.ShapeDtypeStruct((rows, SAMPLES // 2), jnp.float32),
        in_specs=[vmem] * 5,
        out_specs=vmem,
        scratch_shapes=[
            pltpu.VMEM((rows * pitch, LANES), jnp.float32),
            pltpu.VMEM((rows * SAMPLES // 2 // LANES, LANES), jnp.float32),
        ],
        name="spectrum",
    )(got, *tables)


def local(samples, channel_order, merge_table):
    owners = lax.axis_size("sub")
    window, channels = samples.shape
    dmax = merge_table.shape[2]
    margin = window * owners - SAMPLES
    fits = (
        dmax == 256
        and channels == 2 * dmax
        and dmax == 16 * owners
        and margin == dmax
        and window % 16 == 0
        and window <= 1024
    )
    plan = slice_plan if fits else owner_plan
    return plan(samples, channel_order, merge_table)


def solution(mesh):
    in_specs = (P(("groups", "sub"), None), P(), P())
    out_specs = P(("groups", "sub"), None)
    return jax.shard_map(local, mesh=mesh, in_specs=in_specs, out_specs=out_specs, check_vma=False)
```

```python
import functools
import math

import jax
import jax.numpy as jnp
import numpy as np
from jax import lax
from jax.experimental import pallas as pl
from jax.experimental.pallas import tpu as pltpu
from jax.sharding import PartitionSpec as P

LOCAL = 5
CH_DEV = 32
SAMPLES = 8192
LANES = 128


def from_partner(block, axis, apart):
    count = lax.axis_size(axis)
    route = []
    for low in range(count):
        high = low | 1 << apart
        if high != low and high < count:
            route += [(low, high), (high, low)]
    return lax.ppermute(block, axis, route)


def delay_rows(values, shifts, margin, time_axis):
    moved = values
    for bit_num in range(max(1, margin.bit_length())):
        offset = 2**bit_num
        rolled = jnp.pad(moved[:, offset:], ((0, 0), (0, offset)))
        flagged = shifts >> bit_num & 1 == 1
        flagged = flagged[:, None]
        moved = jnp.where(flagged, rolled, moved)
    return moved


def merge_level(current, entries, child_rows, span_rows, time_axis):
    outputs = jnp.arange(entries.shape[1], dtype=jnp.int32)
    starts = 2 * child_rows * (outputs // span_rows)
    lower_rows = jnp.take(current, starts + entries[0], axis=1 - time_axis)
    upper_rows = jnp.take(current, starts + child_rows + entries[1], axis=1 - time_axis)
    moved_rows = delay_rows(upper_rows, entries[2], child_rows, time_axis)
    return (lower_rows.astype(jnp.float32) + moved_rows.astype(jnp.float32)).astype(jnp.bfloat16)


def spectrum(delays, channels):
    row_count = delays.shape[0]
    length = delays.shape[1]
    fold_size = length // 128
    first_index = jnp.arange(fold_size, dtype=jnp.int32)
    lane_index = jnp.arange(128, dtype=jnp.int32)
    half_index = jnp.arange(64, dtype=jnp.int32)
    angle_one = (
        2.0
        * math.pi
        / fold_size
        * (first_index[:, None] * first_index[None, :] % fold_size).astype(jnp.float32)
    )
    cos_one = jnp.cos(angle_one).astype(jnp.bfloat16)
    sin_one = jnp.sin(angle_one).astype(jnp.bfloat16)
    angle_two = (
        2.0
        * math.pi
        / length
        * (first_index[:, None] * lane_index[None, :] % length).astype(jnp.float32)
    )
    twist_cos = jnp.cos(angle_two)
    twist_sin = jnp.sin(angle_two)
    angle_three = (
        2.0 * math.pi / 128 * (lane_index[:, None] * half_index[None, :] % 128).astype(jnp.float32)
    )
    cos_three = jnp.cos(angle_three).astype(jnp.bfloat16)
    sin_three = jnp.sin(angle_three).astype(jnp.bfloat16)
    series = delays.reshape(row_count, fold_size, 128)
    first_re = jnp.einsum("kn,rnm->rkm", cos_one, series, preferred_element_type=jnp.float32)
    first_im = -jnp.einsum("kn,rnm->rkm", sin_one, series, preferred_element_type=jnp.float32)
    twisted_re = (first_re * twist_cos + first_im * twist_sin).astype(jnp.bfloat16)
    twisted_im = (first_im * twist_cos - first_re * twist_sin).astype(jnp.bfloat16)
    out_re = jnp.einsum(
        "rkn,nj->rjk", twisted_re, cos_three, preferred_element_type=jnp.float32
    ) + jnp.einsum("rkn,nj->rjk", twisted_im, sin_three, preferred_element_type=jnp.float32)
    out_im = jnp.einsum(
        "rkn,nj->rjk", twisted_im, cos_three, preferred_element_type=jnp.float32
    ) - jnp.einsum("rkn,nj->rjk", twisted_re, sin_three, preferred_element_type=jnp.float32)
    power = (out_re * out_re + out_im * out_im) / (length * channels)
    return power.reshape(row_count, 64 * fold_size)


def owner_plan(samples, channel_order, merge_table):
    owners = lax.axis_size("sub")
    owner_index = lax.axis_index("sub")
    owned_rows = CH_DEV // 2
    quarter = CH_DEV // 4
    window = samples.shape[0]
    channels = samples.shape[1]
    ordered = jnp.take(samples, channel_order, axis=1).T.reshape(owners, CH_DEV, window)
    current = lax.all_to_all(ordered, "sub", split_axis=0, concat_axis=2, tiled=True).reshape(
        CH_DEV, window * owners
    )
    for level_num in range(1, LOCAL + 1):
        entries = lax.dynamic_slice_in_dim(
            merge_table[level_num - 1], owner_index * owned_rows, owned_rows, 1
        )
        current = merge_level(
            current, entries, max(1, 2 ** (level_num - 2)), 2 ** (level_num - 1), 1
        )
    block_index = jnp.zeros((), jnp.int32)
    for bit_num in range(owners.bit_length() - 1):
        level_num = LOCAL + bit_num + 1
        half_bit = owner_index >> bit_num & 1
        block_index = block_index * 2 + half_bit
        span_rows = owned_rows * 2 ** (bit_num + 1)
        child_rows = span_rows // 2
        subband = owner_index >> bit_num + 1
        entries = lax.dynamic_slice_in_dim(
            merge_table[level_num - 1],
            subband * span_rows + owned_rows * block_index,
            owned_rows,
            1,
        )
        kept_rows = lax.dynamic_slice_in_dim(current, half_bit * quarter, quarter, 0)
        sent_rows = lax.dynamic_slice_in_dim(current, (1 - half_bit) * quarter, quarter, 0)
        partner = from_partner(sent_rows, "sub", bit_num)
        row_base = quarter * block_index
        is_low = half_bit == 0
        lower_part = jnp.where(is_low, kept_rows, partner)
        upper_part = jnp.where(is_low, partner, kept_rows)
        lower_rows = jnp.take(lower_part, entries[0] - row_base, axis=0)
        upper_rows = jnp.take(upper_part, entries[1] - row_base, axis=0)
        moved_rows = delay_rows(upper_rows, entries[2], child_rows, 1)
        current = (lower_rows.astype(jnp.float32) + moved_rows.astype(jnp.float32)).astype(
            jnp.bfloat16
        )
    return spectrum(current[:, :SAMPLES], channels)


def reverse_bits(value, bits):
    flipped = 0
    for bit_num in range(bits):
        flipped |= (value >> bit_num & 1) << (bits - 1 - bit_num)
    return flipped


def take_along(values, index, axis):
    along = lax.GatherDimensionNumbers(
        offset_dims=(),
        collapsed_slice_dims=(axis,),
        start_index_map=(axis,),
        operand_batching_dims=(1 - axis,),
        start_indices_batching_dims=(1 - axis,),
    )
    return lax.gather(
        values, index[:, :, None], along, (1, 1), mode=lax.GatherScatterMode.PROMISE_IN_BOUNDS
    )


def tree_kernel(
    owners, margin, samples_ref, order_ref, table_ref, out_ref, raw_ref, first_ref, pick_ref,
    cur_ref, picked_ref, final_ref, sem,
):
    window, channels = samples_ref.shape
    levels, _, dmax = table_ref.shape
    quarter = CH_DEV // 4
    pad = margin // 2
    length = pad + window
    offset = (lax.axis_index("sub") * window) % LANES
    load = pltpu.make_async_copy(samples_ref, raw_ref, sem)
    load.start()

    final_ref[...] = jnp.zeros(final_ref.shape, final_ref.dtype)
    lane = lax.broadcasted_iota(jnp.int32, (8, LANES), 1)
    place = lax.broadcasted_iota(jnp.int32, (channels, LANES), 0)
    for side in range(2):
        for tile in range(dmax // LANES):
            parts = [
                take_along(
                    jnp.broadcast_to(
                        order_ref[:, (2 * tile + part) * LANES : (2 * tile + part + 1) * LANES],
                        (8, LANES),
                    ),
                    (2 * lane + side) & (LANES - 1),
                    1,
                )
                for part in range(2)
            ]
            chosen = jnp.where(lane < LANES // 2, parts[0], parts[1])[:1]
            at = side * dmax + tile * LANES
            first_ref[:, at : at + LANES] = jnp.where(place == chosen, 1.0, 0.0).astype(
                jnp.bfloat16
            )
    place = lax.broadcasted_iota(jnp.int32, (dmax, dmax), 0)
    index = lax.broadcasted_iota(jnp.int32, (1, dmax), 1)
    for level in range(1, levels):
        child = 2 ** (level - 1)
        start = (index >> level) * (2 * child)
        for side in range(2):
            chosen = start + side * child + table_ref[level, side : side + 1, :]
            pick_ref[level - 1, :, side * dmax : (side + 1) * dmax] = jnp.where(
                place == chosen, 1.0, 0.0
            ).astype(jnp.bfloat16)
    load.wait()

    row = lax.broadcasted_iota(jnp.int32, (8, LANES), 0)
    zero = jnp.zeros((8, LANES), jnp.float32)
    begin = pad
    for level in range(levels):
        last = level == levels - 1
        if level:
            picked_ref[begin:length, :] = jnp.dot(
                cur_ref[begin:length, :], pick_ref[level - 1], preferred_element_type=jnp.float32
            )
        else:
            picked_ref[begin:length, :] = jnp.dot(
                raw_ref[...], first_ref[...], preferred_element_type=jnp.float32
            )
        reached = (pad - 2**level) // 16 * 16
        for tile in range(dmax // LANES):
            output = tile * LANES + lane
            steps = (output & (2**level - 1)) // (2 * quarter)
            least = (tile * LANES & (2**level - 1)) // (2 * quarter)
            most = ((tile * LANES + LANES - 1) & (2**level - 1)) // (2 * quarter)
            if 2**level <= LANES:
                least, most = 0, (2**level - 1) // (2 * quarter)
            bits = (most - least).bit_length()
            shift = jnp.broadcast_to(
                table_ref[level, 2:3, tile * LANES : (tile + 1) * LANES], (8, LANES)
            )
            rest = row + shift - steps * quarter
            here = rest < 8
            source = rest & 7
            flags = [((steps - least) >> bit & 1) == 1 for bit in range(bits)]
            known = {}

            def coarse(bit, at):
                if at >= length // 8:
                    return None
                if (bit, at) not in known:
                    if bit == 0:
                        known[bit, at] = (
                            picked_ref[
                                at * 8 : at * 8 + 8,
                                dmax + tile * LANES : dmax + (tile + 1) * LANES,
                            ]
                            if at * 8 >= begin
                            else None
                        )
                    else:
                        near, far = coarse(bit - 1, at), coarse(bit - 1, at + 2 ** (bit - 1))
                        if near is None and far is None:
                            known[bit, at] = None
                        else:
                            near = zero if near is None else near
                            far = zero if far is None else far
                            known[bit, at] = jnp.where(flags[bit - 1], far, near)
                return known[bit, at]

            def fine(at):
                if ("fine", at) not in known:
                    value = coarse(bits, at + least)
                    known["fine", at] = None if value is None else take_along(value, source, 0)
                return known["fine", at]

            def merged(at):
                near, far = fine(at), fine(at + 1)
                total = None
                if near is not None or far is not None:
                    total = jnp.where(
                        here, zero if near is None else near, zero if far is None else far
                    )
                if begin <= at * 8:
                    low = picked_ref[at * 8 : at * 8 + 8, tile * LANES : (tile + 1) * LANES]
                    total = low if total is None else low + total
                return zero if total is None else total

            lanes = slice(tile * LANES, (tile + 1) * LANES)
            for at in range(reached // 8, length // 8, 2):
                both = jnp.concatenate([merged(at), merged(at + 1)], axis=0).astype(jnp.bfloat16)
                if last:
                    to = pl.multiple_of(offset + at * 8 + pad, 16)
                    final_ref[pl.ds(to, 16), lanes] = both
                else:
                    cur_ref[at * 8 : at * 8 + 16, lanes] = both
        begin = max(reached, 0)

    for tile in range(dmax // LANES):
        for time in range(final_ref.shape[0] // LANES):
            lanes = slice(time * LANES, (time + 1) * LANES)
            turned = final_ref[lanes, tile * LANES : (tile + 1) * LANES].T
            for block in range(LANES // 16):
                owner = reverse_bits(tile * (LANES // 16) + block, (owners - 1).bit_length())
                out_ref[owner, :, lanes] = turned[block * 16 : (block + 1) * 16]


def spectrum_kernel(
    window, margin, scale, got_ref, first_ref, cos_ref, sin_ref, third_ref, out_ref, slot_ref,
    flat_ref,
):
    sources, rows, width = got_ref.shape
    tiles = width // LANES
    pitch = slot_ref.shape[0] // rows
    used = sources * tiles
    bins = first_ref.shape[0] // 2
    halves = third_ref.shape[0] // 2
    for source in range(sources):
        for tile in range(tiles):
            slot_ref[pl.ds(source * tiles + tile, rows, stride=pitch), :] = got_ref[
                source, :, tile * LANES : (tile + 1) * LANES
            ].astype(jnp.float32)
    lane = lax.broadcasted_iota(jnp.int32, (halves // 2, LANES), 1)
    sign = jnp.where(lax.broadcasted_iota(jnp.int32, (halves, LANES), 1) < bins, 1.0, -1.0)
    for row in range(rows):
        series = slot_ref[row * pitch : row * pitch + used, :].astype(jnp.bfloat16)
        turned = jnp.dot(first_ref[...], series, preferred_element_type=jnp.float32)
        real, imag = turned[:bins], turned[bins:]
        twisted_re = (real * cos_ref[...] - imag * sin_ref[...]).astype(jnp.bfloat16)
        twisted_im = (-imag * cos_ref[...] - real * sin_ref[...]).astype(jnp.bfloat16)
        twisted = jnp.concatenate([twisted_re, twisted_im], axis=0)
        mixed = lax.dot_general(
            third_ref[...], twisted, (((1,), (1,)), ((), ())), preferred_element_type=jnp.float32
        )
        value = mixed[:halves] + sign * pltpu.roll(mixed[halves:], bins, axis=1)
        square = value * value
        power = (square + pltpu.roll(square, bins, axis=1)) * scale
        line = jnp.where(lane < bins, power[: halves // 2], power[halves // 2 :])
        flat_ref[
            pl.ds(row // 8 * 8 * (halves // 2) + row % 8, halves // 2, stride=8), :
        ] = line
    for group in range(rows // 8):
        for tile in range(halves // 2):
            at = (group * (halves // 2) + tile) * 8
            out_ref[group * 8 : group * 8 + 8, tile * LANES : (tile + 1) * LANES] = flat_ref[
                at : at + 8, :
            ]


def spectrum_tables(sources, window, margin, tiles):
    fold = SAMPLES // LANES
    k = np.arange(fold)
    n = np.arange(LANES)
    m = np.arange(64)

    def angle(product, period):
        return np.float32(2.0 * math.pi / period) * (product % period).astype(np.float32)

    one = angle(k[:, None] * k[None, :], fold)
    table_one = np.concatenate([np.cos(one), np.sin(one)], axis=0)
    first = np.zeros((2 * fold, sources * tiles), np.float32)
    for source in range(sources):
        start = (source * window) // LANES - margin // LANES
        for tile in range(tiles):
            if 0 <= start + tile < fold:
                first[:, source * tiles + tile] = table_one[:, start + tile]
    two = angle(k[:, None] * n[None, :], SAMPLES)
    m = np.concatenate([m[0::2], m[1::2]])
    three = angle(m[:, None] * n[None, :], LANES)
    third = np.concatenate([np.cos(three), np.sin(three)], axis=0)
    return (
        jnp.asarray(first, jnp.bfloat16),
        jnp.asarray(np.cos(two), jnp.float32),
        jnp.asarray(np.sin(two), jnp.float32),
        jnp.asarray(third, jnp.bfloat16),
    )


def slice_plan(samples, channel_order, merge_table):
    owners = lax.axis_size("sub")
    window, channels = samples.shape
    levels, _, dmax = merge_table.shape
    margin = window * owners - SAMPLES
    rows = dmax // owners
    step = math.gcd(window, LANES)
    body = -(-(window + LANES - step) // LANES)
    width = margin + body * LANES
    kept = margin // 2 + window
    vmem = pl.BlockSpec(memory_space=pltpu.VMEM)
    partial = pl.pallas_call(
        functools.partial(tree_kernel, owners, margin),
        out_shape=jax.ShapeDtypeStruct((owners, rows, width), jnp.bfloat16),
        in_specs=[pl.BlockSpec(memory_space=pl.ANY), vmem, vmem],
        out_specs=vmem,
        scratch_shapes=[
            pltpu.VMEM((window, channels), jnp.bfloat16),
            pltpu.VMEM((channels, 2 * dmax), jnp.bfloat16),
            pltpu.VMEM((levels - 1, dmax, 2 * dmax), jnp.bfloat16),
            pltpu.VMEM((kept, dmax), jnp.bfloat16),
            pltpu.VMEM((kept, 2 * dmax), jnp.float32),
            pltpu.VMEM((width, dmax), jnp.bfloat16),
            pltpu.SemaphoreType.DMA,
        ],
        name="tree",
    )(samples, channel_order.reshape(1, channels), merge_table)
    got = lax.all_to_all(partial, "sub", split_axis=0, concat_axis=0, tiled=True)
    tables = spectrum_tables(owners, window, margin, width // LANES)
    used = owners * width // LANES
    pitch = used + 1
    return pl.pallas_call(
        functools.partial(spectrum_kernel, window, margin, 1.0 / (SAMPLES * channels)),
        out_shape=jax.ShapeDtypeStruct((rows, SAMPLES // 2), jnp.float32),
        in_specs=[vmem] * 5,
        out_specs=vmem,
        scratch_shapes=[
            pltpu.VMEM((rows * pitch, LANES), jnp.float32),
            pltpu.VMEM((rows * SAMPLES // 2 // LANES, LANES), jnp.float32),
        ],
        name="spectrum",
    )(got, *tables)


def local(samples, channel_order, merge_table):
    owners = lax.axis_size("sub")
    window, channels = samples.shape
    dmax = merge_table.shape[2]
    margin = window * owners - SAMPLES
    fits = (
        dmax == 256
        and channels == 2 * dmax
        and dmax == 16 * owners
        and margin == dmax
        and window % 16 == 0
        and window <= 1024
    )
    plan = slice_plan if fits else owner_plan
    return plan(samples, channel_order, merge_table)


def solution(mesh):
    in_specs = (P(("groups", "sub"), None), P(), P())
    out_specs = P(("groups", "sub"), None)
    return jax.shard_map(local, mesh=mesh, in_specs=in_specs, out_specs=out_specs, check_vma=False)
```

```python
import functools
import math

import jax
import jax.numpy as jnp
import numpy as np
from jax import lax
from jax.experimental import pallas as pl
from jax.experimental.pallas import tpu as pltpu
from jax.sharding import PartitionSpec as P

LOCAL = 5
CH_DEV = 32
SAMPLES = 8192
LANES = 128


def from_partner(block, axis, apart):
    count = lax.axis_size(axis)
    route = []
    for low in range(count):
        high = low | 1 << apart
        if high != low and high < count:
            route += [(low, high), (high, low)]
    return lax.ppermute(block, axis, route)


def delay_rows(values, shifts, margin, time_axis):
    moved = values
    for bit_num in range(max(1, margin.bit_length())):
        offset = 2**bit_num
        rolled = jnp.pad(moved[:, offset:], ((0, 0), (0, offset)))
        flagged = shifts >> bit_num & 1 == 1
        flagged = flagged[:, None]
        moved = jnp.where(flagged, rolled, moved)
    return moved


def merge_level(current, entries, child_rows, span_rows, time_axis):
    outputs = jnp.arange(entries.shape[1], dtype=jnp.int32)
    starts = 2 * child_rows * (outputs // span_rows)
    lower_rows = jnp.take(current, starts + entries[0], axis=1 - time_axis)
    upper_rows = jnp.take(current, starts + child_rows + entries[1], axis=1 - time_axis)
    moved_rows = delay_rows(upper_rows, entries[2], child_rows, time_axis)
    return (lower_rows.astype(jnp.float32) + moved_rows.astype(jnp.float32)).astype(jnp.bfloat16)


def spectrum(delays, channels):
    row_count = delays.shape[0]
    length = delays.shape[1]
    fold_size = length // 128
    first_index = jnp.arange(fold_size, dtype=jnp.int32)
    lane_index = jnp.arange(128, dtype=jnp.int32)
    half_index = jnp.arange(64, dtype=jnp.int32)
    angle_one = (
        2.0
        * math.pi
        / fold_size
        * (first_index[:, None] * first_index[None, :] % fold_size).astype(jnp.float32)
    )
    cos_one = jnp.cos(angle_one).astype(jnp.bfloat16)
    sin_one = jnp.sin(angle_one).astype(jnp.bfloat16)
    angle_two = (
        2.0
        * math.pi
        / length
        * (first_index[:, None] * lane_index[None, :] % length).astype(jnp.float32)
    )
    twist_cos = jnp.cos(angle_two)
    twist_sin = jnp.sin(angle_two)
    angle_three = (
        2.0 * math.pi / 128 * (lane_index[:, None] * half_index[None, :] % 128).astype(jnp.float32)
    )
    cos_three = jnp.cos(angle_three).astype(jnp.bfloat16)
    sin_three = jnp.sin(angle_three).astype(jnp.bfloat16)
    series = delays.reshape(row_count, fold_size, 128)
    first_re = jnp.einsum("kn,rnm->rkm", cos_one, series, preferred_element_type=jnp.float32)
    first_im = -jnp.einsum("kn,rnm->rkm", sin_one, series, preferred_element_type=jnp.float32)
    twisted_re = (first_re * twist_cos + first_im * twist_sin).astype(jnp.bfloat16)
    twisted_im = (first_im * twist_cos - first_re * twist_sin).astype(jnp.bfloat16)
    out_re = jnp.einsum(
        "rkn,nj->rjk", twisted_re, cos_three, preferred_element_type=jnp.float32
    ) + jnp.einsum("rkn,nj->rjk", twisted_im, sin_three, preferred_element_type=jnp.float32)
    out_im = jnp.einsum(
        "rkn,nj->rjk", twisted_im, cos_three, preferred_element_type=jnp.float32
    ) - jnp.einsum("rkn,nj->rjk", twisted_re, sin_three, preferred_element_type=jnp.float32)
    power = (out_re * out_re + out_im * out_im) / (length * channels)
    return power.reshape(row_count, 64 * fold_size)


def owner_plan(samples, channel_order, merge_table):
    owners = lax.axis_size("sub")
    owner_index = lax.axis_index("sub")
    owned_rows = CH_DEV // 2
    quarter = CH_DEV // 4
    window = samples.shape[0]
    channels = samples.shape[1]
    ordered = jnp.take(samples, channel_order, axis=1).T.reshape(owners, CH_DEV, window)
    current = lax.all_to_all(ordered, "sub", split_axis=0, concat_axis=2, tiled=True).reshape(
        CH_DEV, window * owners
    )
    for level_num in range(1, LOCAL + 1):
        entries = lax.dynamic_slice_in_dim(
            merge_table[level_num - 1], owner_index * owned_rows, owned_rows, 1
        )
        current = merge_level(
            current, entries, max(1, 2 ** (level_num - 2)), 2 ** (level_num - 1), 1
        )
    block_index = jnp.zeros((), jnp.int32)
    for bit_num in range(owners.bit_length() - 1):
        level_num = LOCAL + bit_num + 1
        half_bit = owner_index >> bit_num & 1
        block_index = block_index * 2 + half_bit
        span_rows = owned_rows * 2 ** (bit_num + 1)
        child_rows = span_rows // 2
        subband = owner_index >> bit_num + 1
        entries = lax.dynamic_slice_in_dim(
            merge_table[level_num - 1],
            subband * span_rows + owned_rows * block_index,
            owned_rows,
            1,
        )
        kept_rows = lax.dynamic_slice_in_dim(current, half_bit * quarter, quarter, 0)
        sent_rows = lax.dynamic_slice_in_dim(current, (1 - half_bit) * quarter, quarter, 0)
        partner = from_partner(sent_rows, "sub", bit_num)
        row_base = quarter * block_index
        is_low = half_bit == 0
        lower_part = jnp.where(is_low, kept_rows, partner)
        upper_part = jnp.where(is_low, partner, kept_rows)
        lower_rows = jnp.take(lower_part, entries[0] - row_base, axis=0)
        upper_rows = jnp.take(upper_part, entries[1] - row_base, axis=0)
        moved_rows = delay_rows(upper_rows, entries[2], child_rows, 1)
        current = (lower_rows.astype(jnp.float32) + moved_rows.astype(jnp.float32)).astype(
            jnp.bfloat16
        )
    return spectrum(current[:, :SAMPLES], channels)


def reverse_bits(value, bits):
    flipped = 0
    for bit_num in range(bits):
        flipped |= (value >> bit_num & 1) << (bits - 1 - bit_num)
    return flipped


def take_along(values, index, axis):
    along = lax.GatherDimensionNumbers(
        offset_dims=(),
        collapsed_slice_dims=(axis,),
        start_index_map=(axis,),
        operand_batching_dims=(1 - axis,),
        start_indices_batching_dims=(1 - axis,),
    )
    return lax.gather(
        values, index[:, :, None], along, (1, 1), mode=lax.GatherScatterMode.PROMISE_IN_BOUNDS
    )


def tree_kernel(
    owners, margin, samples_ref, order_ref, table_ref, out_ref, raw_ref, first_ref, pick_ref,
    cur_ref, picked_ref, final_ref, sem,
):
    window, channels = samples_ref.shape
    levels, _, dmax = table_ref.shape
    quarter = CH_DEV // 4
    pad = margin // 2
    length = pad + window
    offset = (lax.axis_index("sub") * window) % LANES
    load = pltpu.make_async_copy(samples_ref, raw_ref, sem)
    load.start()

    final_ref[...] = jnp.zeros(final_ref.shape, final_ref.dtype)
    lane = lax.broadcasted_iota(jnp.int32, (8, LANES), 1)
    place = lax.broadcasted_iota(jnp.int32, (channels, LANES), 0)
    for side in range(2):
        for tile in range(dmax // LANES):
            parts = [
                take_along(
                    jnp.broadcast_to(
                        order_ref[:, (2 * tile + part) * LANES : (2 * tile + part + 1) * LANES],
                        (8, LANES),
                    ),
                    (2 * lane + side) & (LANES - 1),
                    1,
                )
                for part in range(2)
            ]
            chosen = jnp.where(lane < LANES // 2, parts[0], parts[1])[:1]
            at = side * dmax + tile * LANES
            first_ref[:, at : at + LANES] = jnp.where(place == chosen, 1.0, 0.0).astype(
                jnp.bfloat16
            )
    place = lax.broadcasted_iota(jnp.int32, (dmax, dmax), 0)
    index = lax.broadcasted_iota(jnp.int32, (1, dmax), 1)
    for level in range(1, levels):
        child = 2 ** (level - 1)
        start = (index >> level) * (2 * child)
        for side in range(2):
            chosen = start + side * child + table_ref[level, side : side + 1, :]
            pick_ref[level - 1, :, side * dmax : (side + 1) * dmax] = jnp.where(
                place == chosen, 1.0, 0.0
            ).astype(jnp.bfloat16)
    load.wait()

    row = lax.broadcasted_iota(jnp.int32, (8, LANES), 0)
    zero = jnp.zeros((8, LANES), jnp.float32)
    begin = pad
    for level in range(levels):
        last = level == levels - 1
        if level:
            picked_ref[begin:length, :] = jnp.dot(
                cur_ref[begin:length, :], pick_ref[level - 1], preferred_element_type=jnp.float32
            )
        else:
            picked_ref[begin:length, :] = jnp.dot(
                raw_ref[...], first_ref[...], preferred_element_type=jnp.float32
            )
        reached = (pad - 2**level) // 16 * 16
        for tile in range(dmax // LANES):
            output = tile * LANES + lane
            steps = (output & (2**level - 1)) // (2 * quarter)
            least = (tile * LANES & (2**level - 1)) // (2 * quarter)
            most = ((tile * LANES + LANES - 1) & (2**level - 1)) // (2 * quarter)
            if 2**level <= LANES:
                least, most = 0, (2**level - 1) // (2 * quarter)
            bits = (most - least).bit_length()
            shift = jnp.broadcast_to(
                table_ref[level, 2:3, tile * LANES : (tile + 1) * LANES], (8, LANES)
            )
            rest = row + shift - steps * quarter
            here = rest < 8
            source = rest & 7
            flags = [((steps - least) >> bit & 1) == 1 for bit in range(bits)]
            known = {}

            def coarse(bit, at):
                if at >= length // 8:
                    return None
                if (bit, at) not in known:
                    if bit == 0:
                        known[bit, at] = (
                            picked_ref[
                                at * 8 : at * 8 + 8,
                                dmax + tile * LANES : dmax + (tile + 1) * LANES,
                            ]
                            if at * 8 >= begin
                            else None
                        )
                    else:
                        near, far = coarse(bit - 1, at), coarse(bit - 1, at + 2 ** (bit - 1))
                        if near is None and far is None:
                            known[bit, at] = None
                        else:
                            near = zero if near is None else near
                            far = zero if far is None else far
                            known[bit, at] = jnp.where(flags[bit - 1], far, near)
                return known[bit, at]

            def fine(at):
                if ("fine", at) not in known:
                    value = coarse(bits, at + least)
                    known["fine", at] = None if value is None else take_along(value, source, 0)
                return known["fine", at]

            def merged(at):
                near, far = fine(at), fine(at + 1)
                total = None
                if near is not None or far is not None:
                    total = jnp.where(
                        here, zero if near is None else near, zero if far is None else far
                    )
                if begin <= at * 8:
                    low = picked_ref[at * 8 : at * 8 + 8, tile * LANES : (tile + 1) * LANES]
                    total = low if total is None else low + total
                return zero if total is None else total

            lanes = slice(tile * LANES, (tile + 1) * LANES)
            for at in range(reached // 8, length // 8, 2):
                both = jnp.concatenate([merged(at), merged(at + 1)], axis=0).astype(jnp.bfloat16)
                if last:
                    to = pl.multiple_of(offset + at * 8 + pad, 16)
                    final_ref[pl.ds(to, 16), lanes] = both
                else:
                    cur_ref[at * 8 : at * 8 + 16, lanes] = both
        begin = max(reached, 0)

    for tile in range(dmax // LANES):
        for time in range(final_ref.shape[0] // LANES):
            lanes = slice(time * LANES, (time + 1) * LANES)
            turned = final_ref[lanes, tile * LANES : (tile + 1) * LANES].T
            for block in range(LANES // 16):
                owner = reverse_bits(tile * (LANES // 16) + block, (owners - 1).bit_length())
                out_ref[owner, :, lanes] = turned[block * 16 : (block + 1) * 16]


def spectrum_kernel(
    window, margin, scale, got_ref, first_ref, cos_ref, sin_ref, third_ref, out_ref, slot_ref,
    flat_ref, lines_ref, sems,
):
    sources, rows, width = got_ref.shape
    tiles = width // LANES
    pitch = slot_ref.shape[0] // rows
    used = sources * tiles
    bins = first_ref.shape[0] // 2
    halves = third_ref.shape[0] // 2
    for source in range(sources):
        for tile in range(tiles):
            slot_ref[pl.ds(source * tiles + tile, rows, stride=pitch), :] = got_ref[
                source, :, tile * LANES : (tile + 1) * LANES
            ].astype(jnp.float32)
    lane = lax.broadcasted_iota(jnp.int32, (halves // 2, LANES), 1)
    sign = jnp.where(lax.broadcasted_iota(jnp.int32, (halves, LANES), 1) < bins, 1.0, -1.0)
    stores = []
    for row in range(rows):
        series = slot_ref[row * pitch : row * pitch + used, :].astype(jnp.bfloat16)
        turned = jnp.dot(first_ref[...], series, preferred_element_type=jnp.float32)
        real, imag = turned[:bins], turned[bins:]
        twisted_re = (real * cos_ref[...] - imag * sin_ref[...]).astype(jnp.bfloat16)
        twisted_im = (-imag * cos_ref[...] - real * sin_ref[...]).astype(jnp.bfloat16)
        twisted = jnp.concatenate([twisted_re, twisted_im], axis=0)
        mixed = lax.dot_general(
            third_ref[...], twisted, (((1,), (1,)), ((), ())), preferred_element_type=jnp.float32
        )
        value = mixed[:halves] + sign * pltpu.roll(mixed[halves:], bins, axis=1)
        square = value * value
        power = (square + pltpu.roll(square, bins, axis=1)) * scale
        line = jnp.where(lane < bins, power[: halves // 2], power[halves // 2 :])
        flat_ref[
            pl.ds(row // 8 * 8 * (halves // 2) + row % 8, halves // 2, stride=8), :
        ] = line
        if row % 8 == 7:
            group = row // 8
            for tile in range(halves // 2):
                at = (group * (halves // 2) + tile) * 8
                lines_ref[group * 8 : group * 8 + 8, tile * LANES : (tile + 1) * LANES] = flat_ref[
                    at : at + 8, :
                ]
            stores.append(
                pltpu.make_async_copy(
                    lines_ref.at[pl.ds(group * 8, 8)],
                    out_ref.at[pl.ds(group * 8, 8)],
                    sems.at[group],
                )
            )
            stores[-1].start()
    for store in stores:
        store.wait()


def spectrum_tables(sources, window, margin, tiles):
    fold = SAMPLES // LANES
    k = np.arange(fold)
    n = np.arange(LANES)
    m = np.arange(64)

    def angle(product, period):
        return np.float32(2.0 * math.pi / period) * (product % period).astype(np.float32)

    one = angle(k[:, None] * k[None, :], fold)
    table_one = np.concatenate([np.cos(one), np.sin(one)], axis=0)
    first = np.zeros((2 * fold, sources * tiles), np.float32)
    for source in range(sources):
        start = (source * window) // LANES - margin // LANES
        for tile in range(tiles):
            if 0 <= start + tile < fold:
                first[:, source * tiles + tile] = table_one[:, start + tile]
    two = angle(k[:, None] * n[None, :], SAMPLES)
    m = np.concatenate([m[0::2], m[1::2]])
    three = angle(m[:, None] * n[None, :], LANES)
    third = np.concatenate([np.cos(three), np.sin(three)], axis=0)
    return (
        jnp.asarray(first, jnp.bfloat16),
        jnp.asarray(np.cos(two), jnp.float32),
        jnp.asarray(np.sin(two), jnp.float32),
        jnp.asarray(third, jnp.bfloat16),
    )


def slice_plan(samples, channel_order, merge_table):
    owners = lax.axis_size("sub")
    window, channels = samples.shape
    levels, _, dmax = merge_table.shape
    margin = window * owners - SAMPLES
    rows = dmax // owners
    step = math.gcd(window, LANES)
    body = -(-(window + LANES - step) // LANES)
    width = margin + body * LANES
    kept = margin // 2 + window
    vmem = pl.BlockSpec(memory_space=pltpu.VMEM)
    partial = pl.pallas_call(
        functools.partial(tree_kernel, owners, margin),
        out_shape=pltpu.VMEM((owners, rows, width), jnp.bfloat16),
        in_specs=[pl.BlockSpec(memory_space=pl.ANY), vmem, vmem],
        out_specs=vmem,
        scratch_shapes=[
            pltpu.VMEM((window, channels), jnp.bfloat16),
            pltpu.VMEM((channels, 2 * dmax), jnp.bfloat16),
            pltpu.VMEM((levels - 1, dmax, 2 * dmax), jnp.bfloat16),
            pltpu.VMEM((kept, dmax), jnp.bfloat16),
            pltpu.VMEM((kept, 2 * dmax), jnp.float32),
            pltpu.VMEM((width, dmax), jnp.bfloat16),
            pltpu.SemaphoreType.DMA,
        ],
        name="tree",
    )(samples, channel_order.reshape(1, channels), merge_table)
    got = lax.all_to_all(partial, "sub", split_axis=0, concat_axis=0, tiled=True)
    got = pltpu.with_memory_space_constraint(got, pltpu.VMEM)
    tables = [
        pltpu.with_memory_space_constraint(table, pltpu.VMEM)
        for table in spectrum_tables(owners, window, margin, width // LANES)
    ]
    used = owners * width // LANES
    pitch = used + 1
    return pl.pallas_call(
        functools.partial(spectrum_kernel, window, margin, 1.0 / (SAMPLES * channels)),
        out_shape=jax.ShapeDtypeStruct((rows, SAMPLES // 2), jnp.float32),
        in_specs=[vmem] * 5,
        out_specs=pl.BlockSpec(memory_space=pl.ANY),
        scratch_shapes=[
            pltpu.VMEM((rows * pitch, LANES), jnp.float32),
            pltpu.VMEM((rows * SAMPLES // 2 // LANES, LANES), jnp.float32),
            pltpu.VMEM((rows, SAMPLES // 2), jnp.float32),
            pltpu.SemaphoreType.DMA((rows // 8,)),
        ],
        name="spectrum",
    )(got, *tables)


def local(samples, channel_order, merge_table):
    owners = lax.axis_size("sub")
    window, channels = samples.shape
    dmax = merge_table.shape[2]
    margin = window * owners - SAMPLES
    fits = (
        dmax == 256
        and channels == 2 * dmax
        and dmax == 16 * owners
        and margin == dmax
        and window % 16 == 0
        and window <= 1024
    )
    plan = slice_plan if fits else owner_plan
    return plan(samples, channel_order, merge_table)


def solution(mesh):
    in_specs = (P(("groups", "sub"), None), P(), P())
    out_specs = P(("groups", "sub"), None)
    return jax.shard_map(local, mesh=mesh, in_specs=in_specs, out_specs=out_specs, check_vma=False)
```

```python
import functools
import math

import jax
import jax.numpy as jnp
import numpy as np
from jax import lax
from jax.experimental import pallas as pl
from jax.experimental.pallas import tpu as pltpu
from jax.sharding import PartitionSpec as P

LOCAL = 5
CH_DEV = 32
SAMPLES = 8192
LANES = 128


def from_partner(block, axis, apart):
    count = lax.axis_size(axis)
    route = []
    for low in range(count):
        high = low | 1 << apart
        if high != low and high < count:
            route += [(low, high), (high, low)]
    return lax.ppermute(block, axis, route)


def delay_rows(values, shifts, margin, time_axis):
    moved = values
    for bit_num in range(max(1, margin.bit_length())):
        offset = 2**bit_num
        rolled = jnp.pad(moved[:, offset:], ((0, 0), (0, offset)))
        flagged = shifts >> bit_num & 1 == 1
        flagged = flagged[:, None]
        moved = jnp.where(flagged, rolled, moved)
    return moved


def merge_level(current, entries, child_rows, span_rows, time_axis):
    outputs = jnp.arange(entries.shape[1], dtype=jnp.int32)
    starts = 2 * child_rows * (outputs // span_rows)
    lower_rows = jnp.take(current, starts + entries[0], axis=1 - time_axis)
    upper_rows = jnp.take(current, starts + child_rows + entries[1], axis=1 - time_axis)
    moved_rows = delay_rows(upper_rows, entries[2], child_rows, time_axis)
    return (lower_rows.astype(jnp.float32) + moved_rows.astype(jnp.float32)).astype(jnp.bfloat16)


def spectrum(delays, channels):
    row_count = delays.shape[0]
    length = delays.shape[1]
    fold_size = length // 128
    first_index = jnp.arange(fold_size, dtype=jnp.int32)
    lane_index = jnp.arange(128, dtype=jnp.int32)
    half_index = jnp.arange(64, dtype=jnp.int32)
    angle_one = (
        2.0
        * math.pi
        / fold_size
        * (first_index[:, None] * first_index[None, :] % fold_size).astype(jnp.float32)
    )
    cos_one = jnp.cos(angle_one).astype(jnp.bfloat16)
    sin_one = jnp.sin(angle_one).astype(jnp.bfloat16)
    angle_two = (
        2.0
        * math.pi
        / length
        * (first_index[:, None] * lane_index[None, :] % length).astype(jnp.float32)
    )
    twist_cos = jnp.cos(angle_two)
    twist_sin = jnp.sin(angle_two)
    angle_three = (
        2.0 * math.pi / 128 * (lane_index[:, None] * half_index[None, :] % 128).astype(jnp.float32)
    )
    cos_three = jnp.cos(angle_three).astype(jnp.bfloat16)
    sin_three = jnp.sin(angle_three).astype(jnp.bfloat16)
    series = delays.reshape(row_count, fold_size, 128)
    first_re = jnp.einsum("kn,rnm->rkm", cos_one, series, preferred_element_type=jnp.float32)
    first_im = -jnp.einsum("kn,rnm->rkm", sin_one, series, preferred_element_type=jnp.float32)
    twisted_re = (first_re * twist_cos + first_im * twist_sin).astype(jnp.bfloat16)
    twisted_im = (first_im * twist_cos - first_re * twist_sin).astype(jnp.bfloat16)
    out_re = jnp.einsum(
        "rkn,nj->rjk", twisted_re, cos_three, preferred_element_type=jnp.float32
    ) + jnp.einsum("rkn,nj->rjk", twisted_im, sin_three, preferred_element_type=jnp.float32)
    out_im = jnp.einsum(
        "rkn,nj->rjk", twisted_im, cos_three, preferred_element_type=jnp.float32
    ) - jnp.einsum("rkn,nj->rjk", twisted_re, sin_three, preferred_element_type=jnp.float32)
    power = (out_re * out_re + out_im * out_im) / (length * channels)
    return power.reshape(row_count, 64 * fold_size)


def owner_plan(samples, channel_order, merge_table):
    owners = lax.axis_size("sub")
    owner_index = lax.axis_index("sub")
    owned_rows = CH_DEV // 2
    quarter = CH_DEV // 4
    window = samples.shape[0]
    channels = samples.shape[1]
    ordered = jnp.take(samples, channel_order, axis=1).T.reshape(owners, CH_DEV, window)
    current = lax.all_to_all(ordered, "sub", split_axis=0, concat_axis=2, tiled=True).reshape(
        CH_DEV, window * owners
    )
    for level_num in range(1, LOCAL + 1):
        entries = lax.dynamic_slice_in_dim(
            merge_table[level_num - 1], owner_index * owned_rows, owned_rows, 1
        )
        current = merge_level(
            current, entries, max(1, 2 ** (level_num - 2)), 2 ** (level_num - 1), 1
        )
    block_index = jnp.zeros((), jnp.int32)
    for bit_num in range(owners.bit_length() - 1):
        level_num = LOCAL + bit_num + 1
        half_bit = owner_index >> bit_num & 1
        block_index = block_index * 2 + half_bit
        span_rows = owned_rows * 2 ** (bit_num + 1)
        child_rows = span_rows // 2
        subband = owner_index >> bit_num + 1
        entries = lax.dynamic_slice_in_dim(
            merge_table[level_num - 1],
            subband * span_rows + owned_rows * block_index,
            owned_rows,
            1,
        )
        kept_rows = lax.dynamic_slice_in_dim(current, half_bit * quarter, quarter, 0)
        sent_rows = lax.dynamic_slice_in_dim(current, (1 - half_bit) * quarter, quarter, 0)
        partner = from_partner(sent_rows, "sub", bit_num)
        row_base = quarter * block_index
        is_low = half_bit == 0
        lower_part = jnp.where(is_low, kept_rows, partner)
        upper_part = jnp.where(is_low, partner, kept_rows)
        lower_rows = jnp.take(lower_part, entries[0] - row_base, axis=0)
        upper_rows = jnp.take(upper_part, entries[1] - row_base, axis=0)
        moved_rows = delay_rows(upper_rows, entries[2], child_rows, 1)
        current = (lower_rows.astype(jnp.float32) + moved_rows.astype(jnp.float32)).astype(
            jnp.bfloat16
        )
    return spectrum(current[:, :SAMPLES], channels)


def reverse_bits(value, bits):
    flipped = 0
    for bit_num in range(bits):
        flipped |= (value >> bit_num & 1) << (bits - 1 - bit_num)
    return flipped


def take_along(values, index, axis):
    along = lax.GatherDimensionNumbers(
        offset_dims=(),
        collapsed_slice_dims=(axis,),
        start_index_map=(axis,),
        operand_batching_dims=(1 - axis,),
        start_indices_batching_dims=(1 - axis,),
    )
    return lax.gather(
        values, index[:, :, None], along, (1, 1), mode=lax.GatherScatterMode.PROMISE_IN_BOUNDS
    )


def tree_kernel(
    owners, margin, samples_ref, order_ref, table_ref, keep_ref, send_ref, raw_ref, first_ref,
    pick_ref, cur_ref, picked_ref, final_ref, turned_ref, sem,
):
    window, channels = samples_ref.shape
    levels, _, dmax = table_ref.shape
    quarter = CH_DEV // 4
    pad = margin // 2
    length = pad + window
    offset = (lax.axis_index("sub") * window) % LANES
    load = pltpu.make_async_copy(samples_ref, raw_ref, sem)
    load.start()

    final_ref[...] = jnp.zeros(final_ref.shape, final_ref.dtype)
    lane = lax.broadcasted_iota(jnp.int32, (8, LANES), 1)
    place = lax.broadcasted_iota(jnp.int32, (channels, LANES), 0)
    for side in range(2):
        for tile in range(dmax // LANES):
            parts = [
                take_along(
                    jnp.broadcast_to(
                        order_ref[:, (2 * tile + part) * LANES : (2 * tile + part + 1) * LANES],
                        (8, LANES),
                    ),
                    (2 * lane + side) & (LANES - 1),
                    1,
                )
                for part in range(2)
            ]
            chosen = jnp.where(lane < LANES // 2, parts[0], parts[1])[:1]
            at = side * dmax + tile * LANES
            first_ref[:, at : at + LANES] = jnp.where(place == chosen, 1.0, 0.0).astype(
                jnp.bfloat16
            )
    place = lax.broadcasted_iota(jnp.int32, (dmax, dmax), 0)
    index = lax.broadcasted_iota(jnp.int32, (1, dmax), 1)
    for level in range(1, levels):
        child = 2 ** (level - 1)
        start = (index >> level) * (2 * child)
        for side in range(2):
            chosen = start + side * child + table_ref[level, side : side + 1, :]
            pick_ref[level - 1, :, side * dmax : (side + 1) * dmax] = jnp.where(
                place == chosen, 1.0, 0.0
            ).astype(jnp.bfloat16)
    load.wait()

    row = lax.broadcasted_iota(jnp.int32, (8, LANES), 0)
    zero = jnp.zeros((8, LANES), jnp.float32)
    begin = pad
    for level in range(levels):
        last = level == levels - 1
        if level:
            picked_ref[begin:length, :] = jnp.dot(
                cur_ref[begin:length, :], pick_ref[level - 1], preferred_element_type=jnp.float32
            )
        else:
            picked_ref[begin:length, :] = jnp.dot(
                raw_ref[...], first_ref[...], preferred_element_type=jnp.float32
            )
        reached = (pad - 2**level) // 16 * 16
        for tile in range(dmax // LANES):
            output = tile * LANES + lane
            steps = (output & (2**level - 1)) // (2 * quarter)
            least = (tile * LANES & (2**level - 1)) // (2 * quarter)
            most = ((tile * LANES + LANES - 1) & (2**level - 1)) // (2 * quarter)
            if 2**level <= LANES:
                least, most = 0, (2**level - 1) // (2 * quarter)
            bits = (most - least).bit_length()
            shift = jnp.broadcast_to(
                table_ref[level, 2:3, tile * LANES : (tile + 1) * LANES], (8, LANES)
            )
            rest = row + shift - steps * quarter
            here = rest < 8
            source = rest & 7
            flags = [((steps - least) >> bit & 1) == 1 for bit in range(bits)]
            known = {}

            def coarse(bit, at):
                if at >= length // 8:
                    return None
                if (bit, at) not in known:
                    if bit == 0:
                        known[bit, at] = (
                            picked_ref[
                                at * 8 : at * 8 + 8,
                                dmax + tile * LANES : dmax + (tile + 1) * LANES,
                            ]
                            if at * 8 >= begin
                            else None
                        )
                    else:
                        near, far = coarse(bit - 1, at), coarse(bit - 1, at + 2 ** (bit - 1))
                        if near is None and far is None:
                            known[bit, at] = None
                        else:
                            near = zero if near is None else near
                            far = zero if far is None else far
                            known[bit, at] = jnp.where(flags[bit - 1], far, near)
                return known[bit, at]

            def fine(at):
                if ("fine", at) not in known:
                    value = coarse(bits, at + least)
                    known["fine", at] = None if value is None else take_along(value, source, 0)
                return known["fine", at]

            def merged(at):
                near, far = fine(at), fine(at + 1)
                total = None
                if near is not None or far is not None:
                    total = jnp.where(
                        here, zero if near is None else near, zero if far is None else far
                    )
                if begin <= at * 8:
                    low = picked_ref[at * 8 : at * 8 + 8, tile * LANES : (tile + 1) * LANES]
                    total = low if total is None else low + total
                return zero if total is None else total

            lanes = slice(tile * LANES, (tile + 1) * LANES)
            for at in range(reached // 8, length // 8, 2):
                both = jnp.concatenate([merged(at), merged(at + 1)], axis=0).astype(jnp.bfloat16)
                if last:
                    to = pl.multiple_of(offset + at * 8 + pad, 16)
                    final_ref[pl.ds(to, 16), lanes] = both
                else:
                    cur_ref[at * 8 : at * 8 + 16, lanes] = both
        begin = max(reached, 0)

    for tile in range(dmax // LANES):
        at = slice(tile * LANES, (tile + 1) * LANES)
        for time in range(final_ref.shape[0] // LANES):
            lanes = slice(time * LANES, (time + 1) * LANES)
            turned_ref[at, lanes] = final_ref[lanes, at].T
    me = lax.axis_index("sub")
    bits = (owners - 1).bit_length()
    rows = dmax // owners
    for ref, core in ((keep_ref, me & 1), (send_ref, 1 - (me & 1))):
        for ring in range(ref.shape[0]):
            for relay in range(2):
                chip, side = (2 * ring + core, core ^ relay) if ring else (relay, core)
                block = reverse_bits(((me >> 1) ^ chip) << 1 | side, bits)
                ref[ring, relay] = turned_ref[pl.ds(pl.multiple_of(block * rows, rows), rows), :]


def pair_kernel(apart, keep_ref, got_ref, own_ref, near_ref, *message_refs):
    lower = lax.axis_index("sub") & 1 == 0
    tiles = keep_ref.shape[-1] // LANES
    for ring in range(keep_ref.shape[0]):
        for relay in range(2):
            for tile in range(apart + tiles):
                total = None
                for start, mine in ((0, lower), (apart, ~lower)):
                    if start <= tile < start + tiles:
                        lanes = slice((tile - start) * LANES, (tile - start + 1) * LANES)
                        part = jnp.where(
                            mine, keep_ref[ring, relay, :, lanes], got_ref[ring, relay, :, lanes]
                        ).astype(jnp.float32)
                        total = part if total is None else total + part
                total = total.astype(own_ref.dtype)
                lanes = slice(tile * LANES, (tile + 1) * LANES)
                if ring:
                    message_refs[ring - 1][relay, :, lanes] = total
                else:
                    (near_ref if relay else own_ref)[:, lanes] = total


def relay_kernel(*refs):
    for at, ref in enumerate(refs[1:-1]):
        refs[-1][at] = ref[1]


def spectrum_kernel(
    rings, scale, own_ref, near_ref, *refs
):
    message_refs, refs = refs[: rings - 1], refs[rings - 1 :]
    relay_ref, first_ref, cos_ref, sin_ref, third_ref, out_ref = refs[:6]
    slot_ref, flat_ref, lines_ref, sems = refs[6:]
    rows, width = own_ref.shape
    tiles = width // LANES
    pitch = slot_ref.shape[0] // rows
    used = first_ref.shape[1]
    bins = first_ref.shape[0] // 2
    halves = third_ref.shape[0] // 2
    me = lax.axis_index("sub")
    core = me & 1
    sources = [(own_ref, (), 0), (near_ref, (), 1)]
    for ring in range(1, rings):
        sources.append((message_refs[ring - 1], (0,), 2 * ring + core))
        sources.append((relay_ref, (ring - 1,), 2 * ring + 1 - core))
    for ref, at, apart in sources:
        slot = ((me >> 1) ^ apart) * tiles
        for tile in range(tiles):
            slot_ref[pl.ds(slot + tile, rows, stride=pitch), :] = ref[
                at + (slice(None), slice(tile * LANES, (tile + 1) * LANES))
            ].astype(jnp.float32)
    lane = lax.broadcasted_iota(jnp.int32, (halves // 2, LANES), 1)
    sign = jnp.where(lax.broadcasted_iota(jnp.int32, (halves, LANES), 1) < bins, 1.0, -1.0)
    stores = []
    for row in range(rows):
        series = slot_ref[row * pitch : row * pitch + used, :].astype(jnp.bfloat16)
        turned = jnp.dot(first_ref[...], series, preferred_element_type=jnp.float32)
        real, imag = turned[:bins], turned[bins:]
        twisted_re = (real * cos_ref[...] - imag * sin_ref[...]).astype(jnp.bfloat16)
        twisted_im = (-imag * cos_ref[...] - real * sin_ref[...]).astype(jnp.bfloat16)
        twisted = jnp.concatenate([twisted_re, twisted_im], axis=0)
        mixed = lax.dot_general(
            third_ref[...], twisted, (((1,), (1,)), ((), ())), preferred_element_type=jnp.float32
        )
        value = mixed[:halves] + sign * pltpu.roll(mixed[halves:], bins, axis=1)
        square = value * value
        power = (square + pltpu.roll(square, bins, axis=1)) * scale
        line = jnp.where(lane < bins, power[: halves // 2], power[halves // 2 :])
        flat_ref[
            pl.ds(row // 8 * 8 * (halves // 2) + row % 8, halves // 2, stride=8), :
        ] = line
        if row % 8 == 7:
            group = row // 8
            for tile in range(halves // 2):
                at = (group * (halves // 2) + tile) * 8
                lines_ref[group * 8 : group * 8 + 8, tile * LANES : (tile + 1) * LANES] = flat_ref[
                    at : at + 8, :
                ]
            stores.append(
                pltpu.make_async_copy(
                    lines_ref.at[pl.ds(group * 8, 8)],
                    out_ref.at[pl.ds(group * 8, 8)],
                    sems.at[group],
                )
            )
            stores[-1].start()
    for store in stores:
        store.wait()


def spectrum_tables(sources, window, margin, tiles):
    fold = SAMPLES // LANES
    k = np.arange(fold)
    n = np.arange(LANES)
    m = np.arange(64)

    def angle(product, period):
        return np.float32(2.0 * math.pi / period) * (product % period).astype(np.float32)

    one = angle(k[:, None] * k[None, :], fold)
    table_one = np.concatenate([np.cos(one), np.sin(one)], axis=0)
    first = np.zeros((2 * fold, sources * tiles), np.float32)
    for source in range(sources):
        start = (source * window) // LANES - margin // LANES
        for tile in range(tiles):
            if 0 <= start + tile < fold:
                first[:, source * tiles + tile] = table_one[:, start + tile]
    two = angle(k[:, None] * n[None, :], SAMPLES)
    m = np.concatenate([m[0::2], m[1::2]])
    three = angle(m[:, None] * n[None, :], LANES)
    third = np.concatenate([np.cos(three), np.sin(three)], axis=0)
    return (
        jnp.asarray(first, jnp.bfloat16),
        jnp.asarray(np.cos(two), jnp.float32),
        jnp.asarray(np.sin(two), jnp.float32),
        jnp.asarray(third, jnp.bfloat16),
    )


def pairs_align(window, owners):
    starts = [at * window // LANES for at in range(owners)]
    return all(starts[at + 1] - starts[at] == window // LANES for at in range(0, owners, 2))


def on_chip(values):
    return pltpu.with_memory_space_constraint(values, pltpu.VMEM)


def slice_plan(samples, channel_order, merge_table):
    owners = lax.axis_size("sub")
    window, channels = samples.shape
    levels, _, dmax = merge_table.shape
    margin = window * owners - SAMPLES
    rows = dmax // owners
    rings = owners // 4
    step = math.gcd(window, LANES)
    width = margin + -(-(window + LANES - step) // LANES) * LANES
    kept = margin // 2 + window
    apart = window // LANES
    wide = width + apart * LANES
    vmem = pl.BlockSpec(memory_space=pltpu.VMEM)
    half = pltpu.VMEM((rings, 2, rows, width), jnp.bfloat16)
    keep, send = pl.pallas_call(
        functools.partial(tree_kernel, owners, margin),
        out_shape=[half, half],
        in_specs=[pl.BlockSpec(memory_space=pl.ANY), vmem, vmem],
        out_specs=[vmem, vmem],
        scratch_shapes=[
            pltpu.VMEM((window, channels), jnp.bfloat16),
            pltpu.VMEM((channels, 2 * dmax), jnp.bfloat16),
            pltpu.VMEM((levels - 1, dmax, 2 * dmax), jnp.bfloat16),
            pltpu.VMEM((kept, dmax), jnp.bfloat16),
            pltpu.VMEM((kept, 2 * dmax), jnp.float32),
            pltpu.VMEM((width, dmax), jnp.bfloat16),
            pltpu.VMEM((dmax, width), jnp.bfloat16),
            pltpu.SemaphoreType.DMA,
        ],
        name="tree",
    )(samples, channel_order.reshape(1, channels), merge_table)
    beside = [(low, low ^ 1) for low in range(owners)]
    got = on_chip(lax.ppermute(send, "sub", beside))
    block = pltpu.VMEM((rows, wide), jnp.bfloat16)
    message = pltpu.VMEM((2, rows, wide), jnp.bfloat16)
    own, near, *messages = pl.pallas_call(
        functools.partial(pair_kernel, apart),
        out_shape=[block, block] + [message] * (rings - 1),
        in_specs=[vmem] * 2,
        out_specs=[vmem] * (rings + 1),
        name="pair",
    )(on_chip(keep), got)
    arrived = [
        on_chip(
            lax.ppermute(
                messages[ring - 1], "sub", [(a, a ^ (2 * (2 * ring + a % 2))) for a in range(owners)]
            )
        )
        for ring in range(1, rings)
    ]
    near = on_chip(lax.ppermute(near, "sub", [(a, a ^ 2) for a in range(owners)]))
    relay = pl.pallas_call(
        relay_kernel,
        out_shape=pltpu.VMEM((rings - 1, rows, wide), jnp.bfloat16),
        in_specs=[vmem] * rings,
        out_specs=vmem,
        name="relay",
    )(near, *arrived)
    relay = on_chip(lax.ppermute(relay, "sub", beside))
    pairs = owners // 2
    tables = [
        on_chip(table) for table in spectrum_tables(pairs, 2 * window, margin, wide // LANES)
    ]
    pitch = pairs * wide // LANES + 1
    return pl.pallas_call(
        functools.partial(spectrum_kernel, rings, 1.0 / (SAMPLES * channels)),
        out_shape=jax.ShapeDtypeStruct((rows, SAMPLES // 2), jnp.float32),
        in_specs=[vmem] * (rings + 6),
        out_specs=pl.BlockSpec(memory_space=pl.ANY),
        scratch_shapes=[
            pltpu.VMEM((rows * pitch, LANES), jnp.float32),
            pltpu.VMEM((rows * SAMPLES // 2 // LANES, LANES), jnp.float32),
            pltpu.VMEM((rows, SAMPLES // 2), jnp.float32),
            pltpu.SemaphoreType.DMA((rows // 8,)),
        ],
        name="spectrum",
    )(on_chip(own), near, *arrived, relay, *tables)


def local(samples, channel_order, merge_table):
    owners = lax.axis_size("sub")
    window, channels = samples.shape
    dmax = merge_table.shape[2]
    margin = window * owners - SAMPLES
    fits = (
        dmax == 256
        and channels == 2 * dmax
        and dmax == 16 * owners
        and margin == dmax
        and window % 16 == 0
        and window <= 1024
        and owners % 8 == 0
        and pairs_align(window, owners)
    )
    plan = slice_plan if fits else owner_plan
    return plan(samples, channel_order, merge_table)


def solution(mesh):
    in_specs = (P(("groups", "sub"), None), P(), P())
    out_specs = P(("groups", "sub"), None)
    return jax.shard_map(local, mesh=mesh, in_specs=in_specs, out_specs=out_specs, check_vma=False)
```

```python
import functools
import math

import jax
import jax.numpy as jnp
import numpy as np
from jax import lax
from jax.experimental import pallas as pl
from jax.experimental.pallas import tpu as pltpu
from jax.sharding import PartitionSpec as P


LOCAL = 5
CH_DEV = 32
SAMPLES = 8192
LANES = 128


def from_partner(block, axis, apart):
    count = lax.axis_size(axis)
    route = []
    for low in range(count):
        high = low | 1 << apart
        if high != low and high < count:
            route += [(low, high), (high, low)]
    return lax.ppermute(block, axis, route)


def delay_rows(values, shifts, margin):
    moved = values
    for bit_num in range(max(1, margin.bit_length())):
        offset = 2**bit_num
        rolled = jnp.pad(moved[:, offset:], ((0, 0), (0, offset)))
        flagged = shifts >> bit_num & 1 == 1
        flagged = flagged[:, None]
        moved = jnp.where(flagged, rolled, moved)
    return moved


def merge_level(current, entries, child_rows, span_rows, time_axis):
    outputs = jnp.arange(entries.shape[1], dtype=jnp.int32)
    starts = 2 * child_rows * (outputs // span_rows)
    lower_rows = jnp.take(current, starts + entries[0], axis=1 - time_axis)
    upper_rows = jnp.take(current, starts + child_rows + entries[1], axis=1 - time_axis)
    moved_rows = delay_rows(upper_rows, entries[2], child_rows)
    return (lower_rows.astype(jnp.float32) + moved_rows.astype(jnp.float32)).astype(jnp.bfloat16)


def spectrum(delays, channels):
    row_count = delays.shape[0]
    length = delays.shape[1]
    fold_size = length // 128
    first_index = jnp.arange(fold_size, dtype=jnp.int32)
    lane_index = jnp.arange(128, dtype=jnp.int32)
    half_index = jnp.arange(64, dtype=jnp.int32)
    angle_one = (
        2.0
        * math.pi
        / fold_size
        * (first_index[:, None] * first_index[None, :] % fold_size).astype(jnp.float32)
    )
    cos_one = jnp.cos(angle_one).astype(jnp.bfloat16)
    sin_one = jnp.sin(angle_one).astype(jnp.bfloat16)
    angle_two = (
        2.0
        * math.pi
        / length
        * (first_index[:, None] * lane_index[None, :] % length).astype(jnp.float32)
    )
    twist_cos = jnp.cos(angle_two)
    twist_sin = jnp.sin(angle_two)
    angle_three = (
        2.0 * math.pi / 128 * (lane_index[:, None] * half_index[None, :] % 128).astype(jnp.float32)
    )
    cos_three = jnp.cos(angle_three).astype(jnp.bfloat16)
    sin_three = jnp.sin(angle_three).astype(jnp.bfloat16)
    series = delays.reshape(row_count, fold_size, 128)
    first_re = jnp.einsum("kn,rnm->rkm", cos_one, series, preferred_element_type=jnp.float32)
    first_im = -jnp.einsum("kn,rnm->rkm", sin_one, series, preferred_element_type=jnp.float32)
    twisted_re = (first_re * twist_cos + first_im * twist_sin).astype(jnp.bfloat16)
    twisted_im = (first_im * twist_cos - first_re * twist_sin).astype(jnp.bfloat16)
    out_re = jnp.einsum(
        "rkn,nj->rjk", twisted_re, cos_three, preferred_element_type=jnp.float32
    ) + jnp.einsum("rkn,nj->rjk", twisted_im, sin_three, preferred_element_type=jnp.float32)
    out_im = jnp.einsum(
        "rkn,nj->rjk", twisted_im, cos_three, preferred_element_type=jnp.float32
    ) - jnp.einsum("rkn,nj->rjk", twisted_re, sin_three, preferred_element_type=jnp.float32)
    power = (out_re * out_re + out_im * out_im) / (length * channels)
    return power.reshape(row_count, 64 * fold_size)


def owner_plan(samples, channel_order, merge_table):
    owners = lax.axis_size("sub")
    owner_index = lax.axis_index("sub")
    owned_rows = CH_DEV // 2
    quarter = CH_DEV // 4
    window = samples.shape[0]
    channels = samples.shape[1]
    ordered = jnp.take(samples, channel_order, axis=1).T.reshape(owners, CH_DEV, window)
    current = lax.all_to_all(ordered, "sub", split_axis=0, concat_axis=2, tiled=True).reshape(
        CH_DEV, window * owners
    )
    for level_num in range(1, LOCAL + 1):
        entries = lax.dynamic_slice_in_dim(
            merge_table[level_num - 1], owner_index * owned_rows, owned_rows, 1
        )
        current = merge_level(
            current, entries, max(1, 2 ** (level_num - 2)), 2 ** (level_num - 1), 1
        )
    block_index = jnp.zeros((), jnp.int32)
    for bit_num in range(owners.bit_length() - 1):
        level_num = LOCAL + bit_num + 1
        half_bit = owner_index >> bit_num & 1
        block_index = block_index * 2 + half_bit
        span_rows = owned_rows * 2 ** (bit_num + 1)
        child_rows = span_rows // 2
        subband = owner_index >> bit_num + 1
        entries = lax.dynamic_slice_in_dim(
            merge_table[level_num - 1],
            subband * span_rows + owned_rows * block_index,
            owned_rows,
            1,
        )
        kept_rows = lax.dynamic_slice_in_dim(current, half_bit * quarter, quarter, 0)
        sent_rows = lax.dynamic_slice_in_dim(current, (1 - half_bit) * quarter, quarter, 0)
        partner = from_partner(sent_rows, "sub", bit_num)
        row_base = quarter * block_index
        is_low = half_bit == 0
        lower_part = jnp.where(is_low, kept_rows, partner)
        upper_part = jnp.where(is_low, partner, kept_rows)
        lower_rows = jnp.take(lower_part, entries[0] - row_base, axis=0)
        upper_rows = jnp.take(upper_part, entries[1] - row_base, axis=0)
        moved_rows = delay_rows(upper_rows, entries[2], child_rows)
        current = (lower_rows.astype(jnp.float32) + moved_rows.astype(jnp.float32)).astype(
            jnp.bfloat16
        )
    return spectrum(current[:, :SAMPLES], channels)


def reverse_bits(value, bits):
    flipped = 0
    for bit_num in range(bits):
        flipped |= (value >> bit_num & 1) << (bits - 1 - bit_num)
    return flipped


def take_along(values, index, axis):
    along = lax.GatherDimensionNumbers(
        offset_dims=(),
        collapsed_slice_dims=(axis,),
        start_index_map=(axis,),
        operand_batching_dims=(1 - axis,),
        start_indices_batching_dims=(1 - axis,),
    )
    return lax.gather(
        values, index[:, :, None], along, (1, 1), mode=lax.GatherScatterMode.PROMISE_IN_BOUNDS
    )


def tree_kernel(
    owners, margin, samples_ref, order_ref, table_ref, keep_ref, send_ref, raw_ref, first_ref,
    pick_ref, cur_ref, picked_ref, final_ref, turned_ref, sem,
):
    window, channels = samples_ref.shape
    levels, _, dmax = table_ref.shape
    quarter = CH_DEV // 4
    pad = margin // 2
    length = pad + window
    offset = (lax.axis_index("sub") * window) % LANES
    load = pltpu.make_async_copy(samples_ref, raw_ref, sem)
    load.start()

    final_ref[...] = jnp.zeros(final_ref.shape, final_ref.dtype)
    lane = lax.broadcasted_iota(jnp.int32, (8, LANES), 1)
    place = lax.broadcasted_iota(jnp.int32, (channels, LANES), 0)
    for side in range(2):
        for tile in range(dmax // LANES):
            parts = [
                take_along(
                    jnp.broadcast_to(
                        order_ref[:, (2 * tile + part) * LANES : (2 * tile + part + 1) * LANES],
                        (8, LANES),
                    ),
                    (2 * lane + side) & (LANES - 1),
                    1,
                )
                for part in range(2)
            ]
            chosen = jnp.where(lane < LANES // 2, parts[0], parts[1])[:1]
            at = side * dmax + tile * LANES
            first_ref[:, at : at + LANES] = jnp.where(place == chosen, 1.0, 0.0).astype(
                jnp.bfloat16
            )
    place = lax.broadcasted_iota(jnp.int32, (dmax, dmax), 0)
    index = lax.broadcasted_iota(jnp.int32, (1, dmax), 1)
    for level in range(1, levels):
        child = 2 ** (level - 1)
        start = (index >> level) * (2 * child)
        for side in range(2):
            chosen = start + side * child + table_ref[level, side : side + 1, :]
            pick_ref[level - 1, :, side * dmax : (side + 1) * dmax] = jnp.where(
                place == chosen, 1.0, 0.0
            ).astype(jnp.bfloat16)
    load.wait()

    row = lax.broadcasted_iota(jnp.int32, (8, LANES), 0)
    zero = jnp.zeros((8, LANES), jnp.float32)
    begin = pad
    for level in range(levels):
        last = level == levels - 1
        if level:
            picked_ref[begin:length, :] = jnp.dot(
                cur_ref[begin:length, :], pick_ref[level - 1], preferred_element_type=jnp.float32
            )
        else:
            picked_ref[begin:length, :] = jnp.dot(
                raw_ref[...], first_ref[...], preferred_element_type=jnp.float32
            )
        reached = (pad - 2**level) // 16 * 16
        for tile in range(dmax // LANES):
            output = tile * LANES + lane
            steps = (output & (2**level - 1)) // (2 * quarter)
            least = (tile * LANES & (2**level - 1)) // (2 * quarter)
            most = ((tile * LANES + LANES - 1) & (2**level - 1)) // (2 * quarter)
            if 2**level <= LANES:
                least, most = 0, (2**level - 1) // (2 * quarter)
            bits = (most - least).bit_length()
            shift = jnp.broadcast_to(
                table_ref[level, 2:3, tile * LANES : (tile + 1) * LANES], (8, LANES)
            )
            rest = row + shift - steps * quarter
            here = rest < 8
            source = rest & 7
            flags = [((steps - least) >> bit & 1) == 1 for bit in range(bits)]
            known = {}

            def coarse(bit, at):
                if at >= length // 8:
                    return None
                if (bit, at) not in known:
                    if bit == 0:
                        known[bit, at] = (
                            picked_ref[
                                at * 8 : at * 8 + 8,
                                dmax + tile * LANES : dmax + (tile + 1) * LANES,
                            ]
                            if at * 8 >= begin
                            else None
                        )
                    else:
                        near, far = coarse(bit - 1, at), coarse(bit - 1, at + 2 ** (bit - 1))
                        if near is None and far is None:
                            known[bit, at] = None
                        else:
                            near = zero if near is None else near
                            far = zero if far is None else far
                            known[bit, at] = jnp.where(flags[bit - 1], far, near)
                return known[bit, at]

            def fine(at):
                if ("fine", at) not in known:
                    value = coarse(bits, at + least)
                    known["fine", at] = None if value is None else take_along(value, source, 0)
                return known["fine", at]

            def merged(at):
                near, far = fine(at), fine(at + 1)
                total = None
                if near is not None or far is not None:
                    total = jnp.where(
                        here, zero if near is None else near, zero if far is None else far
                    )
                if begin <= at * 8:
                    low = picked_ref[at * 8 : at * 8 + 8, tile * LANES : (tile + 1) * LANES]
                    total = low if total is None else low + total
                return zero if total is None else total

            lanes = slice(tile * LANES, (tile + 1) * LANES)
            for at in range(reached // 8, length // 8, 2):
                both = jnp.concatenate([merged(at), merged(at + 1)], axis=0).astype(jnp.bfloat16)
                if last:
                    to = pl.multiple_of(offset + at * 8 + pad, 16)
                    final_ref[pl.ds(to, 16), lanes] = both
                else:
                    cur_ref[at * 8 : at * 8 + 16, lanes] = both
        begin = max(reached, 0)

    for tile in range(dmax // LANES):
        at = slice(tile * LANES, (tile + 1) * LANES)
        for time in range(final_ref.shape[0] // LANES):
            lanes = slice(time * LANES, (time + 1) * LANES)
            turned_ref[at, lanes] = final_ref[lanes, at].T
    me = lax.axis_index("sub")
    bits = (owners - 1).bit_length()
    rows = dmax // owners
    for ref, core in ((keep_ref, me & 1), (send_ref, 1 - (me & 1))):
        for ring in range(ref.shape[0]):
            for relay in range(2):
                chip, side = (2 * ring + core, core ^ relay) if ring else (relay, core)
                block = reverse_bits(((me >> 1) ^ chip) << 1 | side, bits)
                ref[ring, relay] = turned_ref[pl.ds(pl.multiple_of(block * rows, rows), rows), :]


def pair_kernel(apart, keep_ref, got_ref, own_ref, near_ref, *message_refs):
    lower = lax.axis_index("sub") & 1 == 0
    tiles = keep_ref.shape[-1] // LANES
    for ring in range(keep_ref.shape[0]):
        for relay in range(2):
            for tile in range(apart + tiles):
                total = None
                for start, mine in ((0, lower), (apart, ~lower)):
                    if start <= tile < start + tiles:
                        lanes = slice((tile - start) * LANES, (tile - start + 1) * LANES)
                        part = jnp.where(
                            mine, keep_ref[ring, relay, :, lanes], got_ref[ring, relay, :, lanes]
                        ).astype(jnp.float32)
                        total = part if total is None else total + part
                total = total.astype(own_ref.dtype)
                lanes = slice(tile * LANES, (tile + 1) * LANES)
                if ring:
                    message_refs[ring - 1][relay, :, lanes] = total
                else:
                    (near_ref if relay else own_ref)[:, lanes] = total


def relay_kernel(*refs):
    for at, ref in enumerate(refs[1:-1]):
        refs[-1][at] = ref[1]


def spectrum_kernel(
    rings, scale, own_ref, near_ref, *refs
):
    message_refs, refs = refs[: rings - 1], refs[rings - 1 :]
    relay_ref, first_ref, cos_ref, sin_ref, third_ref, out_ref = refs[:6]
    slot_ref, flat_ref, lines_ref, sems = refs[6:]
    rows, width = own_ref.shape
    tiles = width // LANES
    pitch = slot_ref.shape[0] // rows
    used = first_ref.shape[1]
    bins = first_ref.shape[0] // 2
    halves = third_ref.shape[0] // 2
    me = lax.axis_index("sub")
    core = me & 1
    sources = [(own_ref, (), 0), (near_ref, (), 1)]
    for ring in range(1, rings):
        sources.append((message_refs[ring - 1], (0,), 2 * ring + core))
        sources.append((relay_ref, (ring - 1,), 2 * ring + 1 - core))
    for ref, at, apart in sources:
        slot = ((me >> 1) ^ apart) * tiles
        for tile in range(tiles):
            slot_ref[pl.ds(slot + tile, rows, stride=pitch), :] = ref[
                at + (slice(None), slice(tile * LANES, (tile + 1) * LANES))
            ].astype(jnp.float32)
    lane = lax.broadcasted_iota(jnp.int32, (halves // 2, LANES), 1)
    sign = jnp.where(lax.broadcasted_iota(jnp.int32, (halves, LANES), 1) < bins, 1.0, -1.0)
    stores = []
    for row in range(rows):
        series = slot_ref[row * pitch : row * pitch + used, :].astype(jnp.bfloat16)
        turned = jnp.dot(first_ref[...], series, preferred_element_type=jnp.float32)
        real, imag = turned[:bins], turned[bins:]
        twisted_re = (real * cos_ref[...] - imag * sin_ref[...]).astype(jnp.bfloat16)
        twisted_im = (-imag * cos_ref[...] - real * sin_ref[...]).astype(jnp.bfloat16)
        twisted = jnp.concatenate([twisted_re, twisted_im], axis=0)
        mixed = lax.dot_general(
            third_ref[...], twisted, (((1,), (1,)), ((), ())), preferred_element_type=jnp.float32
        )
        value = mixed[:halves] + sign * pltpu.roll(mixed[halves:], bins, axis=1)
        square = value * value
        power = (square + pltpu.roll(square, bins, axis=1)) * scale
        line = jnp.where(lane < bins, power[: halves // 2], power[halves // 2 :])
        flat_ref[
            pl.ds(row // 8 * 8 * (halves // 2) + row % 8, halves // 2, stride=8), :
        ] = line
        if row % 8 == 7:
            group = row // 8
            for tile in range(halves // 2):
                at = (group * (halves // 2) + tile) * 8
                lines_ref[group * 8 : group * 8 + 8, tile * LANES : (tile + 1) * LANES] = flat_ref[
                    at : at + 8, :
                ]
            stores.append(
                pltpu.make_async_copy(
                    lines_ref.at[pl.ds(group * 8, 8)],
                    out_ref.at[pl.ds(group * 8, 8)],
                    sems.at[group],
                )
            )
            stores[-1].start()
    for store in stores:
        store.wait()


def spectrum_tables(sources, window, margin, tiles):
    fold = SAMPLES // LANES
    k = np.arange(fold)
    n = np.arange(LANES)
    m = np.arange(64)

    def angle(product, period):
        return np.float32(2.0 * math.pi / period) * (product % period).astype(np.float32)

    one = angle(k[:, None] * k[None, :], fold)
    table_one = np.concatenate([np.cos(one), np.sin(one)], axis=0)
    first = np.zeros((2 * fold, sources * tiles), np.float32)
    for source in range(sources):
        start = (source * window) // LANES - margin // LANES
        for tile in range(tiles):
            if 0 <= start + tile < fold:
                first[:, source * tiles + tile] = table_one[:, start + tile]
    two = angle(k[:, None] * n[None, :], SAMPLES)
    m = np.concatenate([m[0::2], m[1::2]])
    three = angle(m[:, None] * n[None, :], LANES)
    third = np.concatenate([np.cos(three), np.sin(three)], axis=0)
    return (
        jnp.asarray(first, jnp.bfloat16),
        jnp.asarray(np.cos(two), jnp.float32),
        jnp.asarray(np.sin(two), jnp.float32),
        jnp.asarray(third, jnp.bfloat16),
    )


def pairs_align(window, owners):
    starts = [at * window // LANES for at in range(owners)]
    return all(starts[at + 1] - starts[at] == window // LANES for at in range(0, owners, 2))


def on_chip(values):
    return pltpu.with_memory_space_constraint(values, pltpu.VMEM)


def slice_plan(samples, channel_order, merge_table):
    owners = lax.axis_size("sub")
    window, channels = samples.shape
    levels, _, dmax = merge_table.shape
    margin = window * owners - SAMPLES
    rows = dmax // owners
    rings = owners // 4
    step = math.gcd(window, LANES)
    width = margin + -(-(window + LANES - step) // LANES) * LANES
    kept = margin // 2 + window
    apart = window // LANES
    wide = width + apart * LANES
    vmem = pl.BlockSpec(memory_space=pltpu.VMEM)
    half = pltpu.VMEM((rings, 2, rows, width), jnp.bfloat16)
    keep, send = pl.pallas_call(
        functools.partial(tree_kernel, owners, margin),
        out_shape=[half, half],
        in_specs=[pl.BlockSpec(memory_space=pl.ANY), vmem, vmem],
        out_specs=[vmem, vmem],
        scratch_shapes=[
            pltpu.VMEM((window, channels), jnp.bfloat16),
            pltpu.VMEM((channels, 2 * dmax), jnp.bfloat16),
            pltpu.VMEM((levels - 1, dmax, 2 * dmax), jnp.bfloat16),
            pltpu.VMEM((kept, dmax), jnp.bfloat16),
            pltpu.VMEM((kept, 2 * dmax), jnp.float32),
            pltpu.VMEM((width, dmax), jnp.bfloat16),
            pltpu.VMEM((dmax, width), jnp.bfloat16),
            pltpu.SemaphoreType.DMA,
        ],
        name="tree",
    )(samples, channel_order.reshape(1, channels), merge_table)
    beside = [(low, low ^ 1) for low in range(owners)]
    got = on_chip(lax.ppermute(send, "sub", beside))
    block = pltpu.VMEM((rows, wide), jnp.bfloat16)
    message = pltpu.VMEM((2, rows, wide), jnp.bfloat16)
    own, near, *messages = pl.pallas_call(
        functools.partial(pair_kernel, apart),
        out_shape=[block, block] + [message] * (rings - 1),
        in_specs=[vmem] * 2,
        out_specs=[vmem] * (rings + 1),
        name="pair",
    )(on_chip(keep), got)
    arrived = []
    for ring in range(rings):
        route = [(a, a ^ (2 * (2 * ring + a % 2) if ring else 2)) for a in range(owners)]
        message = messages[ring - 1] if ring else near
        arrived.append(on_chip(lax.ppermute(message, "sub", route)))
    near, *arrived = arrived
    relay = pl.pallas_call(
        relay_kernel,
        out_shape=pltpu.VMEM((rings - 1, rows, wide), jnp.bfloat16),
        in_specs=[vmem] * rings,
        out_specs=vmem,
        name="relay",
    )(near, *arrived)
    relay = on_chip(lax.ppermute(relay, "sub", beside))
    pairs = owners // 2
    tables = [
        on_chip(table) for table in spectrum_tables(pairs, 2 * window, margin, wide // LANES)
    ]
    pitch = pairs * wide // LANES + 1
    return pl.pallas_call(
        functools.partial(spectrum_kernel, rings, 1.0 / (SAMPLES * channels)),
        out_shape=jax.ShapeDtypeStruct((rows, SAMPLES // 2), jnp.float32),
        in_specs=[vmem] * (rings + 6),
        out_specs=pl.BlockSpec(memory_space=pl.ANY),
        scratch_shapes=[
            pltpu.VMEM((rows * pitch, LANES), jnp.float32),
            pltpu.VMEM((rows * SAMPLES // 2 // LANES, LANES), jnp.float32),
            pltpu.VMEM((rows, SAMPLES // 2), jnp.float32),
            pltpu.SemaphoreType.DMA((rows // 8,)),
        ],
        name="spectrum",
    )(on_chip(own), near, *arrived, relay, *tables)


def local(samples, channel_order, merge_table):
    owners = lax.axis_size("sub")
    window, channels = samples.shape
    dmax = merge_table.shape[2]
    margin = window * owners - SAMPLES
    fits = (
        dmax == 256
        and channels == 2 * dmax
        and dmax == 16 * owners
        and margin == dmax
        and window % 16 == 0
        and window <= 1024
        and owners % 8 == 0
        and pairs_align(window, owners)
    )
    plan = slice_plan if fits else owner_plan
    return plan(samples, channel_order, merge_table)


def solution(mesh):
    in_specs = (P(("groups", "sub"), None), P(), P())
    out_specs = P(("groups", "sub"), None)
    return jax.shard_map(local, mesh=mesh, in_specs=in_specs, out_specs=out_specs, check_vma=False)
```

```python
import functools
import math

import jax
import jax.numpy as jnp
import numpy as np
from jax import lax
from jax.experimental import pallas as pl
from jax.experimental.pallas import tpu as pltpu
from jax.sharding import PartitionSpec as P


LOCAL = 5
CH_DEV = 32
SAMPLES = 8192
LANES = 128


def from_partner(block, axis, apart):
    count = lax.axis_size(axis)
    route = []
    for low in range(count):
        high = low | 1 << apart
        if high != low and high < count:
            route += [(low, high), (high, low)]
    return lax.ppermute(block, axis, route)


def delay_rows(values, shifts, margin):
    moved = values
    for bit_num in range(max(1, margin.bit_length())):
        offset = 2**bit_num
        rolled = jnp.pad(moved[:, offset:], ((0, 0), (0, offset)))
        flagged = shifts >> bit_num & 1 == 1
        flagged = flagged[:, None]
        moved = jnp.where(flagged, rolled, moved)
    return moved


def merge_level(current, entries, child_rows, span_rows, time_axis):
    outputs = jnp.arange(entries.shape[1], dtype=jnp.int32)
    starts = 2 * child_rows * (outputs // span_rows)
    lower_rows = jnp.take(current, starts + entries[0], axis=1 - time_axis)
    upper_rows = jnp.take(current, starts + child_rows + entries[1], axis=1 - time_axis)
    moved_rows = delay_rows(upper_rows, entries[2], child_rows)
    return (lower_rows.astype(jnp.float32) + moved_rows.astype(jnp.float32)).astype(jnp.bfloat16)


def spectrum(delays, channels):
    row_count = delays.shape[0]
    length = delays.shape[1]
    fold_size = length // 128
    first_index = jnp.arange(fold_size, dtype=jnp.int32)
    lane_index = jnp.arange(128, dtype=jnp.int32)
    half_index = jnp.arange(64, dtype=jnp.int32)
    angle_one = (
        2.0
        * math.pi
        / fold_size
        * (first_index[:, None] * first_index[None, :] % fold_size).astype(jnp.float32)
    )
    cos_one = jnp.cos(angle_one).astype(jnp.bfloat16)
    sin_one = jnp.sin(angle_one).astype(jnp.bfloat16)
    angle_two = (
        2.0
        * math.pi
        / length
        * (first_index[:, None] * lane_index[None, :] % length).astype(jnp.float32)
    )
    twist_cos = jnp.cos(angle_two)
    twist_sin = jnp.sin(angle_two)
    angle_three = (
        2.0 * math.pi / 128 * (lane_index[:, None] * half_index[None, :] % 128).astype(jnp.float32)
    )
    cos_three = jnp.cos(angle_three).astype(jnp.bfloat16)
    sin_three = jnp.sin(angle_three).astype(jnp.bfloat16)
    series = delays.reshape(row_count, fold_size, 128)
    first_re = jnp.einsum("kn,rnm->rkm", cos_one, series, preferred_element_type=jnp.float32)
    first_im = -jnp.einsum("kn,rnm->rkm", sin_one, series, preferred_element_type=jnp.float32)
    twisted_re = (first_re * twist_cos + first_im * twist_sin).astype(jnp.bfloat16)
    twisted_im = (first_im * twist_cos - first_re * twist_sin).astype(jnp.bfloat16)
    out_re = jnp.einsum(
        "rkn,nj->rjk", twisted_re, cos_three, preferred_element_type=jnp.float32
    ) + jnp.einsum("rkn,nj->rjk", twisted_im, sin_three, preferred_element_type=jnp.float32)
    out_im = jnp.einsum(
        "rkn,nj->rjk", twisted_im, cos_three, preferred_element_type=jnp.float32
    ) - jnp.einsum("rkn,nj->rjk", twisted_re, sin_three, preferred_element_type=jnp.float32)
    power = (out_re * out_re + out_im * out_im) / (length * channels)
    return power.reshape(row_count, 64 * fold_size)


def owner_plan(samples, channel_order, merge_table):
    owners = lax.axis_size("sub")
    owner_index = lax.axis_index("sub")
    owned_rows = CH_DEV // 2
    quarter = CH_DEV // 4
    window = samples.shape[0]
    channels = samples.shape[1]
    ordered = jnp.take(samples, channel_order, axis=1).T.reshape(owners, CH_DEV, window)
    current = lax.all_to_all(ordered, "sub", split_axis=0, concat_axis=2, tiled=True).reshape(
        CH_DEV, window * owners
    )
    for level_num in range(1, LOCAL + 1):
        entries = lax.dynamic_slice_in_dim(
            merge_table[level_num - 1], owner_index * owned_rows, owned_rows, 1
        )
        current = merge_level(
            current, entries, max(1, 2 ** (level_num - 2)), 2 ** (level_num - 1), 1
        )
    block_index = jnp.zeros((), jnp.int32)
    for bit_num in range(owners.bit_length() - 1):
        level_num = LOCAL + bit_num + 1
        half_bit = owner_index >> bit_num & 1
        block_index = block_index * 2 + half_bit
        span_rows = owned_rows * 2 ** (bit_num + 1)
        child_rows = span_rows // 2
        subband = owner_index >> bit_num + 1
        entries = lax.dynamic_slice_in_dim(
            merge_table[level_num - 1],
            subband * span_rows + owned_rows * block_index,
            owned_rows,
            1,
        )
        kept_rows = lax.dynamic_slice_in_dim(current, half_bit * quarter, quarter, 0)
        sent_rows = lax.dynamic_slice_in_dim(current, (1 - half_bit) * quarter, quarter, 0)
        partner = from_partner(sent_rows, "sub", bit_num)
        row_base = quarter * block_index
        is_low = half_bit == 0
        lower_part = jnp.where(is_low, kept_rows, partner)
        upper_part = jnp.where(is_low, partner, kept_rows)
        lower_rows = jnp.take(lower_part, entries[0] - row_base, axis=0)
        upper_rows = jnp.take(upper_part, entries[1] - row_base, axis=0)
        moved_rows = delay_rows(upper_rows, entries[2], child_rows)
        current = (lower_rows.astype(jnp.float32) + moved_rows.astype(jnp.float32)).astype(
            jnp.bfloat16
        )
    return spectrum(current[:, :SAMPLES], channels)


def reverse_bits(value, bits):
    flipped = 0
    for bit_num in range(bits):
        flipped |= (value >> bit_num & 1) << (bits - 1 - bit_num)
    return flipped


def take_along(values, index, axis):
    along = lax.GatherDimensionNumbers(
        offset_dims=(),
        collapsed_slice_dims=(axis,),
        start_index_map=(axis,),
        operand_batching_dims=(1 - axis,),
        start_indices_batching_dims=(1 - axis,),
    )
    return lax.gather(
        values, index[:, :, None], along, (1, 1), mode=lax.GatherScatterMode.PROMISE_IN_BOUNDS
    )


def tree_kernel(
    owners, margin, samples_at, order_at, table_at, keep_ref, send_ref, raw_ref, order_ref,
    table_ref, first_ref, pick_ref, cur_ref, picked_ref, final_ref, turned_ref, sems,
):
    window, channels = raw_ref.shape
    levels, _, dmax = table_ref.shape
    quarter = CH_DEV // 4
    pad = margin // 2
    length = pad + window
    offset = (lax.axis_index("sub") * window) % LANES
    loads = [
        pltpu.make_async_copy(source, target, sems.at[at])
        for at, (source, target) in enumerate(
            ((table_at, table_ref), (order_at, order_ref), (samples_at, raw_ref))
        )
    ]
    for load in loads:
        load.start()

    final_ref[...] = jnp.zeros(final_ref.shape, final_ref.dtype)
    lane = lax.broadcasted_iota(jnp.int32, (8, LANES), 1)

    def narrow(numbers):
        return numbers.astype(jnp.float32).astype(jnp.bfloat16)

    def one_hot(place, chosen):
        return jnp.where(
            place == jnp.broadcast_to(narrow(chosen), place.shape),
            jnp.ones(place.shape, jnp.bfloat16),
            jnp.zeros(place.shape, jnp.bfloat16),
        )

    loads[0].wait()
    loads[1].wait()
    place = narrow(lax.broadcasted_iota(jnp.int32, (dmax, LANES), 0))
    for side in range(2):
        for tile in range(dmax // LANES):
            parts = [
                take_along(
                    jnp.broadcast_to(
                        order_ref[:, (2 * tile + part) * LANES : (2 * tile + part + 1) * LANES],
                        (8, LANES),
                    ),
                    (2 * lane + side) & (LANES - 1),
                    1,
                )
                for part in range(2)
            ]
            chosen = jnp.where(lane < LANES // 2, parts[0], parts[1])[:1]
            at = side * dmax + tile * LANES
            for part in range(channels // dmax):
                first_ref[part * dmax : (part + 1) * dmax, at : at + LANES] = one_hot(
                    place, chosen - part * dmax
                )
    index = lax.broadcasted_iota(jnp.int32, (1, dmax), 1)
    place = narrow(lax.broadcasted_iota(jnp.int32, (dmax // 2, LANES), 0))
    for level in range(1, levels):
        child = 2 ** (level - 1)
        start = (index >> level) * (2 * child)
        for side in range(2):
            chosen = (start + side * child + table_ref[level, side : side + 1, :]) & (
                dmax // 2 - 1
            )
            for tile in range(dmax // LANES):
                part, to = (side, tile) if level == levels - 1 else (tile, side)
                pick_ref[level - 1, part, :, to * LANES : (to + 1) * LANES] = one_hot(
                    place, chosen[:, tile * LANES : (tile + 1) * LANES]
                )
    loads[2].wait()

    row = lax.broadcasted_iota(jnp.int32, (8, LANES), 0)
    zero = jnp.zeros((8, LANES), jnp.float32)
    begin = pad
    for level in range(levels):
        last = level == levels - 1
        if level:
            for part in range(2):
                picked_ref[begin:length, part * dmax : (part + 1) * dmax] = jnp.dot(
                    cur_ref[begin:length, part * LANES : (part + 1) * LANES],
                    pick_ref[level - 1, part],
                    preferred_element_type=jnp.float32,
                )
        else:
            picked_ref[begin:length, :] = jnp.dot(
                raw_ref[...], first_ref[...], preferred_element_type=jnp.float32
            )
        reached = (pad - 2**level) // 16 * 16
        for tile in range(dmax // LANES):
            low_at = tile if last or not level else 2 * tile
            high_at = low_at + (2 if last or not level else 1)
            low_lanes = slice(low_at * LANES, (low_at + 1) * LANES)
            high_lanes = slice(high_at * LANES, (high_at + 1) * LANES)
            output = tile * LANES + lane
            steps = (output & (2**level - 1)) // (2 * quarter)
            least = (tile * LANES & (2**level - 1)) // (2 * quarter)
            most = ((tile * LANES + LANES - 1) & (2**level - 1)) // (2 * quarter)
            if 2**level <= LANES:
                least, most = 0, (2**level - 1) // (2 * quarter)
            bits = (most - least).bit_length()
            shift = jnp.broadcast_to(
                table_ref[level, 2:3, tile * LANES : (tile + 1) * LANES], (8, LANES)
            )
            rest = row + shift - steps * quarter
            here = rest < 8
            source = rest & 7
            flags = [((steps - least) >> bit & 1) == 1 for bit in range(bits)]
            known = {}

            def coarse(bit, at):
                if at >= length // 8:
                    return None
                if (bit, at) not in known:
                    if bit == 0:
                        known[bit, at] = (
                            picked_ref[at * 8 : at * 8 + 8, high_lanes]
                            if at * 8 >= begin
                            else None
                        )
                    else:
                        near, far = coarse(bit - 1, at), coarse(bit - 1, at + 2 ** (bit - 1))
                        if near is None and far is None:
                            known[bit, at] = None
                        else:
                            near = zero if near is None else near
                            far = zero if far is None else far
                            known[bit, at] = jnp.where(flags[bit - 1], far, near)
                return known[bit, at]

            def fine(at):
                if ("fine", at) not in known:
                    value = coarse(bits, at + least)
                    known["fine", at] = None if value is None else take_along(value, source, 0)
                return known["fine", at]

            def merged(at):
                near, far = fine(at), fine(at + 1)
                total = None
                if near is not None or far is not None:
                    total = jnp.where(
                        here, zero if near is None else near, zero if far is None else far
                    )
                if begin <= at * 8:
                    low = picked_ref[at * 8 : at * 8 + 8, low_lanes]
                    total = low if total is None else low + total
                return zero if total is None else total

            lanes = slice(tile * LANES, (tile + 1) * LANES)
            for at in range(reached // 8, length // 8, 2):
                both = jnp.concatenate([merged(at), merged(at + 1)], axis=0).astype(jnp.bfloat16)
                if last:
                    to = pl.multiple_of(offset + at * 8 + pad, 16)
                    final_ref[pl.ds(to, 16), lanes] = both
                else:
                    cur_ref[at * 8 : at * 8 + 16, lanes] = both
        begin = max(reached, 0)

    for tile in range(dmax // LANES):
        at = slice(tile * LANES, (tile + 1) * LANES)
        for time in range(final_ref.shape[0] // LANES):
            lanes = slice(time * LANES, (time + 1) * LANES)
            turned_ref[at, lanes] = final_ref[lanes, at].T
    me = lax.axis_index("sub")
    bits = (owners - 1).bit_length()
    rows = dmax // owners
    for ref, core in ((keep_ref, me & 1), (send_ref, 1 - (me & 1))):
        for ring in range(ref.shape[0]):
            for relay in range(2):
                chip, side = (2 * ring + core, core ^ relay) if ring else (relay, core)
                block = reverse_bits(((me >> 1) ^ chip) << 1 | side, bits)
                ref[ring, relay] = turned_ref[pl.ds(pl.multiple_of(block * rows, rows), rows), :]


def pair_kernel(apart, keep_ref, got_ref, own_ref, near_ref, *message_refs):
    lower = lax.axis_index("sub") & 1 == 0
    tiles = keep_ref.shape[-1] // LANES
    for ring in range(keep_ref.shape[0]):
        for relay in range(2):
            for tile in range(apart + tiles):
                total = None
                for start, mine in ((0, lower), (apart, ~lower)):
                    if start <= tile < start + tiles:
                        lanes = slice((tile - start) * LANES, (tile - start + 1) * LANES)
                        part = jnp.where(
                            mine, keep_ref[ring, relay, :, lanes], got_ref[ring, relay, :, lanes]
                        ).astype(jnp.float32)
                        total = part if total is None else total + part
                total = total.astype(own_ref.dtype)
                lanes = slice(tile * LANES, (tile + 1) * LANES)
                if ring:
                    message_refs[ring - 1][relay, :, lanes] = total
                else:
                    (near_ref if relay else own_ref)[:, lanes] = total


def relay_kernel(*refs):
    for at, ref in enumerate(refs[1:-1]):
        refs[-1][at] = ref[1]


def spectrum_kernel(
    rings, scale, own_ref, near_ref, *refs
):
    message_refs, refs = refs[: rings - 1], refs[rings - 1 :]
    relay_ref, first_ref, cos_ref, sin_ref, third_ref, out_ref = refs[:6]
    slot_ref, flat_ref, lines_ref, sems = refs[6:]
    rows, width = own_ref.shape
    tiles = width // LANES
    pitch = slot_ref.shape[0] // rows
    used = first_ref.shape[1]
    bins = first_ref.shape[0] // 2
    halves = third_ref.shape[0] // 2
    me = lax.axis_index("sub")
    core = me & 1
    sources = [(own_ref, (), 0), (near_ref, (), 1)]
    for ring in range(1, rings):
        sources.append((message_refs[ring - 1], (0,), 2 * ring + core))
        sources.append((relay_ref, (ring - 1,), 2 * ring + 1 - core))
    for ref, at, apart in sources:
        slot = ((me >> 1) ^ apart) * tiles
        for tile in range(tiles):
            slot_ref[pl.ds(slot + tile, rows, stride=pitch), :] = ref[
                at + (slice(None), slice(tile * LANES, (tile + 1) * LANES))
            ].astype(jnp.float32)
    lane = lax.broadcasted_iota(jnp.int32, (halves // 2, LANES), 1)
    sign = jnp.where(lax.broadcasted_iota(jnp.int32, (halves, LANES), 1) < bins, 1.0, -1.0)
    stores = []
    for row in range(rows):
        series = slot_ref[row * pitch : row * pitch + used, :].astype(jnp.bfloat16)
        turned = jnp.dot(first_ref[...], series, preferred_element_type=jnp.float32)
        real, imag = turned[:bins], turned[bins:]
        twisted_re = (real * cos_ref[...] - imag * sin_ref[...]).astype(jnp.bfloat16)
        twisted_im = (-imag * cos_ref[...] - real * sin_ref[...]).astype(jnp.bfloat16)
        twisted = jnp.concatenate([twisted_re, twisted_im], axis=0)
        mixed = lax.dot_general(
            third_ref[...], twisted, (((1,), (1,)), ((), ())), preferred_element_type=jnp.float32
        )
        value = mixed[:halves] + sign * pltpu.roll(mixed[halves:], bins, axis=1)
        square = value * value
        power = (square + pltpu.roll(square, bins, axis=1)) * scale
        line = jnp.where(lane < bins, power[: halves // 2], power[halves // 2 :])
        flat_ref[
            pl.ds(row // 8 * 8 * (halves // 2) + row % 8, halves // 2, stride=8), :
        ] = line
        if row % 8 == 7:
            group = row // 8
            for tile in range(halves // 2):
                at = (group * (halves // 2) + tile) * 8
                lines_ref[group * 8 : group * 8 + 8, tile * LANES : (tile + 1) * LANES] = flat_ref[
                    at : at + 8, :
                ]
            stores.append(
                pltpu.make_async_copy(
                    lines_ref.at[pl.ds(group * 8, 8)],
                    out_ref.at[pl.ds(group * 8, 8)],
                    sems.at[group],
                )
            )
            stores[-1].start()
    for store in stores:
        store.wait()


def spectrum_tables(sources, window, margin, tiles):
    fold = SAMPLES // LANES
    k = np.arange(fold)
    n = np.arange(LANES)
    m = np.arange(64)

    def angle(product, period):
        return np.float32(2.0 * math.pi / period) * (product % period).astype(np.float32)

    one = angle(k[:, None] * k[None, :], fold)
    table_one = np.concatenate([np.cos(one), np.sin(one)], axis=0)
    first = np.zeros((2 * fold, sources * tiles), np.float32)
    for source in range(sources):
        start = (source * window) // LANES - margin // LANES
        for tile in range(tiles):
            if 0 <= start + tile < fold:
                first[:, source * tiles + tile] = table_one[:, start + tile]
    two = angle(k[:, None] * n[None, :], SAMPLES)
    m = np.concatenate([m[0::2], m[1::2]])
    three = angle(m[:, None] * n[None, :], LANES)
    third = np.concatenate([np.cos(three), np.sin(three)], axis=0)
    return (
        jnp.asarray(first, jnp.bfloat16),
        jnp.asarray(np.cos(two), jnp.float32),
        jnp.asarray(np.sin(two), jnp.float32),
        jnp.asarray(third, jnp.bfloat16),
    )


def pairs_align(window, owners):
    starts = [at * window // LANES for at in range(owners)]
    return all(starts[at + 1] - starts[at] == window // LANES for at in range(0, owners, 2))


def on_chip(values):
    return pltpu.with_memory_space_constraint(values, pltpu.VMEM)


def slice_plan(samples, channel_order, merge_table):
    owners = lax.axis_size("sub")
    window, channels = samples.shape
    levels, _, dmax = merge_table.shape
    margin = window * owners - SAMPLES
    rows = dmax // owners
    rings = owners // 4
    step = math.gcd(window, LANES)
    width = margin + -(-(window + LANES - step) // LANES) * LANES
    kept = margin // 2 + window
    apart = window // LANES
    wide = width + apart * LANES
    vmem = pl.BlockSpec(memory_space=pltpu.VMEM)
    half = pltpu.VMEM((rings, 2, rows, width), jnp.bfloat16)
    keep, send = pl.pallas_call(
        functools.partial(tree_kernel, owners, margin),
        out_shape=[half, half],
        in_specs=[pl.BlockSpec(memory_space=pl.ANY)] * 3,
        out_specs=[vmem, vmem],
        scratch_shapes=[
            pltpu.VMEM((window, channels), jnp.bfloat16),
            pltpu.VMEM((1, channels), jnp.int32),
            pltpu.VMEM((levels, 3, dmax), jnp.int32),
            pltpu.VMEM((channels, 2 * dmax), jnp.bfloat16),
            pltpu.VMEM((levels - 1, 2, dmax // 2, dmax), jnp.bfloat16),
            pltpu.VMEM((kept, dmax), jnp.bfloat16),
            pltpu.VMEM((kept, 2 * dmax), jnp.float32),
            pltpu.VMEM((width, dmax), jnp.bfloat16),
            pltpu.VMEM((dmax, width), jnp.bfloat16),
            pltpu.SemaphoreType.DMA((3,)),
        ],
        name="tree",
    )(samples, channel_order.reshape(1, channels), merge_table)
    beside = [(low, low ^ 1) for low in range(owners)]
    got = on_chip(lax.ppermute(send, "sub", beside))
    block = pltpu.VMEM((rows, wide), jnp.bfloat16)
    message = pltpu.VMEM((2, rows, wide), jnp.bfloat16)
    own, near, *messages = pl.pallas_call(
        functools.partial(pair_kernel, apart),
        out_shape=[block, block] + [message] * (rings - 1),
        in_specs=[vmem] * 2,
        out_specs=[vmem] * (rings + 1),
        name="pair",
    )(on_chip(keep), got)
    arrived = []
    for ring in range(rings):
        route = [(a, a ^ (2 * (2 * ring + a % 2) if ring else 2)) for a in range(owners)]
        message = messages[ring - 1] if ring else near
        arrived.append(on_chip(lax.ppermute(message, "sub", route)))
    near, *arrived = arrived
    relay = pl.pallas_call(
        relay_kernel,
        out_shape=pltpu.VMEM((rings - 1, rows, wide), jnp.bfloat16),
        in_specs=[vmem] * rings,
        out_specs=vmem,
        name="relay",
    )(near, *arrived)
    relay = on_chip(lax.ppermute(relay, "sub", beside))
    pairs = owners // 2
    tables = [
        on_chip(table) for table in spectrum_tables(pairs, 2 * window, margin, wide // LANES)
    ]
    pitch = pairs * wide // LANES + 1
    return pl.pallas_call(
        functools.partial(spectrum_kernel, rings, 1.0 / (SAMPLES * channels)),
        out_shape=jax.ShapeDtypeStruct((rows, SAMPLES // 2), jnp.float32),
        in_specs=[vmem] * (rings + 6),
        out_specs=pl.BlockSpec(memory_space=pl.ANY),
        scratch_shapes=[
            pltpu.VMEM((rows * pitch, LANES), jnp.float32),
            pltpu.VMEM((rows * SAMPLES // 2 // LANES, LANES), jnp.float32),
            pltpu.VMEM((rows, SAMPLES // 2), jnp.float32),
            pltpu.SemaphoreType.DMA((rows // 8,)),
        ],
        name="spectrum",
    )(on_chip(own), near, *arrived, relay, *tables)


def local(samples, channel_order, merge_table):
    owners = lax.axis_size("sub")
    window, channels = samples.shape
    dmax = merge_table.shape[2]
    margin = window * owners - SAMPLES
    fits = (
        dmax == 256
        and channels == 2 * dmax
        and dmax == 16 * owners
        and margin == dmax
        and window % 16 == 0
        and window <= 1024
        and owners % 8 == 0
        and pairs_align(window, owners)
    )
    plan = slice_plan if fits else owner_plan
    return plan(samples, channel_order, merge_table)


def solution(mesh):
    in_specs = (P(("groups", "sub"), None), P(), P())
    out_specs = P(("groups", "sub"), None)
    return jax.shard_map(local, mesh=mesh, in_specs=in_specs, out_specs=out_specs, check_vma=False)
```

```python
import functools
import math

import jax
import jax.numpy as jnp
import numpy as np
from jax import lax
from jax.experimental import pallas as pl
from jax.experimental.pallas import tpu as pltpu
from jax.sharding import PartitionSpec as P


LOCAL = 5
CH_DEV = 32
SAMPLES = 8192
LANES = 128


def from_partner(block, axis, apart):
    count = lax.axis_size(axis)
    route = []
    for low in range(count):
        high = low | 1 << apart
        if high != low and high < count:
            route += [(low, high), (high, low)]
    return lax.ppermute(block, axis, route)


def delay_rows(values, shifts, margin):
    moved = values
    for bit_num in range(max(1, margin.bit_length())):
        offset = 2**bit_num
        rolled = jnp.pad(moved[:, offset:], ((0, 0), (0, offset)))
        flagged = shifts >> bit_num & 1 == 1
        flagged = flagged[:, None]
        moved = jnp.where(flagged, rolled, moved)
    return moved


def merge_level(current, entries, child_rows, span_rows, time_axis):
    outputs = jnp.arange(entries.shape[1], dtype=jnp.int32)
    starts = 2 * child_rows * (outputs // span_rows)
    lower_rows = jnp.take(current, starts + entries[0], axis=1 - time_axis)
    upper_rows = jnp.take(current, starts + child_rows + entries[1], axis=1 - time_axis)
    moved_rows = delay_rows(upper_rows, entries[2], child_rows)
    return (lower_rows.astype(jnp.float32) + moved_rows.astype(jnp.float32)).astype(jnp.bfloat16)


def spectrum(delays, channels):
    row_count = delays.shape[0]
    length = delays.shape[1]
    fold_size = length // 128
    first_index = jnp.arange(fold_size, dtype=jnp.int32)
    lane_index = jnp.arange(128, dtype=jnp.int32)
    half_index = jnp.arange(64, dtype=jnp.int32)
    angle_one = (
        2.0
        * math.pi
        / fold_size
        * (first_index[:, None] * first_index[None, :] % fold_size).astype(jnp.float32)
    )
    cos_one = jnp.cos(angle_one).astype(jnp.bfloat16)
    sin_one = jnp.sin(angle_one).astype(jnp.bfloat16)
    angle_two = (
        2.0
        * math.pi
        / length
        * (first_index[:, None] * lane_index[None, :] % length).astype(jnp.float32)
    )
    twist_cos = jnp.cos(angle_two)
    twist_sin = jnp.sin(angle_two)
    angle_three = (
        2.0 * math.pi / 128 * (lane_index[:, None] * half_index[None, :] % 128).astype(jnp.float32)
    )
    cos_three = jnp.cos(angle_three).astype(jnp.bfloat16)
    sin_three = jnp.sin(angle_three).astype(jnp.bfloat16)
    series = delays.reshape(row_count, fold_size, 128)
    first_re = jnp.einsum("kn,rnm->rkm", cos_one, series, preferred_element_type=jnp.float32)
    first_im = -jnp.einsum("kn,rnm->rkm", sin_one, series, preferred_element_type=jnp.float32)
    twisted_re = (first_re * twist_cos + first_im * twist_sin).astype(jnp.bfloat16)
    twisted_im = (first_im * twist_cos - first_re * twist_sin).astype(jnp.bfloat16)
    out_re = jnp.einsum(
        "rkn,nj->rjk", twisted_re, cos_three, preferred_element_type=jnp.float32
    ) + jnp.einsum("rkn,nj->rjk", twisted_im, sin_three, preferred_element_type=jnp.float32)
    out_im = jnp.einsum(
        "rkn,nj->rjk", twisted_im, cos_three, preferred_element_type=jnp.float32
    ) - jnp.einsum("rkn,nj->rjk", twisted_re, sin_three, preferred_element_type=jnp.float32)
    power = (out_re * out_re + out_im * out_im) / (length * channels)
    return power.reshape(row_count, 64 * fold_size)


def owner_plan(samples, channel_order, merge_table):
    owners = lax.axis_size("sub")
    owner_index = lax.axis_index("sub")
    owned_rows = CH_DEV // 2
    quarter = CH_DEV // 4
    window = samples.shape[0]
    channels = samples.shape[1]
    ordered = jnp.take(samples, channel_order, axis=1).T.reshape(owners, CH_DEV, window)
    current = lax.all_to_all(ordered, "sub", split_axis=0, concat_axis=2, tiled=True).reshape(
        CH_DEV, window * owners
    )
    for level_num in range(1, LOCAL + 1):
        entries = lax.dynamic_slice_in_dim(
            merge_table[level_num - 1], owner_index * owned_rows, owned_rows, 1
        )
        current = merge_level(
            current, entries, max(1, 2 ** (level_num - 2)), 2 ** (level_num - 1), 1
        )
    block_index = jnp.zeros((), jnp.int32)
    for bit_num in range(owners.bit_length() - 1):
        level_num = LOCAL + bit_num + 1
        half_bit = owner_index >> bit_num & 1
        block_index = block_index * 2 + half_bit
        span_rows = owned_rows * 2 ** (bit_num + 1)
        child_rows = span_rows // 2
        subband = owner_index >> bit_num + 1
        entries = lax.dynamic_slice_in_dim(
            merge_table[level_num - 1],
            subband * span_rows + owned_rows * block_index,
            owned_rows,
            1,
        )
        kept_rows = lax.dynamic_slice_in_dim(current, half_bit * quarter, quarter, 0)
        sent_rows = lax.dynamic_slice_in_dim(current, (1 - half_bit) * quarter, quarter, 0)
        partner = from_partner(sent_rows, "sub", bit_num)
        row_base = quarter * block_index
        is_low = half_bit == 0
        lower_part = jnp.where(is_low, kept_rows, partner)
        upper_part = jnp.where(is_low, partner, kept_rows)
        lower_rows = jnp.take(lower_part, entries[0] - row_base, axis=0)
        upper_rows = jnp.take(upper_part, entries[1] - row_base, axis=0)
        moved_rows = delay_rows(upper_rows, entries[2], child_rows)
        current = (lower_rows.astype(jnp.float32) + moved_rows.astype(jnp.float32)).astype(
            jnp.bfloat16
        )
    return spectrum(current[:, :SAMPLES], channels)


def reverse_bits(value, bits):
    flipped = 0
    for bit_num in range(bits):
        flipped |= (value >> bit_num & 1) << (bits - 1 - bit_num)
    return flipped


def take_along(values, index, axis):
    along = lax.GatherDimensionNumbers(
        offset_dims=(),
        collapsed_slice_dims=(axis,),
        start_index_map=(axis,),
        operand_batching_dims=(1 - axis,),
        start_indices_batching_dims=(1 - axis,),
    )
    return lax.gather(
        values, index[:, :, None], along, (1, 1), mode=lax.GatherScatterMode.PROMISE_IN_BOUNDS
    )


def tree_kernel(
    owners, margin, samples_at, order_at, table_at, keep_ref, send_ref, raw_ref, order_ref,
    table_ref, first_ref, pick_ref, cur_ref, picked_ref, final_ref, turned_ref, sems,
):
    window, channels = raw_ref.shape
    levels, _, dmax = table_ref.shape
    quarter = CH_DEV // 4
    pad = margin // 2
    length = pad + window
    offset = (lax.axis_index("sub") * window) % LANES
    loads = [
        pltpu.make_async_copy(source, target, sems.at[at])
        for at, (source, target) in enumerate(
            ((table_at, table_ref), (order_at, order_ref), (samples_at, raw_ref))
        )
    ]
    for load in loads:
        load.start()

    final_ref[...] = jnp.zeros(final_ref.shape, final_ref.dtype)
    lane = lax.broadcasted_iota(jnp.int32, (8, LANES), 1)

    def narrow(numbers):
        return numbers.astype(jnp.float32).astype(jnp.bfloat16)

    def one_hot(place, chosen):
        return jnp.where(
            place == jnp.broadcast_to(narrow(chosen), place.shape),
            jnp.ones(place.shape, jnp.bfloat16),
            jnp.zeros(place.shape, jnp.bfloat16),
        )

    loads[0].wait()
    loads[1].wait()
    place = narrow(lax.broadcasted_iota(jnp.int32, (dmax, LANES), 0))
    for side in range(2):
        for tile in range(dmax // LANES):
            parts = [
                take_along(
                    jnp.broadcast_to(
                        order_ref[:, (2 * tile + part) * LANES : (2 * tile + part + 1) * LANES],
                        (8, LANES),
                    ),
                    (2 * lane + side) & (LANES - 1),
                    1,
                )
                for part in range(2)
            ]
            chosen = jnp.where(lane < LANES // 2, parts[0], parts[1])[:1]
            at = side * dmax + tile * LANES
            for part in range(channels // dmax):
                first_ref[part * dmax : (part + 1) * dmax, at : at + LANES] = one_hot(
                    place, chosen - part * dmax
                )
    index = lax.broadcasted_iota(jnp.int32, (1, dmax), 1)
    place = narrow(lax.broadcasted_iota(jnp.int32, (dmax // 2, LANES), 0))
    for level in range(1, levels):
        child = 2 ** (level - 1)
        start = (index >> level) * (2 * child)
        for side in range(2):
            chosen = (start + side * child + table_ref[level, side : side + 1, :]) & (
                dmax // 2 - 1
            )
            for tile in range(dmax // LANES):
                part, to = (side, tile) if level == levels - 1 else (tile, side)
                pick_ref[level - 1, part, :, to * LANES : (to + 1) * LANES] = one_hot(
                    place, chosen[:, tile * LANES : (tile + 1) * LANES]
                )
    loads[2].wait()

    row = lax.broadcasted_iota(jnp.int32, (8, LANES), 0)
    zero = jnp.zeros((8, LANES), jnp.float32)
    begin = pad
    for level in range(levels):
        last = level == levels - 1
        if level:
            for part in range(2):
                picked_ref[begin:length, part * dmax : (part + 1) * dmax] = jnp.dot(
                    cur_ref[begin:length, part * LANES : (part + 1) * LANES],
                    pick_ref[level - 1, part],
                    preferred_element_type=jnp.float32,
                )
        else:
            picked_ref[begin:length, :] = jnp.dot(
                raw_ref[...], first_ref[...], preferred_element_type=jnp.float32
            )
        reached = (pad - 2**level) // 16 * 16
        for tile in range(dmax // LANES):
            low_at = tile if last or not level else 2 * tile
            high_at = low_at + (2 if last or not level else 1)
            low_lanes = slice(low_at * LANES, (low_at + 1) * LANES)
            high_lanes = slice(high_at * LANES, (high_at + 1) * LANES)
            output = tile * LANES + lane
            steps = (output & (2**level - 1)) // (2 * quarter)
            least = (tile * LANES & (2**level - 1)) // (2 * quarter)
            most = ((tile * LANES + LANES - 1) & (2**level - 1)) // (2 * quarter)
            if 2**level <= LANES:
                least, most = 0, (2**level - 1) // (2 * quarter)
            bits = (most - least).bit_length()
            shift = jnp.broadcast_to(
                table_ref[level, 2:3, tile * LANES : (tile + 1) * LANES], (8, LANES)
            )
            rest = row + shift - steps * quarter
            here = rest < 8
            source = rest & 7
            flags = [((steps - least) >> bit & 1) == 1 for bit in range(bits)]
            known = {}

            def coarse(bit, at):
                if at >= length // 8:
                    return None
                if (bit, at) not in known:
                    if bit == 0:
                        known[bit, at] = (
                            picked_ref[at * 8 : at * 8 + 8, high_lanes]
                            if at * 8 >= begin
                            else None
                        )
                    else:
                        near, far = coarse(bit - 1, at), coarse(bit - 1, at + 2 ** (bit - 1))
                        if near is None and far is None:
                            known[bit, at] = None
                        else:
                            near = zero if near is None else near
                            far = zero if far is None else far
                            known[bit, at] = jnp.where(flags[bit - 1], far, near)
                return known[bit, at]

            def fine(at):
                if ("fine", at) not in known:
                    value = coarse(bits, at + least)
                    known["fine", at] = None if value is None else take_along(value, source, 0)
                return known["fine", at]

            def merged(at):
                near, far = fine(at), fine(at + 1)
                total = None
                if near is not None or far is not None:
                    total = jnp.where(
                        here, zero if near is None else near, zero if far is None else far
                    )
                if begin <= at * 8:
                    low = picked_ref[at * 8 : at * 8 + 8, low_lanes]
                    total = low if total is None else low + total
                return zero if total is None else total

            lanes = slice(tile * LANES, (tile + 1) * LANES)
            for at in range(reached // 8, length // 8, 2):
                both = jnp.concatenate([merged(at), merged(at + 1)], axis=0).astype(jnp.bfloat16)
                if last:
                    to = pl.multiple_of(offset + at * 8 + pad, 16)
                    final_ref[pl.ds(to, 16), lanes] = both
                else:
                    cur_ref[at * 8 : at * 8 + 16, lanes] = both
        begin = max(reached, 0)

    for tile in range(dmax // LANES):
        at = slice(tile * LANES, (tile + 1) * LANES)
        for time in range(final_ref.shape[0] // LANES):
            lanes = slice(time * LANES, (time + 1) * LANES)
            turned_ref[at, lanes] = final_ref[lanes, at].T
    me = lax.axis_index("sub")
    bits = (owners - 1).bit_length()
    rows = dmax // owners
    for ref, core in ((keep_ref, me & 1), (send_ref, 1 - (me & 1))):
        for ring in range(ref.shape[0]):
            for relay in range(2):
                chip, side = (2 * ring + core, core ^ relay) if ring else (relay, core)
                block = reverse_bits(((me >> 1) ^ chip) << 1 | side, bits)
                ref[ring, relay] = turned_ref[pl.ds(pl.multiple_of(block * rows, rows), rows), :]


def pair_kernel(apart, keep_ref, got_ref, own_ref, near_ref, *message_refs):
    lower = lax.axis_index("sub") & 1 == 0
    tiles = keep_ref.shape[-1] // LANES
    for ring in range(keep_ref.shape[0]):
        for relay in range(2):
            for tile in range(apart + tiles):
                total = None
                for start, mine in ((0, lower), (apart, ~lower)):
                    if start <= tile < start + tiles:
                        lanes = slice((tile - start) * LANES, (tile - start + 1) * LANES)
                        part = jnp.where(
                            mine, keep_ref[ring, relay, :, lanes], got_ref[ring, relay, :, lanes]
                        ).astype(jnp.float32)
                        total = part if total is None else total + part
                total = total.astype(own_ref.dtype)
                lanes = slice(tile * LANES, (tile + 1) * LANES)
                if ring:
                    message_refs[ring - 1][relay, :, lanes] = total
                else:
                    (near_ref if relay else own_ref)[:, lanes] = total


def relay_kernel(*refs):
    for at, ref in enumerate(refs[1:-1]):
        refs[-1][at] = ref[1]


def spectrum_kernel(
    rings, scale, own_ref, near_ref, *refs
):
    message_refs, refs = refs[: rings - 1], refs[rings - 1 :]
    relay_ref, first_ref, cos_ref, sin_ref, third_ref, out_ref = refs[:6]
    slot_ref, flat_ref, lines_ref, sems = refs[6:]
    rows, width = own_ref.shape
    tiles = width // LANES
    pitch = slot_ref.shape[0] // rows
    used = first_ref.shape[1]
    bins = first_ref.shape[0] // 2
    halves = third_ref.shape[0] // 2
    me = lax.axis_index("sub")
    core = me & 1
    sources = [(own_ref, (), 0), (near_ref, (), 1)]
    for ring in range(1, rings):
        sources.append((message_refs[ring - 1], (0,), 2 * ring + core))
        sources.append((relay_ref, (ring - 1,), 2 * ring + 1 - core))
    for ref, at, apart in sources:
        slot = ((me >> 1) ^ apart) * tiles
        for tile in range(tiles):
            slot_ref[pl.ds(slot + tile, rows, stride=pitch), :] = ref[
                at + (slice(None), slice(tile * LANES, (tile + 1) * LANES))
            ].astype(jnp.float32)
    lines = halves // 2
    lane = lax.broadcasted_iota(jnp.int32, (lines, LANES), 1)
    group = 4
    stores = []

    def first_stage(start):
        series = jnp.concatenate(
            [
                slot_ref[row * pitch : row * pitch + used, :].astype(jnp.bfloat16)
                for row in range(start, start + group)
            ],
            axis=1,
        )
        return jnp.dot(first_ref[...], series, preferred_element_type=jnp.float32)

    def twist(turned):
        twisted = []
        for at in range(group):
            real = turned[:bins, at * LANES : (at + 1) * LANES]
            imag = turned[bins:, at * LANES : (at + 1) * LANES]
            twisted.append(
                jnp.concatenate(
                    [
                        (real * cos_ref[...] - imag * sin_ref[...]).astype(jnp.bfloat16),
                        (-imag * cos_ref[...] - real * sin_ref[...]).astype(jnp.bfloat16),
                    ],
                    axis=1,
                )
            )
        return jnp.concatenate(twisted, axis=0)

    def last_stage(start, twisted):
        mixed = lax.dot_general(
            third_ref[...], twisted, (((1,), (1,)), ((), ())), preferred_element_type=jnp.float32
        )
        real, imag = mixed[:halves], mixed[halves:]
        power = (real * real + imag * imag) * scale
        for at in range(0, group, 2):
            both = power[:, at * bins : at * bins + LANES]
            even, odd = both[:lines], both[lines:]
            left = jnp.where(lane < bins, even, pltpu.roll(odd, bins, axis=1))
            right = jnp.where(lane < bins, pltpu.roll(even, bins, axis=1), odd)
            for row, line in ((start + at, left), (start + at + 1, right)):
                flat_ref[pl.ds(row // 8 * 8 * lines + row % 8, lines, stride=8), :] = line
        row = start + group - 1
        if row % 8 == 7:
            part = row // 8
            for tile in range(lines):
                at = (part * lines + tile) * 8
                lines_ref[part * 8 : part * 8 + 8, tile * LANES : (tile + 1) * LANES] = flat_ref[
                    at : at + 8, :
                ]
            stores.append(
                pltpu.make_async_copy(
                    lines_ref.at[pl.ds(part * 8, 8)],
                    out_ref.at[pl.ds(part * 8, 8)],
                    sems.at[part],
                )
            )
            stores[-1].start()

    turned = first_stage(0)
    for start in range(0, rows, group):
        twisted = twist(turned)
        if start + group < rows:
            turned = first_stage(start + group)
        last_stage(start, twisted)
    for store in stores:
        store.wait()


def spectrum_tables(sources, window, margin, tiles):
    fold = SAMPLES // LANES
    k = np.arange(fold)
    n = np.arange(LANES)
    m = np.arange(64)

    def angle(product, period):
        return np.float32(2.0 * math.pi / period) * (product % period).astype(np.float32)

    one = angle(k[:, None] * k[None, :], fold)
    table_one = np.concatenate([np.cos(one), np.sin(one)], axis=0)
    first = np.zeros((2 * fold, sources * tiles), np.float32)
    for source in range(sources):
        start = (source * window) // LANES - margin // LANES
        for tile in range(tiles):
            if 0 <= start + tile < fold:
                first[:, source * tiles + tile] = table_one[:, start + tile]
    two = angle(k[:, None] * n[None, :], SAMPLES)
    m = np.concatenate([m[0::2], m[1::2]])
    three = angle(m[:, None] * n[None, :], LANES)
    cos_three, sin_three = np.cos(three), np.sin(three)
    third = np.block([[cos_three, sin_three], [-sin_three, cos_three]])
    return (
        jnp.asarray(first, jnp.bfloat16),
        jnp.asarray(np.cos(two), jnp.float32),
        jnp.asarray(np.sin(two), jnp.float32),
        jnp.asarray(third, jnp.bfloat16),
    )


def pairs_align(window, owners):
    starts = [at * window // LANES for at in range(owners)]
    return all(starts[at + 1] - starts[at] == window // LANES for at in range(0, owners, 2))


def on_chip(values):
    return pltpu.with_memory_space_constraint(values, pltpu.VMEM)


def slice_plan(samples, channel_order, merge_table):
    owners = lax.axis_size("sub")
    window, channels = samples.shape
    levels, _, dmax = merge_table.shape
    margin = window * owners - SAMPLES
    rows = dmax // owners
    rings = owners // 4
    step = math.gcd(window, LANES)
    width = margin + -(-(window + LANES - step) // LANES) * LANES
    kept = margin // 2 + window
    apart = window // LANES
    wide = width + apart * LANES
    vmem = pl.BlockSpec(memory_space=pltpu.VMEM)
    half = pltpu.VMEM((rings, 2, rows, width), jnp.bfloat16)
    keep, send = pl.pallas_call(
        functools.partial(tree_kernel, owners, margin),
        out_shape=[half, half],
        in_specs=[pl.BlockSpec(memory_space=pl.ANY)] * 3,
        out_specs=[vmem, vmem],
        scratch_shapes=[
            pltpu.VMEM((window, channels), jnp.bfloat16),
            pltpu.VMEM((1, channels), jnp.int32),
            pltpu.VMEM((levels, 3, dmax), jnp.int32),
            pltpu.VMEM((channels, 2 * dmax), jnp.bfloat16),
            pltpu.VMEM((levels - 1, 2, dmax // 2, dmax), jnp.bfloat16),
            pltpu.VMEM((kept, dmax), jnp.bfloat16),
            pltpu.VMEM((kept, 2 * dmax), jnp.float32),
            pltpu.VMEM((width, dmax), jnp.bfloat16),
            pltpu.VMEM((dmax, width), jnp.bfloat16),
            pltpu.SemaphoreType.DMA((3,)),
        ],
        name="tree",
    )(samples, channel_order.reshape(1, channels), merge_table)
    beside = [(low, low ^ 1) for low in range(owners)]
    got = on_chip(lax.ppermute(send, "sub", beside))
    block = pltpu.VMEM((rows, wide), jnp.bfloat16)
    message = pltpu.VMEM((2, rows, wide), jnp.bfloat16)
    own, near, *messages = pl.pallas_call(
        functools.partial(pair_kernel, apart),
        out_shape=[block, block] + [message] * (rings - 1),
        in_specs=[vmem] * 2,
        out_specs=[vmem] * (rings + 1),
        name="pair",
    )(on_chip(keep), got)
    arrived = []
    for ring in range(rings):
        route = [(a, a ^ (2 * (2 * ring + a % 2) if ring else 2)) for a in range(owners)]
        message = messages[ring - 1] if ring else near
        arrived.append(on_chip(lax.ppermute(message, "sub", route)))
    near, *arrived = arrived
    relay = pl.pallas_call(
        relay_kernel,
        out_shape=pltpu.VMEM((rings - 1, rows, wide), jnp.bfloat16),
        in_specs=[vmem] * rings,
        out_specs=vmem,
        name="relay",
    )(near, *arrived)
    relay = on_chip(lax.ppermute(relay, "sub", beside))
    pairs = owners // 2
    tables = [
        on_chip(table) for table in spectrum_tables(pairs, 2 * window, margin, wide // LANES)
    ]
    pitch = pairs * wide // LANES + 1
    return pl.pallas_call(
        functools.partial(spectrum_kernel, rings, 1.0 / (SAMPLES * channels)),
        out_shape=jax.ShapeDtypeStruct((rows, SAMPLES // 2), jnp.float32),
        in_specs=[vmem] * (rings + 6),
        out_specs=pl.BlockSpec(memory_space=pl.ANY),
        scratch_shapes=[
            pltpu.VMEM((rows * pitch, LANES), jnp.float32),
            pltpu.VMEM((rows * SAMPLES // 2 // LANES, LANES), jnp.float32),
            pltpu.VMEM((rows, SAMPLES // 2), jnp.float32),
            pltpu.SemaphoreType.DMA((rows // 8,)),
        ],
        name="spectrum",
    )(on_chip(own), near, *arrived, relay, *tables)


def local(samples, channel_order, merge_table):
    owners = lax.axis_size("sub")
    window, channels = samples.shape
    dmax = merge_table.shape[2]
    margin = window * owners - SAMPLES
    fits = (
        dmax == 256
        and channels == 2 * dmax
        and dmax == 16 * owners
        and margin == dmax
        and window % 16 == 0
        and window <= 1024
        and owners % 8 == 0
        and pairs_align(window, owners)
    )
    plan = slice_plan if fits else owner_plan
    return plan(samples, channel_order, merge_table)


def solution(mesh):
    in_specs = (P(("groups", "sub"), None), P(), P())
    out_specs = P(("groups", "sub"), None)
    return jax.shard_map(local, mesh=mesh, in_specs=in_specs, out_specs=out_specs, check_vma=False)
```

```python
import functools
import math

import jax
import jax.numpy as jnp
import numpy as np
from jax import lax
from jax.experimental import pallas as pl
from jax.experimental.pallas import tpu as pltpu
from jax.sharding import PartitionSpec as P


LOCAL = 5
CH_DEV = 32
SAMPLES = 8192
LANES = 128


def from_partner(block, axis, apart):
    count = lax.axis_size(axis)
    route = []
    for low in range(count):
        high = low | 1 << apart
        if high != low and high < count:
            route += [(low, high), (high, low)]
    return lax.ppermute(block, axis, route)


def delay_rows(values, shifts, margin):
    moved = values
    for bit_num in range(max(1, margin.bit_length())):
        offset = 2**bit_num
        rolled = jnp.pad(moved[:, offset:], ((0, 0), (0, offset)))
        flagged = shifts >> bit_num & 1 == 1
        flagged = flagged[:, None]
        moved = jnp.where(flagged, rolled, moved)
    return moved


def merge_level(current, entries, child_rows, span_rows, time_axis):
    outputs = jnp.arange(entries.shape[1], dtype=jnp.int32)
    starts = 2 * child_rows * (outputs // span_rows)
    lower_rows = jnp.take(current, starts + entries[0], axis=1 - time_axis)
    upper_rows = jnp.take(current, starts + child_rows + entries[1], axis=1 - time_axis)
    moved_rows = delay_rows(upper_rows, entries[2], child_rows)
    return (lower_rows.astype(jnp.float32) + moved_rows.astype(jnp.float32)).astype(jnp.bfloat16)


def spectrum(delays, channels):
    row_count = delays.shape[0]
    length = delays.shape[1]
    fold_size = length // 128
    first_index = jnp.arange(fold_size, dtype=jnp.int32)
    lane_index = jnp.arange(128, dtype=jnp.int32)
    half_index = jnp.arange(64, dtype=jnp.int32)
    angle_one = (
        2.0
        * math.pi
        / fold_size
        * (first_index[:, None] * first_index[None, :] % fold_size).astype(jnp.float32)
    )
    cos_one = jnp.cos(angle_one).astype(jnp.bfloat16)
    sin_one = jnp.sin(angle_one).astype(jnp.bfloat16)
    angle_two = (
        2.0
        * math.pi
        / length
        * (first_index[:, None] * lane_index[None, :] % length).astype(jnp.float32)
    )
    twist_cos = jnp.cos(angle_two)
    twist_sin = jnp.sin(angle_two)
    angle_three = (
        2.0 * math.pi / 128 * (lane_index[:, None] * half_index[None, :] % 128).astype(jnp.float32)
    )
    cos_three = jnp.cos(angle_three).astype(jnp.bfloat16)
    sin_three = jnp.sin(angle_three).astype(jnp.bfloat16)
    series = delays.reshape(row_count, fold_size, 128)
    first_re = jnp.einsum("kn,rnm->rkm", cos_one, series, preferred_element_type=jnp.float32)
    first_im = -jnp.einsum("kn,rnm->rkm", sin_one, series, preferred_element_type=jnp.float32)
    twisted_re = (first_re * twist_cos + first_im * twist_sin).astype(jnp.bfloat16)
    twisted_im = (first_im * twist_cos - first_re * twist_sin).astype(jnp.bfloat16)
    out_re = jnp.einsum(
        "rkn,nj->rjk", twisted_re, cos_three, preferred_element_type=jnp.float32
    ) + jnp.einsum("rkn,nj->rjk", twisted_im, sin_three, preferred_element_type=jnp.float32)
    out_im = jnp.einsum(
        "rkn,nj->rjk", twisted_im, cos_three, preferred_element_type=jnp.float32
    ) - jnp.einsum("rkn,nj->rjk", twisted_re, sin_three, preferred_element_type=jnp.float32)
    power = (out_re * out_re + out_im * out_im) / (length * channels)
    return power.reshape(row_count, 64 * fold_size)


def owner_plan(samples, channel_order, merge_table):
    owners = lax.axis_size("sub")
    owner_index = lax.axis_index("sub")
    owned_rows = CH_DEV // 2
    quarter = CH_DEV // 4
    window = samples.shape[0]
    channels = samples.shape[1]
    ordered = jnp.take(samples, channel_order, axis=1).T.reshape(owners, CH_DEV, window)
    current = lax.all_to_all(ordered, "sub", split_axis=0, concat_axis=2, tiled=True).reshape(
        CH_DEV, window * owners
    )
    for level_num in range(1, LOCAL + 1):
        entries = lax.dynamic_slice_in_dim(
            merge_table[level_num - 1], owner_index * owned_rows, owned_rows, 1
        )
        current = merge_level(
            current, entries, max(1, 2 ** (level_num - 2)), 2 ** (level_num - 1), 1
        )
    block_index = jnp.zeros((), jnp.int32)
    for bit_num in range(owners.bit_length() - 1):
        level_num = LOCAL + bit_num + 1
        half_bit = owner_index >> bit_num & 1
        block_index = block_index * 2 + half_bit
        span_rows = owned_rows * 2 ** (bit_num + 1)
        child_rows = span_rows // 2
        subband = owner_index >> bit_num + 1
        entries = lax.dynamic_slice_in_dim(
            merge_table[level_num - 1],
            subband * span_rows + owned_rows * block_index,
            owned_rows,
            1,
        )
        kept_rows = lax.dynamic_slice_in_dim(current, half_bit * quarter, quarter, 0)
        sent_rows = lax.dynamic_slice_in_dim(current, (1 - half_bit) * quarter, quarter, 0)
        partner = from_partner(sent_rows, "sub", bit_num)
        row_base = quarter * block_index
        is_low = half_bit == 0
        lower_part = jnp.where(is_low, kept_rows, partner)
        upper_part = jnp.where(is_low, partner, kept_rows)
        lower_rows = jnp.take(lower_part, entries[0] - row_base, axis=0)
        upper_rows = jnp.take(upper_part, entries[1] - row_base, axis=0)
        moved_rows = delay_rows(upper_rows, entries[2], child_rows)
        current = (lower_rows.astype(jnp.float32) + moved_rows.astype(jnp.float32)).astype(
            jnp.bfloat16
        )
    return spectrum(current[:, :SAMPLES], channels)


def reverse_bits(value, bits):
    flipped = 0
    for bit_num in range(bits):
        flipped |= (value >> bit_num & 1) << (bits - 1 - bit_num)
    return flipped


def take_along(values, index, axis):
    along = lax.GatherDimensionNumbers(
        offset_dims=(),
        collapsed_slice_dims=(axis,),
        start_index_map=(axis,),
        operand_batching_dims=(1 - axis,),
        start_indices_batching_dims=(1 - axis,),
    )
    return lax.gather(
        values, index[:, :, None], along, (1, 1), mode=lax.GatherScatterMode.PROMISE_IN_BOUNDS
    )


def tree_kernel(
    owners, margin, samples_at, order_at, table_at, turned_ref, send_ref, raw_ref, order_ref,
    table_ref, first_ref, pick_ref, cur_ref, picked_ref, final_ref, sems,
):
    window, channels = raw_ref.shape
    levels, _, dmax = table_ref.shape
    quarter = CH_DEV // 4
    pad = margin // 2
    length = pad + window
    offset = (lax.axis_index("sub") * window) % LANES
    loads = [
        pltpu.make_async_copy(source, target, sems.at[at])
        for at, (source, target) in enumerate(
            ((table_at, table_ref), (order_at, order_ref), (samples_at, raw_ref))
        )
    ]
    for load in loads:
        load.start()

    final_ref[...] = jnp.zeros(final_ref.shape, final_ref.dtype)
    lane = lax.broadcasted_iota(jnp.int32, (8, LANES), 1)

    def narrow(numbers):
        return numbers.astype(jnp.float32).astype(jnp.bfloat16)

    def one_hot(place, chosen):
        return jnp.where(
            place == jnp.broadcast_to(narrow(chosen), place.shape),
            jnp.ones(place.shape, jnp.bfloat16),
            jnp.zeros(place.shape, jnp.bfloat16),
        )

    loads[0].wait()
    loads[1].wait()
    place = narrow(lax.broadcasted_iota(jnp.int32, (dmax, LANES), 0))
    for side in range(2):
        for tile in range(dmax // LANES):
            parts = [
                take_along(
                    jnp.broadcast_to(
                        order_ref[:, (2 * tile + part) * LANES : (2 * tile + part + 1) * LANES],
                        (8, LANES),
                    ),
                    (2 * lane + side) & (LANES - 1),
                    1,
                )
                for part in range(2)
            ]
            chosen = jnp.where(lane < LANES // 2, parts[0], parts[1])[:1]
            at = side * dmax + tile * LANES
            for part in range(channels // dmax):
                first_ref[part * dmax : (part + 1) * dmax, at : at + LANES] = one_hot(
                    place, chosen - part * dmax
                )
    index = lax.broadcasted_iota(jnp.int32, (1, dmax), 1)
    place = narrow(lax.broadcasted_iota(jnp.int32, (dmax // 2, LANES), 0))
    for level in range(1, levels):
        child = 2 ** (level - 1)
        start = (index >> level) * (2 * child)
        for side in range(2):
            chosen = (start + side * child + table_ref[level, side : side + 1, :]) & (
                dmax // 2 - 1
            )
            for tile in range(dmax // LANES):
                part, to = (side, tile) if level == levels - 1 else (tile, side)
                pick_ref[level - 1, part, :, to * LANES : (to + 1) * LANES] = one_hot(
                    place, chosen[:, tile * LANES : (tile + 1) * LANES]
                )
    loads[2].wait()

    row = lax.broadcasted_iota(jnp.int32, (8, LANES), 0)
    zero = jnp.zeros((8, LANES), jnp.float32)
    begin = pad
    for level in range(levels):
        last = level == levels - 1
        if level:
            for part in range(2):
                picked_ref[begin:length, part * dmax : (part + 1) * dmax] = jnp.dot(
                    cur_ref[begin:length, part * LANES : (part + 1) * LANES],
                    pick_ref[level - 1, part],
                    preferred_element_type=jnp.float32,
                )
        else:
            picked_ref[begin:length, :] = jnp.dot(
                raw_ref[...], first_ref[...], preferred_element_type=jnp.float32
            )
        reached = (pad - 2**level) // 16 * 16
        for tile in range(dmax // LANES):
            low_at = tile if last or not level else 2 * tile
            high_at = low_at + (2 if last or not level else 1)
            low_lanes = slice(low_at * LANES, (low_at + 1) * LANES)
            high_lanes = slice(high_at * LANES, (high_at + 1) * LANES)
            output = tile * LANES + lane
            steps = (output & (2**level - 1)) // (2 * quarter)
            least = (tile * LANES & (2**level - 1)) // (2 * quarter)
            most = ((tile * LANES + LANES - 1) & (2**level - 1)) // (2 * quarter)
            if 2**level <= LANES:
                least, most = 0, (2**level - 1) // (2 * quarter)
            bits = (most - least).bit_length()
            shift = jnp.broadcast_to(
                table_ref[level, 2:3, tile * LANES : (tile + 1) * LANES], (8, LANES)
            )
            rest = row + shift - steps * quarter
            here = rest < 8
            source = rest & 7
            flags = [((steps - least) >> bit & 1) == 1 for bit in range(bits)]
            known = {}

            def coarse(bit, at):
                if at >= length // 8:
                    return None
                if (bit, at) not in known:
                    if bit == 0:
                        known[bit, at] = (
                            picked_ref[at * 8 : at * 8 + 8, high_lanes]
                            if at * 8 >= begin
                            else None
                        )
                    else:
                        near, far = coarse(bit - 1, at), coarse(bit - 1, at + 2 ** (bit - 1))
                        if near is None and far is None:
                            known[bit, at] = None
                        else:
                            near = zero if near is None else near
                            far = zero if far is None else far
                            known[bit, at] = jnp.where(flags[bit - 1], far, near)
                return known[bit, at]

            def fine(at):
                if ("fine", at) not in known:
                    value = coarse(bits, at + least)
                    known["fine", at] = None if value is None else take_along(value, source, 0)
                return known["fine", at]

            def merged(at):
                near, far = fine(at), fine(at + 1)
                total = None
                if near is not None or far is not None:
                    total = jnp.where(
                        here, zero if near is None else near, zero if far is None else far
                    )
                if begin <= at * 8:
                    low = picked_ref[at * 8 : at * 8 + 8, low_lanes]
                    total = low if total is None else low + total
                return zero if total is None else total

            lanes = slice(tile * LANES, (tile + 1) * LANES)
            for at in range(reached // 8, length // 8, 2):
                both = jnp.concatenate([merged(at), merged(at + 1)], axis=0).astype(jnp.bfloat16)
                if last:
                    to = pl.multiple_of(offset + at * 8 + pad, 16)
                    final_ref[pl.ds(to, 16), lanes] = both
                else:
                    cur_ref[at * 8 : at * 8 + 16, lanes] = both
        begin = max(reached, 0)

    for tile in range(dmax // LANES):
        at = slice(tile * LANES, (tile + 1) * LANES)
        for time in range(final_ref.shape[0] // LANES):
            lanes = slice(time * LANES, (time + 1) * LANES)
            turned_ref[at, lanes] = final_ref[lanes, at].T
    other = 1 - (lax.axis_index("sub") & 1)
    for ring in range(send_ref.shape[0]):
        for relay in range(2):
            send_ref[ring, relay] = turned_ref[rows_for(owners, dmax, ring, relay, other), :]


def rows_for(owners, dmax, ring, relay, core):
    chip, side = (2 * ring + core, core ^ relay) if ring else (relay, core)
    owner = ((lax.axis_index("sub") >> 1) ^ chip) << 1 | side
    rows = dmax // owners
    block = reverse_bits(owner, (owners - 1).bit_length())
    return pl.ds(pl.multiple_of(block * rows, rows), rows)


def pair_kernel(owners, apart, turned_ref, got_ref, own_ref, near_ref, *message_refs):
    core = lax.axis_index("sub") & 1
    lower = core == 0
    tiles = turned_ref.shape[-1] // LANES
    for ring in range(got_ref.shape[0]):
        for relay in range(2):
            rows = rows_for(owners, turned_ref.shape[0], ring, relay, core)
            for tile in range(apart + tiles):
                total = None
                for start, mine in ((0, lower), (apart, ~lower)):
                    if start <= tile < start + tiles:
                        lanes = slice((tile - start) * LANES, (tile - start + 1) * LANES)
                        part = jnp.where(
                            mine, turned_ref[rows, lanes], got_ref[ring, relay, :, lanes]
                        ).astype(jnp.float32)
                        total = part if total is None else total + part
                total = total.astype(own_ref.dtype)
                lanes = slice(tile * LANES, (tile + 1) * LANES)
                if ring:
                    message_refs[ring - 1][relay, :, lanes] = total
                else:
                    (near_ref if relay else own_ref)[:, lanes] = total


def spectrum_kernel(
    rings, scale, own_ref, near_ref, *refs
):
    message_refs, refs = refs[: rings - 1], refs[rings - 1 :]
    relay_refs, refs = refs[: rings - 1], refs[rings - 1 :]
    first_ref, cos_ref, sin_ref, third_ref, out_ref = refs[:5]
    slot_ref, flat_ref, lines_ref, sems = refs[5:]
    rows, width = own_ref.shape
    tiles = width // LANES
    pitch = slot_ref.shape[0] // rows
    used = first_ref.shape[1]
    bins = first_ref.shape[0] // 2
    halves = third_ref.shape[0] // 2
    me = lax.axis_index("sub")
    core = me & 1
    sources = [(own_ref, (), 0), (near_ref, (), 1)]
    for ring in range(1, rings):
        sources.append((message_refs[ring - 1], (0,), 2 * ring + core))
        sources.append((relay_refs[ring - 1], (1,), 2 * ring + 1 - core))
    for ref, at, apart in sources:
        slot = ((me >> 1) ^ apart) * tiles
        for tile in range(tiles):
            slot_ref[pl.ds(slot + tile, rows, stride=pitch), :] = ref[
                at + (slice(None), slice(tile * LANES, (tile + 1) * LANES))
            ].astype(jnp.float32)
    lines = halves // 2
    lane = lax.broadcasted_iota(jnp.int32, (lines, LANES), 1)
    group = 4
    stores = []

    def first_stage(start):
        series = jnp.concatenate(
            [
                slot_ref[row * pitch : row * pitch + used, :].astype(jnp.bfloat16)
                for row in range(start, start + group)
            ],
            axis=1,
        )
        return jnp.dot(first_ref[...], series, preferred_element_type=jnp.float32)

    def twist(turned):
        twisted = []
        for at in range(group):
            real = turned[:bins, at * LANES : (at + 1) * LANES]
            imag = turned[bins:, at * LANES : (at + 1) * LANES]
            twisted.append(
                jnp.concatenate(
                    [
                        (real * cos_ref[...] - imag * sin_ref[...]).astype(jnp.bfloat16),
                        (-imag * cos_ref[...] - real * sin_ref[...]).astype(jnp.bfloat16),
                    ],
                    axis=1,
                )
            )
        return jnp.concatenate(twisted, axis=0)

    def last_stage(start, twisted):
        mixed = lax.dot_general(
            third_ref[...], twisted, (((1,), (1,)), ((), ())), preferred_element_type=jnp.float32
        )
        real, imag = mixed[:halves], mixed[halves:]
        power = (real * real + imag * imag) * scale
        for at in range(0, group, 2):
            both = power[:, at * bins : at * bins + LANES]
            even, odd = both[:lines], both[lines:]
            left = jnp.where(lane < bins, even, pltpu.roll(odd, bins, axis=1))
            right = jnp.where(lane < bins, pltpu.roll(even, bins, axis=1), odd)
            for row, line in ((start + at, left), (start + at + 1, right)):
                flat_ref[pl.ds(row // 8 * 8 * lines + row % 8, lines, stride=8), :] = line
        row = start + group - 1
        if row % 8 == 7:
            part = row // 8
            for tile in range(lines):
                at = (part * lines + tile) * 8
                lines_ref[part * 8 : part * 8 + 8, tile * LANES : (tile + 1) * LANES] = flat_ref[
                    at : at + 8, :
                ]
            stores.append(
                pltpu.make_async_copy(
                    lines_ref.at[pl.ds(part * 8, 8)],
                    out_ref.at[pl.ds(part * 8, 8)],
                    sems.at[part],
                )
            )
            stores[-1].start()

    turned = first_stage(0)
    for start in range(0, rows, group):
        twisted = twist(turned)
        if start + group < rows:
            turned = first_stage(start + group)
        last_stage(start, twisted)
    for store in stores:
        store.wait()


def spectrum_tables(sources, window, margin, tiles):
    fold = SAMPLES // LANES
    k = np.arange(fold)
    n = np.arange(LANES)
    m = np.arange(64)

    def angle(product, period):
        return np.float32(2.0 * math.pi / period) * (product % period).astype(np.float32)

    one = angle(k[:, None] * k[None, :], fold)
    table_one = np.concatenate([np.cos(one), np.sin(one)], axis=0)
    first = np.zeros((2 * fold, sources * tiles), np.float32)
    for source in range(sources):
        start = (source * window) // LANES - margin // LANES
        for tile in range(tiles):
            if 0 <= start + tile < fold:
                first[:, source * tiles + tile] = table_one[:, start + tile]
    two = angle(k[:, None] * n[None, :], SAMPLES)
    m = np.concatenate([m[0::2], m[1::2]])
    three = angle(m[:, None] * n[None, :], LANES)
    cos_three, sin_three = np.cos(three), np.sin(three)
    third = np.block([[cos_three, sin_three], [-sin_three, cos_three]])
    return (
        jnp.asarray(first, jnp.bfloat16),
        jnp.asarray(np.cos(two), jnp.float32),
        jnp.asarray(np.sin(two), jnp.float32),
        jnp.asarray(third, jnp.bfloat16),
    )


def pairs_align(window, owners):
    starts = [at * window // LANES for at in range(owners)]
    return all(starts[at + 1] - starts[at] == window // LANES for at in range(0, owners, 2))


def on_chip(values):
    return pltpu.with_memory_space_constraint(values, pltpu.VMEM)


def slice_plan(samples, channel_order, merge_table):
    owners = lax.axis_size("sub")
    window, channels = samples.shape
    levels, _, dmax = merge_table.shape
    margin = window * owners - SAMPLES
    rows = dmax // owners
    rings = owners // 4
    step = math.gcd(window, LANES)
    width = margin + -(-(window + LANES - step) // LANES) * LANES
    kept = margin // 2 + window
    apart = window // LANES
    wide = width + apart * LANES
    vmem = pl.BlockSpec(memory_space=pltpu.VMEM)
    half = pltpu.VMEM((rings, 2, rows, width), jnp.bfloat16)
    turned, send = pl.pallas_call(
        functools.partial(tree_kernel, owners, margin),
        out_shape=[pltpu.VMEM((dmax, width), jnp.bfloat16), half],
        in_specs=[pl.BlockSpec(memory_space=pl.ANY)] * 3,
        out_specs=[vmem, vmem],
        scratch_shapes=[
            pltpu.VMEM((window, channels), jnp.bfloat16),
            pltpu.VMEM((1, channels), jnp.int32),
            pltpu.VMEM((levels, 3, dmax), jnp.int32),
            pltpu.VMEM((channels, 2 * dmax), jnp.bfloat16),
            pltpu.VMEM((levels - 1, 2, dmax // 2, dmax), jnp.bfloat16),
            pltpu.VMEM((kept, dmax), jnp.bfloat16),
            pltpu.VMEM((kept, 2 * dmax), jnp.float32),
            pltpu.VMEM((width, dmax), jnp.bfloat16),
            pltpu.SemaphoreType.DMA((3,)),
        ],
        name="tree",
    )(samples, channel_order.reshape(1, channels), merge_table)
    beside = [(low, low ^ 1) for low in range(owners)]
    got = on_chip(lax.ppermute(send, "sub", beside))
    block = pltpu.VMEM((rows, wide), jnp.bfloat16)
    message = pltpu.VMEM((2, rows, wide), jnp.bfloat16)
    own, near, *messages = pl.pallas_call(
        functools.partial(pair_kernel, owners, apart),
        out_shape=[block, block] + [message] * (rings - 1),
        in_specs=[vmem] * 2,
        out_specs=[vmem] * (rings + 1),
        name="pair",
    )(on_chip(turned), got)
    arrived = []
    for ring in range(rings):
        route = [(a, a ^ (2 * (2 * ring + a % 2) if ring else 2)) for a in range(owners)]
        message = messages[ring - 1] if ring else near
        arrived.append(on_chip(lax.ppermute(message, "sub", route)))
    near, *arrived = arrived
    relayed = []
    for ring in range(1, rings):
        relayed.append(on_chip(lax.ppermute(arrived[ring - 1], "sub", beside)))
    pairs = owners // 2
    tables = [
        on_chip(table) for table in spectrum_tables(pairs, 2 * window, margin, wide // LANES)
    ]
    pitch = pairs * wide // LANES + 1
    return pl.pallas_call(
        functools.partial(spectrum_kernel, rings, 1.0 / (SAMPLES * channels)),
        out_shape=jax.ShapeDtypeStruct((rows, SAMPLES // 2), jnp.float32),
        in_specs=[vmem] * (2 * rings + 4),
        out_specs=pl.BlockSpec(memory_space=pl.ANY),
        scratch_shapes=[
            pltpu.VMEM((rows * pitch, LANES), jnp.float32),
            pltpu.VMEM((rows * SAMPLES // 2 // LANES, LANES), jnp.float32),
            pltpu.VMEM((rows, SAMPLES // 2), jnp.float32),
            pltpu.SemaphoreType.DMA((rows // 8,)),
        ],
        name="spectrum",
    )(on_chip(own), near, *arrived, *relayed, *tables)


def local(samples, channel_order, merge_table):
    owners = lax.axis_size("sub")
    window, channels = samples.shape
    dmax = merge_table.shape[2]
    margin = window * owners - SAMPLES
    fits = (
        dmax == 256
        and channels == 2 * dmax
        and dmax == 16 * owners
        and margin == dmax
        and window % 16 == 0
        and window <= 1024
        and owners % 8 == 0
        and pairs_align(window, owners)
    )
    plan = slice_plan if fits else owner_plan
    return plan(samples, channel_order, merge_table)


def solution(mesh):
    in_specs = (P(("groups", "sub"), None), P(), P())
    out_specs = P(("groups", "sub"), None)
    return jax.shard_map(local, mesh=mesh, in_specs=in_specs, out_specs=out_specs, check_vma=False)
```

```python
import functools
import math

import jax
import jax.numpy as jnp
import numpy as np
from jax import lax
from jax.experimental import pallas as pl
from jax.experimental.pallas import tpu as pltpu
from jax.sharding import PartitionSpec as P


LOCAL = 5
CH_DEV = 32
SAMPLES = 8192
LANES = 128


def from_partner(block, axis, apart):
    count = lax.axis_size(axis)
    route = []
    for low in range(count):
        high = low | 1 << apart
        if high != low and high < count:
            route += [(low, high), (high, low)]
    return lax.ppermute(block, axis, route)


def delay_rows(values, shifts, margin):
    moved = values
    for bit_num in range(max(1, margin.bit_length())):
        offset = 2**bit_num
        rolled = jnp.pad(moved[:, offset:], ((0, 0), (0, offset)))
        flagged = shifts >> bit_num & 1 == 1
        flagged = flagged[:, None]
        moved = jnp.where(flagged, rolled, moved)
    return moved


def merge_level(current, entries, child_rows, span_rows, time_axis):
    outputs = jnp.arange(entries.shape[1], dtype=jnp.int32)
    starts = 2 * child_rows * (outputs // span_rows)
    lower_rows = jnp.take(current, starts + entries[0], axis=1 - time_axis)
    upper_rows = jnp.take(current, starts + child_rows + entries[1], axis=1 - time_axis)
    moved_rows = delay_rows(upper_rows, entries[2], child_rows)
    return (lower_rows.astype(jnp.float32) + moved_rows.astype(jnp.float32)).astype(jnp.bfloat16)


def spectrum(delays, channels):
    row_count = delays.shape[0]
    length = delays.shape[1]
    fold_size = length // 128
    first_index = jnp.arange(fold_size, dtype=jnp.int32)
    lane_index = jnp.arange(128, dtype=jnp.int32)
    half_index = jnp.arange(64, dtype=jnp.int32)
    angle_one = (
        2.0
        * math.pi
        / fold_size
        * (first_index[:, None] * first_index[None, :] % fold_size).astype(jnp.float32)
    )
    cos_one = jnp.cos(angle_one).astype(jnp.bfloat16)
    sin_one = jnp.sin(angle_one).astype(jnp.bfloat16)
    angle_two = (
        2.0
        * math.pi
        / length
        * (first_index[:, None] * lane_index[None, :] % length).astype(jnp.float32)
    )
    twist_cos = jnp.cos(angle_two)
    twist_sin = jnp.sin(angle_two)
    angle_three = (
        2.0 * math.pi / 128 * (lane_index[:, None] * half_index[None, :] % 128).astype(jnp.float32)
    )
    cos_three = jnp.cos(angle_three).astype(jnp.bfloat16)
    sin_three = jnp.sin(angle_three).astype(jnp.bfloat16)
    series = delays.reshape(row_count, fold_size, 128)
    first_re = jnp.einsum("kn,rnm->rkm", cos_one, series, preferred_element_type=jnp.float32)
    first_im = -jnp.einsum("kn,rnm->rkm", sin_one, series, preferred_element_type=jnp.float32)
    twisted_re = (first_re * twist_cos + first_im * twist_sin).astype(jnp.bfloat16)
    twisted_im = (first_im * twist_cos - first_re * twist_sin).astype(jnp.bfloat16)
    out_re = jnp.einsum(
        "rkn,nj->rjk", twisted_re, cos_three, preferred_element_type=jnp.float32
    ) + jnp.einsum("rkn,nj->rjk", twisted_im, sin_three, preferred_element_type=jnp.float32)
    out_im = jnp.einsum(
        "rkn,nj->rjk", twisted_im, cos_three, preferred_element_type=jnp.float32
    ) - jnp.einsum("rkn,nj->rjk", twisted_re, sin_three, preferred_element_type=jnp.float32)
    power = (out_re * out_re + out_im * out_im) / (length * channels)
    return power.reshape(row_count, 64 * fold_size)


def owner_plan(samples, channel_order, merge_table):
    owners = lax.axis_size("sub")
    owner_index = lax.axis_index("sub")
    owned_rows = CH_DEV // 2
    quarter = CH_DEV // 4
    window = samples.shape[0]
    channels = samples.shape[1]
    ordered = jnp.take(samples, channel_order, axis=1).T.reshape(owners, CH_DEV, window)
    current = lax.all_to_all(ordered, "sub", split_axis=0, concat_axis=2, tiled=True).reshape(
        CH_DEV, window * owners
    )
    for level_num in range(1, LOCAL + 1):
        entries = lax.dynamic_slice_in_dim(
            merge_table[level_num - 1], owner_index * owned_rows, owned_rows, 1
        )
        current = merge_level(
            current, entries, max(1, 2 ** (level_num - 2)), 2 ** (level_num - 1), 1
        )
    block_index = jnp.zeros((), jnp.int32)
    for bit_num in range(owners.bit_length() - 1):
        level_num = LOCAL + bit_num + 1
        half_bit = owner_index >> bit_num & 1
        block_index = block_index * 2 + half_bit
        span_rows = owned_rows * 2 ** (bit_num + 1)
        child_rows = span_rows // 2
        subband = owner_index >> bit_num + 1
        entries = lax.dynamic_slice_in_dim(
            merge_table[level_num - 1],
            subband * span_rows + owned_rows * block_index,
            owned_rows,
            1,
        )
        kept_rows = lax.dynamic_slice_in_dim(current, half_bit * quarter, quarter, 0)
        sent_rows = lax.dynamic_slice_in_dim(current, (1 - half_bit) * quarter, quarter, 0)
        partner = from_partner(sent_rows, "sub", bit_num)
        row_base = quarter * block_index
        is_low = half_bit == 0
        lower_part = jnp.where(is_low, kept_rows, partner)
        upper_part = jnp.where(is_low, partner, kept_rows)
        lower_rows = jnp.take(lower_part, entries[0] - row_base, axis=0)
        upper_rows = jnp.take(upper_part, entries[1] - row_base, axis=0)
        moved_rows = delay_rows(upper_rows, entries[2], child_rows)
        current = (lower_rows.astype(jnp.float32) + moved_rows.astype(jnp.float32)).astype(
            jnp.bfloat16
        )
    return spectrum(current[:, :SAMPLES], channels)


def reverse_bits(value, bits):
    flipped = 0
    for bit_num in range(bits):
        flipped |= (value >> bit_num & 1) << (bits - 1 - bit_num)
    return flipped


def take_along(values, index, axis):
    along = lax.GatherDimensionNumbers(
        offset_dims=(),
        collapsed_slice_dims=(axis,),
        start_index_map=(axis,),
        operand_batching_dims=(1 - axis,),
        start_indices_batching_dims=(1 - axis,),
    )
    return lax.gather(
        values, index[:, :, None], along, (1, 1), mode=lax.GatherScatterMode.PROMISE_IN_BOUNDS
    )


def tree_kernel(
    owners, margin, samples_at, order_at, table_at, turned_ref, send_ref, raw_ref, order_ref,
    table_ref, first_ref, pick_ref, cur_ref, picked_ref, final_ref, sems,
):
    window, channels = raw_ref.shape
    levels, _, dmax = table_ref.shape
    quarter = CH_DEV // 4
    pad = margin // 2
    length = pad + window
    offset = (lax.axis_index("sub") * window) % LANES
    loads = [
        pltpu.make_async_copy(source, target, sems.at[at])
        for at, (source, target) in enumerate(
            ((table_at, table_ref), (order_at, order_ref), (samples_at, raw_ref))
        )
    ]
    for load in loads:
        load.start()

    for edge in (slice(0, LANES), slice(margin + window, final_ref.shape[0])):
        final_ref[edge] = jnp.zeros((edge.stop - edge.start, dmax), final_ref.dtype)
    lane = lax.broadcasted_iota(jnp.int32, (8, LANES), 1)

    def narrow(numbers):
        return numbers.astype(jnp.float32).astype(jnp.bfloat16)

    def one_hot(place, chosen):
        return jnp.where(
            place == jnp.broadcast_to(narrow(chosen), place.shape),
            jnp.ones(place.shape, jnp.bfloat16),
            jnp.zeros(place.shape, jnp.bfloat16),
        )

    loads[0].wait()
    loads[1].wait()
    place = narrow(lax.broadcasted_iota(jnp.int32, (dmax, LANES), 0))
    for side in range(2):
        for tile in range(dmax // LANES):
            parts = [
                take_along(
                    jnp.broadcast_to(
                        order_ref[:, (2 * tile + part) * LANES : (2 * tile + part + 1) * LANES],
                        (8, LANES),
                    ),
                    (2 * lane + side) & (LANES - 1),
                    1,
                )
                for part in range(2)
            ]
            chosen = jnp.where(lane < LANES // 2, parts[0], parts[1])[:1]
            at = side * dmax + tile * LANES
            for part in range(channels // dmax):
                first_ref[part * dmax : (part + 1) * dmax, at : at + LANES] = one_hot(
                    place, chosen - part * dmax
                )
    index = lax.broadcasted_iota(jnp.int32, (1, dmax), 1)
    place = narrow(lax.broadcasted_iota(jnp.int32, (dmax // 2, LANES), 0))
    for level in range(1, levels):
        child = 2 ** (level - 1)
        start = (index >> level) * (2 * child)
        for side in range(2):
            chosen = (start + side * child + table_ref[level, side : side + 1, :]) & (
                dmax // 2 - 1
            )
            for tile in range(dmax // LANES):
                part, to = (side, tile) if level == levels - 1 else (tile, side)
                pick_ref[level - 1, part, :, to * LANES : (to + 1) * LANES] = one_hot(
                    place, chosen[:, tile * LANES : (tile + 1) * LANES]
                )
    loads[2].wait()

    row = lax.broadcasted_iota(jnp.int32, (8, LANES), 0)
    zero = jnp.zeros((8, LANES), jnp.float32)
    begin = pad
    for level in range(levels):
        last = level == levels - 1
        if level:
            for part in range(2):
                picked_ref[begin:length, part * dmax : (part + 1) * dmax] = jnp.dot(
                    cur_ref[begin:length, part * LANES : (part + 1) * LANES],
                    pick_ref[level - 1, part],
                    preferred_element_type=jnp.float32,
                )
        else:
            picked_ref[begin:length, :] = jnp.dot(
                raw_ref[...], first_ref[...], preferred_element_type=jnp.float32
            )
        reached = (pad - 2**level) // 16 * 16
        for tile in range(dmax // LANES):
            low_at = tile if last or not level else 2 * tile
            high_at = low_at + (2 if last or not level else 1)
            low_lanes = slice(low_at * LANES, (low_at + 1) * LANES)
            high_lanes = slice(high_at * LANES, (high_at + 1) * LANES)
            output = tile * LANES + lane
            steps = (output & (2**level - 1)) // (2 * quarter)
            least = (tile * LANES & (2**level - 1)) // (2 * quarter)
            most = ((tile * LANES + LANES - 1) & (2**level - 1)) // (2 * quarter)
            if 2**level <= LANES:
                least, most = 0, (2**level - 1) // (2 * quarter)
            bits = (most - least).bit_length()
            shift = jnp.broadcast_to(
                table_ref[level, 2:3, tile * LANES : (tile + 1) * LANES], (8, LANES)
            )
            rest = row + shift - steps * quarter
            here = rest < 8
            source = rest & 7
            flags = [((steps - least) >> bit & 1) == 1 for bit in range(bits)]
            known = {}

            def coarse(bit, at):
                if at >= length // 8:
                    return None
                if (bit, at) not in known:
                    if bit == 0:
                        known[bit, at] = (
                            picked_ref[at * 8 : at * 8 + 8, high_lanes]
                            if at * 8 >= begin
                            else None
                        )
                    else:
                        near, far = coarse(bit - 1, at), coarse(bit - 1, at + 2 ** (bit - 1))
                        if near is None and far is None:
                            known[bit, at] = None
                        else:
                            near = zero if near is None else near
                            far = zero if far is None else far
                            known[bit, at] = jnp.where(flags[bit - 1], far, near)
                return known[bit, at]

            def fine(at):
                if ("fine", at) not in known:
                    value = coarse(bits, at + least)
                    known["fine", at] = None if value is None else take_along(value, source, 0)
                return known["fine", at]

            def merged(at):
                near, far = fine(at), fine(at + 1)
                total = None
                if near is not None or far is not None:
                    total = jnp.where(
                        here, zero if near is None else near, zero if far is None else far
                    )
                if begin <= at * 8:
                    low = picked_ref[at * 8 : at * 8 + 8, low_lanes]
                    total = low if total is None else low + total
                return zero if total is None else total

            lanes = slice(tile * LANES, (tile + 1) * LANES)
            for at in range(reached // 8, length // 8, 2):
                both = jnp.concatenate([merged(at), merged(at + 1)], axis=0).astype(jnp.bfloat16)
                if last:
                    to = pl.multiple_of(offset + at * 8 + pad, 16)
                    final_ref[pl.ds(to, 16), lanes] = both
                else:
                    cur_ref[at * 8 : at * 8 + 16, lanes] = both
        begin = max(reached, 0)

    for tile in range(dmax // LANES):
        at = slice(tile * LANES, (tile + 1) * LANES)
        for time in range(final_ref.shape[0] // LANES):
            lanes = slice(time * LANES, (time + 1) * LANES)
            turned_ref[at, lanes] = final_ref[lanes, at].T
    other = 1 - (lax.axis_index("sub") & 1)
    for ring in range(send_ref.shape[0]):
        for relay in range(2):
            send_ref[ring, relay] = turned_ref[rows_for(owners, dmax, ring, relay, other), :]


def rows_for(owners, dmax, ring, relay, core):
    chip, side = (2 * ring + core, core ^ relay) if ring else (relay, core)
    owner = ((lax.axis_index("sub") >> 1) ^ chip) << 1 | side
    rows = dmax // owners
    block = reverse_bits(owner, (owners - 1).bit_length())
    return pl.ds(pl.multiple_of(block * rows, rows), rows)


def pair_kernel(owners, apart, turned_ref, got_ref, own_ref, near_ref, *message_refs):
    core = lax.axis_index("sub") & 1
    lower = core == 0
    tiles = turned_ref.shape[-1] // LANES
    for ring in range(got_ref.shape[0]):
        for relay in range(2):
            rows = rows_for(owners, turned_ref.shape[0], ring, relay, core)
            for tile in range(apart + tiles):
                total = None
                for start, mine in ((0, lower), (apart, ~lower)):
                    if start <= tile < start + tiles:
                        lanes = slice((tile - start) * LANES, (tile - start + 1) * LANES)
                        part = jnp.where(
                            mine, turned_ref[rows, lanes], got_ref[ring, relay, :, lanes]
                        ).astype(jnp.float32)
                        total = part if total is None else total + part
                total = total.astype(own_ref.dtype)
                lanes = slice(tile * LANES, (tile + 1) * LANES)
                if ring:
                    message_refs[ring - 1][relay, :, lanes] = total
                else:
                    (near_ref if relay else own_ref)[:, lanes] = total


def spectrum_kernel(
    rings, scale, own_ref, near_ref, *refs
):
    message_refs, refs = refs[: rings - 1], refs[rings - 1 :]
    relay_refs, refs = refs[: rings - 1], refs[rings - 1 :]
    first_ref, cos_ref, sin_ref, third_ref, out_ref = refs[:5]
    slot_ref, flat_ref, lines_ref, sems = refs[5:]
    rows, width = own_ref.shape
    tiles = width // LANES
    pitch = slot_ref.shape[0] // rows
    used = first_ref.shape[1]
    bins = first_ref.shape[0] // 2
    halves = third_ref.shape[0] // 2
    me = lax.axis_index("sub")
    core = me & 1
    sources = [(own_ref, (), 0), (near_ref, (), 1)]
    for ring in range(1, rings):
        sources.append((message_refs[ring - 1], (0,), 2 * ring + core))
        sources.append((relay_refs[ring - 1], (1,), 2 * ring + 1 - core))
    for ref, at, apart in sources:
        slot = ((me >> 1) ^ apart) * tiles
        for tile in range(tiles):
            slot_ref[pl.ds(slot + tile, rows, stride=pitch), :] = ref[
                at + (slice(None), slice(tile * LANES, (tile + 1) * LANES))
            ].astype(jnp.float32)
    lines = halves // 2
    lane = lax.broadcasted_iota(jnp.int32, (lines, LANES), 1)
    group = 8
    stores = []

    def first_stage(start):
        series = jnp.concatenate(
            [
                slot_ref[row * pitch : row * pitch + used, :].astype(jnp.bfloat16)
                for row in range(start, start + group)
            ],
            axis=1,
        )
        return jnp.dot(first_ref[...], series, preferred_element_type=jnp.float32)

    def twist(turned):
        twisted = []
        for at in range(group):
            real = turned[:bins, at * LANES : (at + 1) * LANES]
            imag = turned[bins:, at * LANES : (at + 1) * LANES]
            twisted.append(
                jnp.concatenate(
                    [
                        (real * cos_ref[...] - imag * sin_ref[...]).astype(jnp.bfloat16),
                        (-imag * cos_ref[...] - real * sin_ref[...]).astype(jnp.bfloat16),
                    ],
                    axis=1,
                )
            )
        return jnp.concatenate(twisted, axis=0)

    def last_stage(start, twisted):
        mixed = lax.dot_general(
            third_ref[...], twisted, (((1,), (1,)), ((), ())), preferred_element_type=jnp.float32
        )
        real, imag = mixed[:halves], mixed[halves:]
        power = (real * real + imag * imag) * scale
        for at in range(0, group, 2):
            both = power[:, at * bins : at * bins + LANES]
            even, odd = both[:lines], both[lines:]
            left = jnp.where(lane < bins, even, pltpu.roll(odd, bins, axis=1))
            right = jnp.where(lane < bins, pltpu.roll(even, bins, axis=1), odd)
            for row, line in ((start + at, left), (start + at + 1, right)):
                flat_ref[pl.ds(row // 8 * 8 * lines + row % 8, lines, stride=8), :] = line
        row = start + group - 1
        if row % 8 == 7:
            part = row // 8
            for tile in range(lines):
                at = (part * lines + tile) * 8
                lines_ref[part * 8 : part * 8 + 8, tile * LANES : (tile + 1) * LANES] = flat_ref[
                    at : at + 8, :
                ]
            stores.append(
                pltpu.make_async_copy(
                    lines_ref.at[pl.ds(part * 8, 8)],
                    out_ref.at[pl.ds(part * 8, 8)],
                    sems.at[part],
                )
            )
            stores[-1].start()

    turned = first_stage(0)
    for start in range(0, rows, group):
        twisted = twist(turned)
        if start + group < rows:
            turned = first_stage(start + group)
        last_stage(start, twisted)
    for store in stores:
        store.wait()


def spectrum_tables(sources, window, margin, tiles):
    fold = SAMPLES // LANES
    k = np.arange(fold)
    n = np.arange(LANES)
    m = np.arange(64)

    def angle(product, period):
        return np.float32(2.0 * math.pi / period) * (product % period).astype(np.float32)

    one = angle(k[:, None] * k[None, :], fold)
    table_one = np.concatenate([np.cos(one), np.sin(one)], axis=0)
    first = np.zeros((2 * fold, sources * tiles), np.float32)
    for source in range(sources):
        start = (source * window) // LANES - margin // LANES
        for tile in range(tiles):
            if 0 <= start + tile < fold:
                first[:, source * tiles + tile] = table_one[:, start + tile]
    two = angle(k[:, None] * n[None, :], SAMPLES)
    m = np.concatenate([m[0::2], m[1::2]])
    three = angle(m[:, None] * n[None, :], LANES)
    cos_three, sin_three = np.cos(three), np.sin(three)
    third = np.block([[cos_three, sin_three], [-sin_three, cos_three]])
    return (
        jnp.asarray(first, jnp.bfloat16),
        jnp.asarray(np.cos(two), jnp.float32),
        jnp.asarray(np.sin(two), jnp.float32),
        jnp.asarray(third, jnp.bfloat16),
    )


def pairs_align(window, owners):
    starts = [at * window // LANES for at in range(owners)]
    return all(starts[at + 1] - starts[at] == window // LANES for at in range(0, owners, 2))


def on_chip(values):
    return pltpu.with_memory_space_constraint(values, pltpu.VMEM)


def slice_plan(samples, channel_order, merge_table):
    owners = lax.axis_size("sub")
    window, channels = samples.shape
    levels, _, dmax = merge_table.shape
    margin = window * owners - SAMPLES
    rows = dmax // owners
    rings = owners // 4
    step = math.gcd(window, LANES)
    width = margin + -(-(window + LANES - step) // LANES) * LANES
    kept = margin // 2 + window
    apart = window // LANES
    wide = width + apart * LANES
    vmem = pl.BlockSpec(memory_space=pltpu.VMEM)
    half = pltpu.VMEM((rings, 2, rows, width), jnp.bfloat16)
    turned, send = pl.pallas_call(
        functools.partial(tree_kernel, owners, margin),
        out_shape=[pltpu.VMEM((dmax, width), jnp.bfloat16), half],
        in_specs=[pl.BlockSpec(memory_space=pl.ANY)] * 3,
        out_specs=[vmem, vmem],
        scratch_shapes=[
            pltpu.VMEM((window, channels), jnp.bfloat16),
            pltpu.VMEM((1, channels), jnp.int32),
            pltpu.VMEM((levels, 3, dmax), jnp.int32),
            pltpu.VMEM((channels, 2 * dmax), jnp.bfloat16),
            pltpu.VMEM((levels - 1, 2, dmax // 2, dmax), jnp.bfloat16),
            pltpu.VMEM((kept, dmax), jnp.bfloat16),
            pltpu.VMEM((kept, 2 * dmax), jnp.float32),
            pltpu.VMEM((width, dmax), jnp.bfloat16),
            pltpu.SemaphoreType.DMA((3,)),
        ],
        name="tree",
    )(samples, channel_order.reshape(1, channels), merge_table)
    beside = [(low, low ^ 1) for low in range(owners)]
    got = on_chip(lax.ppermute(send, "sub", beside))
    block = pltpu.VMEM((rows, wide), jnp.bfloat16)
    message = pltpu.VMEM((2, rows, wide), jnp.bfloat16)
    own, near, *messages = pl.pallas_call(
        functools.partial(pair_kernel, owners, apart),
        out_shape=[block, block] + [message] * (rings - 1),
        in_specs=[vmem] * 2,
        out_specs=[vmem] * (rings + 1),
        name="pair",
    )(on_chip(turned), got)
    arrived = []
    for ring in range(rings):
        route = [(a, a ^ (2 * (2 * ring + a % 2) if ring else 2)) for a in range(owners)]
        message = messages[ring - 1] if ring else near
        arrived.append(on_chip(lax.ppermute(message, "sub", route)))
    near, *arrived = arrived
    relayed = []
    for ring in range(1, rings):
        relayed.append(on_chip(lax.ppermute(arrived[ring - 1], "sub", beside)))
    pairs = owners // 2
    tables = [
        on_chip(table) for table in spectrum_tables(pairs, 2 * window, margin, wide // LANES)
    ]
    pitch = pairs * wide // LANES + 1
    return pl.pallas_call(
        functools.partial(spectrum_kernel, rings, 1.0 / (SAMPLES * channels)),
        out_shape=jax.ShapeDtypeStruct((rows, SAMPLES // 2), jnp.float32),
        in_specs=[vmem] * (2 * rings + 4),
        out_specs=pl.BlockSpec(memory_space=pl.ANY),
        scratch_shapes=[
            pltpu.VMEM((rows * pitch, LANES), jnp.float32),
            pltpu.VMEM((rows * SAMPLES // 2 // LANES, LANES), jnp.float32),
            pltpu.VMEM((rows, SAMPLES // 2), jnp.float32),
            pltpu.SemaphoreType.DMA((rows // 8,)),
        ],
        name="spectrum",
    )(on_chip(own), near, *arrived, *relayed, *tables)


def local(samples, channel_order, merge_table):
    owners = lax.axis_size("sub")
    window, channels = samples.shape
    dmax = merge_table.shape[2]
    margin = window * owners - SAMPLES
    fits = (
        dmax == 256
        and channels == 2 * dmax
        and dmax == 16 * owners
        and margin == dmax
        and window % 16 == 0
        and window <= 1024
        and owners % 8 == 0
        and pairs_align(window, owners)
    )
    plan = slice_plan if fits else owner_plan
    return plan(samples, channel_order, merge_table)


def solution(mesh):
    in_specs = (P(("groups", "sub"), None), P(), P())
    out_specs = P(("groups", "sub"), None)
    return jax.shard_map(local, mesh=mesh, in_specs=in_specs, out_specs=out_specs, check_vma=False)
```
